32 devices in a mesh: dp: 8 (over y, x, core), tensor: 4 (over z).
Axes of the slice: x: 2, y: 2, z: 4, core: 2. Of those that a mesh axis runs over, the one named last changes fastest.
Arguments:
- block_input: bfloat16 [16384, 768], P(('dp', 'tensor')), may hold values from -6 to 6
- cotangent: bfloat16 [16384, 768], P(('dp', 'tensor')), may hold values from -6 to 6
- segment_ids: int32 [16384], P('dp'), may hold values from 0 to 1, as said below
- pad_mask: int32 [16384], P('dp'), may hold values from 0 to 1, as said below
- w_query: bfloat16 [768, 768], P(None, 'tensor'), may hold values from -0.21875 to 0.21875
- b_query: bfloat16 [768], P('tensor'), may hold values from -1.5 to 1.5
- w_key: bfloat16 [768, 768], P(None, 'tensor'), may hold values from -0.21875 to 0.21875
- w_value: bfloat16 [768, 768], P(None, 'tensor'), may hold values from -0.21875 to 0.21875
- b_value: bfloat16 [768], P('tensor'), may hold values from -1.5 to 1.5
- w_out: bfloat16 [768, 768], P('tensor'), may hold values from -0.875 to 0.875
- b_out: bfloat16 [768], replicated, may hold values from -1.5 to 1.5
- gain_one: bfloat16 [768], replicated, may hold values from 0.25 to 1.75
- shift_one: bfloat16 [768], replicated, may hold values from -1.5 to 1.5
- w_inner: bfloat16 [768, 3072], P(None, 'tensor'), may hold values from -0.21875 to 0.21875
- b_inner: bfloat16 [3072], P('tensor'), may hold values from -1.5 to 1.5
- w_outer: bfloat16 [3072, 768], P('tensor'), may hold values from -0.15625 to 0.15625
- b_outer: bfloat16 [768], replicated, may hold values from -1.5 to 1.5
- gain_two: bfloat16 [768], replicated, may hold values from 0.25 to 1.75
- shift_two: bfloat16 [768], replicated, may hold values from -1.5 to 1.5
Outputs:
- output: bfloat16 [16384, 768], P(('dp', 'tensor'))
- grad_input: float32 [16384, 768], P(('dp', 'tensor'))
- grad_w_query: float32 [768, 768], P(None, 'tensor')
- grad_b_query: float32 [768], P('tensor')
- grad_w_key: float32 [768, 768], P(None, 'tensor')
- grad_w_value: float32 [768, 768], P(None, 'tensor')
- grad_b_value: float32 [768], P('tensor')
- grad_w_out: float32 [768, 768], P('tensor')
- grad_b_out: float32 [768], replicated
- grad_gain_one: float32 [768], replicated
- grad_shift_one: float32 [768], replicated
- grad_w_inner: float32 [768, 3072], P(None, 'tensor')
- grad_b_inner: float32 [3072], P('tensor')
- grad_w_outer: float32 [3072, 768], P('tensor')
- grad_b_outer: float32 [768], replicated
- grad_gain_two: float32 [768], replicated
- grad_shift_two: float32 [768], replicated
The draws below stay inside these ranges and needn't reach their ends.
Inputs may be any that keep to these rules, and one draw needn't show every extreme that they name: `segment_ids`: tokens form rows of 128 positions; a row holds one sequence with id 0, or two of 64 positions with ids 0 then 1. `pad_mask`: the real tokens of each sequence are its first ones, 4 or more.
All inputs are finite; a program needn't handle non-finite values.
Results may differ from the reference program's by a relative error of at most 0.017.
Values may be sent and summed in bfloat16 or wider, within the bound.
A program may use at most 128 MiB of HBM per device.

```python
import math
import jax
import jax.numpy as jnp
from jax import lax

D = 768
HEADS = 12
HEAD_DIM = 64
FF = 3072
SEQ = 128
TOKENS = 16384


def row_layout(key):
    row_total = TOKENS // SEQ
    base = jax.random.fold_in(key, 17)
    packed = jax.random.randint(base, (row_total,), 0, 3) == 0
    single_len = jax.random.randint(jax.random.fold_in(base, 1), (row_total,), 4, SEQ + 1)
    first_len = jax.random.randint(jax.random.fold_in(base, 2), (row_total,), 4, SEQ // 2 + 1)
    second_len = jax.random.randint(jax.random.fold_in(base, 3), (row_total,), 4, SEQ // 2 + 1)
    return (packed, single_len, first_len, second_len)


def draw_segment_ids(key, part):
    packed = row_layout(key)[0]
    places = jnp.arange(SEQ, dtype=jnp.int32)[None, :]
    ids = jnp.where(packed[:, None] & (places >= SEQ // 2), 1, 0)
    return ids.astype(jnp.int32).reshape(TOKENS)


def draw_pad_mask(key, part):
    packed, single_len, first_len, second_len = row_layout(key)
    places = jnp.arange(SEQ, dtype=jnp.int32)[None, :]
    single_real = places < single_len[:, None]
    packed_real = jnp.where(places < SEQ // 2, places < first_len[:, None], places - SEQ // 2 < second_len[:, None])
    real = jnp.where(packed[:, None], packed_real, single_real)
    return jnp.where(real, 1, 0).astype(jnp.int32).reshape(TOKENS)


def draw_cotangent(key, part):
    places = jnp.arange(TOKENS, dtype=jnp.float32)[:, None]
    scaling = 0.5 + places / TOKENS
    noise = jnp.clip(jax.random.normal(key, (TOKENS, D), jnp.float32), -4.0, 4.0)
    return (noise * scaling).astype(jnp.bfloat16)


def block_scale(own_key, shape, pieces, smallest, high):
    def one(position, blocks):
        heights = jax.random.uniform(jax.random.fold_in(jax.random.fold_in(own_key, 6), position), (blocks,), jnp.float32, smallest / len(pieces), high / len(pieces))
        return jnp.repeat(jnp.exp(heights), shape[position] // blocks).reshape((-1,) + (1,) * (len(shape) - position - 1))

    gain = one(*pieces[0])
    for cut in pieces[1:]:
        gain = gain * one(*cut)
    return gain


def centred(stream_key, shape, scale, most, split=(), held_as=jnp.bfloat16):
    array = scale * jax.random.normal(stream_key, shape, jnp.float32)
    if split:
        array = array * block_scale(stream_key, shape, split, -0.22, 0.18)
    return jnp.clip(array, -most, most).astype(held_as)


def setup_inputs(seed: int = 0) -> dict:
    streams_of = jax.random.split(jax.random.key(seed), 20)
    return {
        "block_input": centred(streams_of[0], (TOKENS, D), 1.0, 6.0, ((0, 32),)),
        "cotangent": draw_cotangent(jax.random.fold_in(streams_of[19], 71), 0),
        "segment_ids": draw_segment_ids(jax.random.fold_in(streams_of[19], 71), 0),
        "pad_mask": draw_pad_mask(jax.random.fold_in(streams_of[19], 71), 0),
        "w_query": centred(streams_of[4], (D, D), D ** -0.5, 0.21875, ((1, 4),)),
        "b_query": centred(streams_of[5], (D,), 0.3, 1.5, ((0, 4),)),
        "w_key": centred(streams_of[6], (D, D), D ** -0.5, 0.21875, ((1, 4),)),
        "w_value": centred(streams_of[7], (D, D), D ** -0.5, 0.21875, ((1, 4),)),
        "b_value": centred(streams_of[8], (D,), 0.3, 1.5, ((0, 4),)),
        "w_out": centred(streams_of[9], (D, D), (D // 16) ** -0.5, 0.875, ((0, 4),)),
        "b_out": centred(streams_of[10], (D,), 0.3, 1.5),
        "gain_one": jnp.clip(1.0 + 0.15 * jax.random.normal(streams_of[11], (D,), jnp.float32), 0.25, 1.75).astype(jnp.bfloat16),
        "shift_one": centred(streams_of[12], (D,), 0.3, 1.5),
        "w_inner": centred(streams_of[13], (D, FF), D ** -0.5, 0.21875, ((1, 4),)),
        "b_inner": centred(streams_of[14], (FF,), 0.3, 1.5, ((0, 4),)),
        "w_outer": centred(streams_of[15], (FF, D), (FF // 2) ** -0.5, 0.15625, ((0, 4),)),
        "b_outer": centred(streams_of[16], (D,), 0.3, 1.5),
        "gain_two": jnp.clip(1.0 + 0.15 * jax.random.normal(streams_of[17], (D,), jnp.float32), 0.25, 1.75).astype(jnp.bfloat16),
        "shift_two": centred(streams_of[18], (D,), 0.3, 1.5),
    }


EPSILON = 1e-05

@jax.custom_vjp
def low(v):
    return lax.optimization_barrier(v.astype(jnp.bfloat16)).astype(jnp.float32)

@jax.custom_vjp
def low_back(v):
    return v

def low_keep(v):
    return (low(v), None)

def low_pass(kept, grad):
    return (grad,)

def back_keep(v):
    return (v, None)

def back_low(kept, grad):
    return (low(grad),)
low.defvjp(low_keep, low_pass)
low_back.defvjp(back_keep, back_low)

def matmul(left_side, right_side):
    return jnp.dot(left_side, right_side, precision=lax.Precision.HIGHEST)

def layer_norm(values, gain_in, shift_in):
    center = values - lax.optimization_barrier(jnp.mean(values, axis=-1, keepdims=True))
    spread = lax.optimization_barrier(jnp.mean(center * center, axis=-1, keepdims=True))
    return center * lax.rsqrt(spread + EPSILON) * gain_in + shift_in

def split_heads(values):
    return values.reshape(values.shape[0] // SEQ, SEQ, HEADS, HEAD_DIM)

def forward(inputs, allowed, w_query, b_query, w_key, w_value, b_value, w_out, b_out, gain_one, shift_one, w_inner, b_inner, w_outer, b_outer, gain_two, shift_two):
    scaling = 1.0 / math.sqrt(HEAD_DIM)
    rounded = low(inputs)
    queries = low_back(low(matmul(rounded, w_query) + b_query))
    key_rows = low_back(low(matmul(rounded, w_key)))
    value_rows = low_back(low(matmul(rounded, w_value) + b_value))
    scores = jnp.einsum('rqhd,rkhd->rhqk', split_heads(queries), split_heads(key_rows), precision=lax.Precision.HIGHEST) * scaling
    scores = low_back(jnp.where(allowed, scores, -1e+30))
    attn_probs = low(jax.nn.softmax(scores, axis=-1))
    context = jnp.einsum('rhqk,rkhd->rqhd', attn_probs, split_heads(value_rows), precision=lax.Precision.HIGHEST)
    context = low_back(low(context.reshape(inputs.shape[0], D)))
    first_sum = low_back(matmul(context, w_out)) + b_out + inputs
    hidden = layer_norm(first_sum, gain_one, shift_one)
    pre_act = low_back(matmul(low(hidden), w_inner) + b_inner)
    activated = low(jax.nn.gelu(pre_act, approximate=False))
    second_sum = low_back(matmul(activated, w_outer)) + b_outer + hidden
    return layer_norm(second_sum, gain_two, shift_two)

def reference(block_input, cotangent, segment_ids, pad_mask, w_query, b_query, w_key, w_value, b_value, w_out, b_out, gain_one, shift_one, w_inner, b_inner, w_outer, b_outer, gain_two, shift_two):
    params = tuple((item.astype(jnp.float32) for item in (w_query, b_query, w_key, w_value, b_value, w_out, b_out, gain_one, shift_one, w_inner, b_inner, w_outer, b_outer, gain_two, shift_two)))
    block_tokens = math.gcd(TOKENS, 4096)
    block_count = TOKENS // block_tokens
    input_blocks = block_input.astype(jnp.float32).reshape(block_count, block_tokens, D)
    cot_blocks = cotangent.astype(jnp.float32).reshape(block_count, block_tokens, D)
    seg_blocks = segment_ids.reshape(block_count, block_tokens // SEQ, SEQ)
    pad_blocks = pad_mask.reshape(block_count, block_tokens // SEQ, SEQ)

    def scan_step(totals, item):
        block_rows, cot_rows, seg_rows, pad_rows = item
        allowed = ((seg_rows[:, :, None] == seg_rows[:, None, :]) & (pad_rows[:, None, :] == 1))[:, None]

        def run_block(inputs, *weights_in):
            return forward(inputs, allowed, *weights_in)
        result, pullback = jax.vjp(run_block, block_rows, *params)
        pulled = pullback(cot_rows)
        totals = tuple((first + second for first, second in zip(totals, pulled[1:])))
        return (totals, (result, pulled[0]))
    initial = tuple((jnp.zeros(item.shape, jnp.float32) for item in params))
    totals, (results, input_grads) = lax.scan(scan_step, initial, (input_blocks, cot_blocks, seg_blocks, pad_blocks))
    output = results.reshape(TOKENS, D).astype(jnp.bfloat16)
    grad_input = input_grads.reshape(TOKENS, D)
    return (output, grad_input, totals[0], totals[1], totals[2], totals[3], totals[4], totals[5], totals[6], totals[7], totals[8], totals[9], totals[10], totals[11], totals[12], totals[13], totals[14])
```

```python
import functools
import math

import jax
import jax.numpy as jnp
from jax import lax
from jax.experimental import pallas as pl
from jax.experimental.pallas import tpu as pltpu
from jax.sharding import PartitionSpec as P

HEAD_DIM = 64
SEQ = 128
EPSILON = 1e-05
MASKED = -1e30
BF = jnp.bfloat16
F32 = jnp.float32
MESH = pl.DeviceIdType.MESH
GROUP = 8


def places():
    dp = lax.axis_index("dp")
    z = lax.axis_index("tensor")
    core = dp % 2
    along_x = (dp // 2) % 2
    along_y = (dp // 4) % 2
    peers = {
        "c": {"dp": dp + 1 - 2 * core, "tensor": z},
        "x": {"dp": dp + 2 - 4 * along_x, "tensor": z},
        "y": {"dp": dp + 4 - 8 * along_y, "tensor": z},
        1: {"dp": dp, "tensor": z + 1 - 2 * (z % 2)},
        2: {"dp": dp, "tensor": (z + 2) % 4},
        3: {"dp": dp, "tensor": 3 - z},
    }
    return dp, z, core, along_x, along_y, peers


def outer_peers(dp, z, outer):
    found = []
    weight = GROUP
    while weight < GROUP * outer:
        bit = (dp // weight) % 2
        found.append({"dp": dp + weight - 2 * weight * bit, "tensor": z})
        weight *= 2
    return found


def greet(peer_list):
    barrier = pltpu.get_barrier_semaphore()
    for peer in peer_list:
        pl.semaphore_signal(barrier, inc=1, device_id=peer, device_id_type=MESH)
    pl.semaphore_wait(barrier, len(peer_list))


def rows(start, size):
    return pl.ds(pl.multiple_of(start, 16), size)


class Spread:
    def __init__(self, block, half, send, recv):
        _, _, core, ax, ay, peers = places()
        base = core * half
        part = half // 2
        quarter = part // 2
        eighth = quarter // 2
        first = base + ax * quarter
        second = base + part + ay * quarter
        self.steps = []
        plan = (
            ((rows(first + ay * eighth, eighth), "y"), (rows(second + ax * eighth, eighth), "x")),
            ((rows(first, quarter), "x"), (rows(second, quarter), "y")),
            ((rows(base, half), "c"),),
        )
        place = 0
        for step in plan:
            copies = []
            for span, name in step:
                copies.append(
                    pltpu.make_async_remote_copy(
                        src_ref=block.at[span],
                        dst_ref=block.at[span],
                        send_sem=send.at[place],
                        recv_sem=recv.at[place],
                        device_id=peers[name],
                        device_id_type=MESH,
                    )
                )
                place += 1
            self.steps.append(copies)
        self.own = (rows(first + ay * eighth, eighth), rows(second + ax * eighth, eighth))

    def start(self, step):
        for copy in self.steps[step]:
            copy.start()

    def finish(self, step):
        for copy in self.steps[step]:
            copy.wait_recv()

    def drain(self):
        for step in self.steps:
            for copy in step:
                copy.wait_send()


def gather_kernel(own_refs, out, zsend, zrecv, send, recv, local):
    kinds = len(own_refs)
    dp, z, core, ax, ay, peers = places()
    locals_ = []
    for k in range(kinds):
        copy = pltpu.make_async_copy(own_refs[k], out.at[k, 0], local.at[k])
        copy.start()
        locals_.append(copy)
    greet([peers[name] for name in ("c", "x", "y", 1, 2, 3)])
    half = own_refs[0].shape[0] // 2
    spreads = {}
    crossing = {}
    for k in range(kinds):
        for j in (1, 2, 3):
            spreads[k, j] = Spread(out.at[k, j], half, send.at[k, j - 1], recv.at[k, j - 1])
            crossing[k, j] = [
                pltpu.make_async_remote_copy(
                    src_ref=own_refs[k].at[span],
                    dst_ref=out.at[k, j, span],
                    send_sem=zsend.at[k, j - 1, piece],
                    recv_sem=zrecv.at[k, j - 1, piece],
                    device_id=peers[j],
                    device_id_type=MESH,
                )
                for piece, span in enumerate(spreads[k, j].own)
            ]
    order = [(k, j) for k in range(kinds) for j in (1, 2, 3)]
    for item in order:
        for copy in crossing[item]:
            copy.start()
    total = len(order)
    for turn in range(total + 3):
        if turn < total:
            item = order[turn]
            for copy in crossing[item]:
                copy.wait_recv()
            spreads[item].start(0)
        for lag in (1, 2):
            if 0 <= turn - lag < total:
                item = order[turn - lag]
                spreads[item].finish(lag - 1)
                spreads[item].start(lag)
        if 0 <= turn - 3 < total:
            spreads[order[turn - 3]].finish(2)
    for item in order:
        for copy in crossing[item]:
            copy.wait_send()
        spreads[item].drain()
    for copy in locals_:
        copy.wait()


def gather_body(a_ref, b_ref, c_ref, out, zsend, zrecv, send, recv, local):
    gather_kernel([a_ref, b_ref, c_ref], out, zsend, zrecv, send, recv, local)


def gather_weights(own_a, own_b, own_c):
    side = own_a.shape
    return pl.pallas_call(
        gather_body,
        out_shape=jax.ShapeDtypeStruct((3, 4) + side, BF),
        in_specs=[pl.BlockSpec(memory_space=pltpu.VMEM)] * 3,
        out_specs=pl.BlockSpec(memory_space=pltpu.VMEM),
        scratch_shapes=[
            pltpu.SemaphoreType.DMA((3, 3, 2)),
            pltpu.SemaphoreType.DMA((3, 3, 2)),
            pltpu.SemaphoreType.DMA((3, 3, 5)),
            pltpu.SemaphoreType.DMA((3, 3, 5)),
            pltpu.SemaphoreType.DMA((3,)),
        ],
        compiler_params=pltpu.CompilerParams(
            collective_id=0, has_side_effects=True, vmem_limit_bytes=60 * 2**20
        ),
        name="gather_weights",
    )(own_a, own_b, own_c)


def plus(left, right):
    return (left.astype(F32) + right.astype(F32)).astype(BF)


class Fold:
    def __init__(self, held, from_core, from_one, from_two, send, recv):
        _, _, core, ax, ay, peers = places()
        half = held.shape[0]
        part, quarter, eighth = half // 2, half // 4, half // 8
        self.held = held
        self.from_core = from_core
        self.from_one = from_one
        self.from_two = from_two
        self.quarter, self.eighth = quarter, eighth
        self.give_one = (rows((1 - ax) * quarter, quarter), rows(part + (1 - ay) * quarter, quarter))
        self.keep_one = (rows(ax * quarter, quarter), rows(part + ay * quarter, quarter))
        self.give_two = (
            rows(ax * quarter + (1 - ay) * eighth, eighth),
            rows(part + ay * quarter + (1 - ax) * eighth, eighth),
        )
        self.keep_two = (
            rows(ax * quarter + ay * eighth, eighth),
            rows(part + ay * quarter + ax * eighth, eighth),
        )
        self.inside = (rows((1 - ay) * eighth, eighth), rows((1 - ax) * eighth, eighth))
        self.inside_keep = (rows(ay * eighth, eighth), rows(ax * eighth, eighth))
        self.one = [
            pltpu.make_async_remote_copy(
                src_ref=held.at[self.give_one[p]],
                dst_ref=from_one.at[p],
                send_sem=send.at[p],
                recv_sem=recv.at[p],
                device_id=peers["xy"[p]],
                device_id_type=MESH,
            )
            for p in (0, 1)
        ]
        self.two = [
            pltpu.make_async_remote_copy(
                src_ref=held.at[self.give_two[p]],
                dst_ref=from_two.at[p],
                send_sem=send.at[2 + p],
                recv_sem=recv.at[2 + p],
                device_id=peers["yx"[p]],
                device_id_type=MESH,
            )
            for p in (0, 1)
        ]

    def step_core(self, own):
        for spans in (self.give_one, self.keep_one):
            for p in (0, 1):
                span = spans[p]
                self.held[span] = plus(own[span], self.from_core[span])
            if spans is self.give_one:
                for copy in self.one:
                    copy.start()

    def step_one(self):
        for copy in self.one:
            copy.wait_recv()
        for p in (0, 1):
            self.held[self.give_two[p]] = plus(self.held[self.give_two[p]], self.from_one[p, self.inside[p]])
            self.two[p].start()
        for p in (0, 1):
            self.held[self.keep_two[p]] = plus(self.held[self.keep_two[p]], self.from_one[p, self.inside_keep[p]])

    def step_two(self, result):
        for p in (0, 1):
            self.two[p].wait_recv()
            result[p * self.eighth : (p + 1) * self.eighth] = plus(self.held[self.keep_two[p]], self.from_two[p])

    def drain(self):
        for copy in self.one + self.two:
            copy.wait_send()


class Everyone:
    def __init__(self, total, landing, send, recv, peer_list):
        self.total, self.landing = total, landing
        self.copies = [
            pltpu.make_async_remote_copy(
                src_ref=total.at[step],
                dst_ref=landing.at[step],
                send_sem=send.at[step],
                recv_sem=recv.at[step],
                device_id=peer,
                device_id_type=MESH,
            )
            for step, peer in enumerate(peer_list)
        ]

    def start(self, step):
        self.copies[step].start()

    def finish(self, step):
        self.copies[step].wait_recv()
        self.total[step + 1] = self.total[step] + self.landing[step]

    def drain(self):
        for copy in self.copies:
            copy.wait_send()


def reduce_body(
    outer,
    grads, small, out, small_out,
    held, from_core, from_one, from_two, zone, from_z, outer_in, totals, landing,
    csend, crecv, fsend, frecv, zsend, zrecv, asend, arecv, osend, orecv, ssend, srecv,
):
    dp, z, core, ax, ay, peers = places()
    others = outer_peers(dp, z, outer)
    everyone = [peers[name] for name in ("c", "x", "y", 1, 2)] + others
    greet([peers[name] for name in ("c", "x", "y", 1, 2, 3)] + others)
    kinds = grads.shape[0]
    half = grads.shape[2] // 2
    eighth = half // 8
    order = [(k, j) for k in range(kinds) for j in (1, 2, 3, 0)]
    mine, theirs = rows(core * half, half), rows((1 - core) * half, half)
    swaps = {
        (k, j): pltpu.make_async_remote_copy(
            src_ref=grads.at[k, j, theirs],
            dst_ref=from_core.at[k, j],
            send_sem=csend.at[k, j],
            recv_sem=crecv.at[k, j],
            device_id=peers["c"],
            device_id_type=MESH,
        )
        for k, j in order
    }
    folds = {
        (k, j): Fold(held.at[k, j], from_core.at[k, j], from_one.at[k, j], from_two.at[k, j], fsend.at[k, j], frecv.at[k, j])
        for k, j in order
    }
    crossing = {
        (k, j): pltpu.make_async_remote_copy(
            src_ref=zone.at[k, j],
            dst_ref=from_z.at[k, j - 1],
            send_sem=zsend.at[k, j - 1],
            recv_sem=zrecv.at[k, j - 1],
            device_id=peers[j],
            device_id_type=MESH,
        )
        for k, j in order
        if j
    }
    spreads = [Spread(out.at[k], half, asend.at[k], arecv.at[k]) for k in range(kinds)]
    tiny = Everyone(totals, landing, ssend, srecv, everyone)
    totals[0] = small[...]
    tiny.start(0)
    for item in order:
        swaps[item].start()
    total = len(order)

    def settle(k):
        for j in (1, 2, 3):
            crossing[k, j].wait_recv()
        summed = zone[k, 0].astype(F32)
        for j in (1, 2, 3):
            summed = summed + from_z[k, j - 1].astype(F32)
        for step, peer in enumerate(others):
            outer_in[k, step, 0] = summed.astype(BF)
            copy = pltpu.make_async_remote_copy(
                src_ref=outer_in.at[k, step, 0],
                dst_ref=outer_in.at[k, step, 1],
                send_sem=osend.at[k, step],
                recv_sem=orecv.at[k, step],
                device_id=peer,
                device_id_type=MESH,
            )
            copy.start()
            copy.wait()
            summed = outer_in[k, step, 0].astype(F32) + outer_in[k, step, 1].astype(F32)
        for p in (0, 1):
            out[k, spreads[k].own[p]] = summed[p * eighth : (p + 1) * eighth].astype(BF)
        spreads[k].start(0)

    later = []
    for turn in range(total + 8):
        if turn < total:
            item = order[turn]
            swaps[item].wait_recv()
            folds[item].step_core(grads.at[item[0], item[1], mine])
        if 0 <= turn - 1 < total:
            folds[order[turn - 1]].step_one()
        if 0 <= turn - 2 < total:
            item = order[turn - 2]
            folds[item].step_two(zone.at[item[0], item[1]])
            if item[1]:
                crossing[item].start()
        if turn - 3 >= 0 and (turn - 3) % 4 == 3 and turn - 3 < total:
            settle((turn - 3) // 4)
        for step in (0, 1, 2):
            back = turn - 4 - step
            if back >= 0 and back % 4 == 3 and back < total:
                k = back // 4
                spreads[k].finish(step)
                if step < 2:
                    spreads[k].start(step + 1)
        if turn >= 1 and turn - 1 < len(everyone):
            tiny.finish(turn - 1)
            if turn < len(everyone):
                tiny.start(turn)
    small_out[...] = totals[len(everyone)]
    for item in order:
        swaps[item].wait_send()
        folds[item].drain()
        if item[1]:
            crossing[item].wait_send()
    for spread in spreads:
        spread.drain()
    tiny.drain()


def reduce_grads(grads, small, outer):
    kinds, slots, height, width = grads.shape
    half = height // 2
    steps = 5 + int(math.log2(outer))
    more = max(steps - 5, 1)
    dma = pltpu.SemaphoreType.DMA
    return pl.pallas_call(
        functools.partial(reduce_body, outer),
        out_shape=(
            jax.ShapeDtypeStruct((kinds, height, width), BF),
            jax.ShapeDtypeStruct(small.shape, F32),
        ),
        in_specs=[pl.BlockSpec(memory_space=pltpu.VMEM)] * 2,
        out_specs=(pl.BlockSpec(memory_space=pltpu.VMEM),) * 2,
        scratch_shapes=[
            pltpu.VMEM((kinds, slots, half, width), BF),
            pltpu.VMEM((kinds, slots, half, width), BF),
            pltpu.VMEM((kinds, slots, 2, half // 4, width), BF),
            pltpu.VMEM((kinds, slots, 2, half // 8, width), BF),
            pltpu.VMEM((kinds, slots, half // 4, width), BF),
            pltpu.VMEM((kinds, 3, half // 4, width), BF),
            pltpu.VMEM((kinds, more, 2, half // 4, width), BF),
            pltpu.VMEM((steps + 1,) + small.shape, F32),
            pltpu.VMEM((steps,) + small.shape, F32),
            dma((kinds, slots)), dma((kinds, slots)),
            dma((kinds, slots, 4)), dma((kinds, slots, 4)),
            dma((kinds, 3)), dma((kinds, 3)),
            dma((kinds, 5)), dma((kinds, 5)),
            dma((kinds, more)), dma((kinds, more)),
            dma((steps,)), dma((steps,)),
        ],
        compiler_params=pltpu.CompilerParams(
            collective_id=1, has_side_effects=True, vmem_limit_bytes=63 * 2**20
        ),
        name="reduce_grads",
    )(grads, small)


def layer_norm(values, gain_in, shift_in):
    center = values - jnp.mean(values, axis=-1, keepdims=True)
    spread = jnp.mean(center * center, axis=-1, keepdims=True)
    return center * lax.rsqrt(spread + EPSILON) * gain_in + shift_in


def gelu_exact(values):
    return jax.nn.gelu(values, approximate=False)


def dot(spec, left, right):
    return jnp.einsum(spec, left, right, preferred_element_type=F32)


def local(
    outer, block_input, cotangent, segment_ids, pad_mask,
    w_query, b_query, w_key, w_value, b_value, w_out, b_out, gain_one, shift_one,
    w_inner, b_inner, w_outer, b_outer, gain_two, shift_two,
):
    tokens, width = block_input.shape
    cols = w_query.shape[1]
    heads = cols // HEAD_DIM
    z = lax.axis_index("tensor")
    slot_shard = jnp.stack([z, z + 1 - 2 * (z % 2), (z + 2) % 4, 3 - z])
    own_a = jnp.concatenate([w_query.T, w_key.T, w_value.T, w_out], axis=0)
    weights = gather_weights(own_a, w_inner, w_outer)
    bias = lax.all_gather(jnp.concatenate([b_query, b_value, b_inner]), "tensor")[slot_shard].astype(F32)
    zero = jnp.zeros((4, cols), F32)
    qkv_bias = jnp.concatenate([bias[:, :cols], zero, bias[:, cols : 2 * cols]], axis=1)
    inner_bias = bias[:, 2 * cols :]
    start = z * tokens
    seg_rows = lax.dynamic_slice(segment_ids, (start,), (tokens,)).reshape(-1, SEQ)
    pad_rows = lax.dynamic_slice(pad_mask, (start,), (tokens,)).reshape(-1, SEQ)
    row_count = tokens // SEQ
    qkv = (dot("td,jed->jte", block_input, weights[0, :, : 3 * cols]) + qkv_bias[:, None]).astype(BF)
    split = lambda v: v.reshape(4, row_count, SEQ, heads, HEAD_DIM)
    query, key, value = (split(qkv[:, :, i * cols : (i + 1) * cols]) for i in range(3))
    allowed = (seg_rows[:, :, None] == seg_rows[:, None, :]) & (pad_rows[:, None, :] == 1)
    scaling = 1.0 / math.sqrt(HEAD_DIM)
    scores = jnp.where(allowed[None, :, None], dot("jrqhd,jrkhd->jrhqk", query, key) * scaling, MASKED)
    probs = jax.nn.softmax(scores, axis=-1)
    probs_low = probs.astype(BF)
    context = dot("jrhqk,jrkhd->jrqhd", probs_low, value).astype(BF).reshape(4, tokens, cols)
    first_sum = dot("jtc,jcd->td", context, weights[0, :, 3 * cols :]) + b_out.astype(F32) + block_input.astype(F32)
    hidden, first_pull = jax.vjp(layer_norm, first_sum, gain_one.astype(F32), shift_one.astype(F32))
    hidden_low = hidden.astype(BF)
    pre_act = dot("td,jdf->jtf", hidden_low, weights[1]) + inner_bias[:, None]
    activated_full, gelu_pull = jax.vjp(gelu_exact, pre_act)
    activated = activated_full.astype(BF)
    second_sum = dot("jtf,jfd->td", activated, weights[2]) + b_outer.astype(F32) + hidden
    output, second_pull = jax.vjp(layer_norm, second_sum, gain_two.astype(F32), shift_two.astype(F32))
    d_second, grad_gain_two, grad_shift_two = second_pull(cotangent.astype(F32))
    grad_b_outer = jnp.sum(d_second, axis=0)
    d_second_low = d_second.astype(BF)
    grad_outer = dot("jtf,td->jfd", activated, d_second_low)
    d_pre = gelu_pull(dot("td,jfd->jtf", d_second_low, weights[2]))[0].astype(BF)
    grad_inner = dot("td,jtf->jdf", hidden_low, d_pre)
    grad_b_inner = jnp.sum(d_pre, axis=1, dtype=F32)
    d_hidden = dot("jtf,jdf->td", d_pre, weights[1]) + d_second
    d_first, grad_gain_one, grad_shift_one = first_pull(d_hidden)
    grad_b_out = jnp.sum(d_first, axis=0)
    d_first_low = d_first.astype(BF)
    grad_out = dot("jtc,td->jcd", context, d_first_low)
    d_context = split(dot("td,jcd->jtc", d_first_low, weights[0, :, 3 * cols :]).astype(BF))
    d_probs = dot("jrqhd,jrkhd->jrhqk", d_context, value)
    d_value = dot("jrhqk,jrqhd->jrkhd", probs_low, d_context)
    inner = jnp.sum(d_probs * probs, axis=-1, keepdims=True)
    d_scores = (probs * (d_probs - inner)).astype(BF)
    d_query = dot("jrhqk,jrkhd->jrqhd", d_scores, key) * scaling
    d_key = dot("jrhqk,jrqhd->jrkhd", d_scores, query) * scaling
    d_qkv = jnp.concatenate([v.astype(BF).reshape(4, tokens, cols) for v in (d_query, d_key, d_value)], axis=2)
    grad_qkv = dot("jte,td->jed", d_qkv, block_input)
    grad_bias = jnp.sum(d_qkv, axis=1, dtype=F32)
    grad_input = dot("jte,jed->td", d_qkv, weights[0, :, : 3 * cols]) + d_first
    grads = jnp.stack(
        [grad_outer.astype(BF), grad_inner.astype(BF), jnp.concatenate([grad_qkv, grad_out], axis=1).astype(BF)]
    )
    by_shard = jnp.zeros((4, 2 * cols), F32).at[slot_shard].set(
        jnp.concatenate([grad_bias[:, :cols], grad_bias[:, 2 * cols :]], axis=1)
    )
    inner_by_shard = jnp.zeros_like(grad_b_inner).at[slot_shard].set(grad_b_inner)
    small = jnp.concatenate(
        [
            jnp.stack([grad_b_out, grad_gain_one, grad_shift_one, grad_b_outer, grad_gain_two, grad_shift_two]),
            jnp.zeros((2, width), F32),
            jnp.pad(by_shard, ((0, 0), (0, width - 2 * cols))),
            inner_by_shard,
        ]
    )
    summed, small = reduce_grads(grads, small, outer)
    summed = summed.astype(F32)
    own = lax.dynamic_slice(small, (8 + z, 0), (1, width))[0]
    own_inner = lax.dynamic_slice(small, (12 + z, 0), (1, width))[0]
    return (
        output.astype(BF),
        grad_input,
        summed[2, :cols].T,
        own[:cols],
        summed[2, cols : 2 * cols].T,
        summed[2, 2 * cols : 3 * cols].T,
        own[cols : 2 * cols],
        summed[2, 3 * cols :],
        small[0],
        small[1],
        small[2],
        summed[1],
        own_inner,
        summed[0],
        small[3],
        small[4],
        small[5],
    )


def solution(mesh):
    outer = mesh.shape["dp"] // GROUP
    row, col, both, rep = P("tensor", None), P(None, "tensor"), P(("dp", "tensor"), None), P()
    part = P("tensor")
    return jax.shard_map(
        functools.partial(local, outer),
        mesh=mesh,
        in_specs=(
            both, both, P("dp"), P("dp"), col, part, col, col, part, row, rep, rep, rep,
            col, part, row, rep, rep, rep,
        ),
        out_specs=(
            both, both, col, part, col, col, part, row, rep, rep, rep, col, part, row, rep, rep, rep,
        ),
        check_vma=False,
    )
```

```python
import functools
import math

import jax
import jax.numpy as jnp
from jax import lax
from jax.experimental import pallas as pl
from jax.experimental.pallas import tpu as pltpu
from jax.sharding import PartitionSpec as P

HEAD_DIM = 64
SEQ = 128
EPSILON = 1e-05
MASKED = -1e30
BF = jnp.bfloat16
F32 = jnp.float32
MESH = pl.DeviceIdType.MESH
GROUP = 8


def places():
    dp = lax.axis_index("dp")
    z = lax.axis_index("tensor")
    core = dp % 2
    along_x = (dp // 2) % 2
    along_y = (dp // 4) % 2
    peers = {
        "c": {"dp": dp + 1 - 2 * core, "tensor": z},
        "x": {"dp": dp + 2 - 4 * along_x, "tensor": z},
        "y": {"dp": dp + 4 - 8 * along_y, "tensor": z},
        1: {"dp": dp, "tensor": z + 1 - 2 * (z % 2)},
        2: {"dp": dp, "tensor": (z + 2) % 4},
        3: {"dp": dp, "tensor": 3 - z},
    }
    return dp, z, core, along_x, along_y, peers


def outer_peers(dp, z, outer):
    found = []
    weight = GROUP
    while weight < GROUP * outer:
        bit = (dp // weight) % 2
        found.append({"dp": dp + weight - 2 * weight * bit, "tensor": z})
        weight *= 2
    return found


def greet(peer_list):
    barrier = pltpu.get_barrier_semaphore()
    for peer in peer_list:
        pl.semaphore_signal(barrier, inc=1, device_id=peer, device_id_type=MESH)
    pl.semaphore_wait(barrier, len(peer_list))


def rows(start, size):
    return pl.ds(pl.multiple_of(start, 16), size)


class Spread:
    def __init__(self, block, half, send, recv):
        _, _, core, ax, ay, peers = places()
        base = core * half
        part = half // 2
        quarter = part // 2
        eighth = quarter // 2
        first = base + ax * quarter
        second = base + part + ay * quarter
        self.steps = []
        plan = (
            ((rows(first + ay * eighth, eighth), "y"), (rows(second + ax * eighth, eighth), "x")),
            ((rows(first, quarter), "x"), (rows(second, quarter), "y")),
            ((rows(base, half), "c"),),
        )
        place = 0
        for step in plan:
            copies = []
            for span, name in step:
                copies.append(
                    pltpu.make_async_remote_copy(
                        src_ref=block.at[span],
                        dst_ref=block.at[span],
                        send_sem=send.at[place],
                        recv_sem=recv.at[place],
                        device_id=peers[name],
                        device_id_type=MESH,
                    )
                )
                place += 1
            self.steps.append(copies)
        self.own = (rows(first + ay * eighth, eighth), rows(second + ax * eighth, eighth))

    def start(self, step):
        for copy in self.steps[step]:
            copy.start()

    def finish(self, step):
        for copy in self.steps[step]:
            copy.wait_recv()

    def drain(self):
        for step in self.steps:
            for copy in step:
                copy.wait_send()


def plus(left, right):
    return (left.astype(F32) + right.astype(F32)).astype(BF)


class Fold:
    def __init__(self, held, from_core, from_one, from_two, send, recv):
        _, _, core, ax, ay, peers = places()
        half = held.shape[0]
        part, quarter, eighth = half // 2, half // 4, half // 8
        self.held = held
        self.from_core = from_core
        self.from_one = from_one
        self.from_two = from_two
        self.quarter, self.eighth = quarter, eighth
        self.give_one = (rows((1 - ax) * quarter, quarter), rows(part + (1 - ay) * quarter, quarter))
        self.keep_one = (rows(ax * quarter, quarter), rows(part + ay * quarter, quarter))
        self.give_two = (
            rows(ax * quarter + (1 - ay) * eighth, eighth),
            rows(part + ay * quarter + (1 - ax) * eighth, eighth),
        )
        self.keep_two = (
            rows(ax * quarter + ay * eighth, eighth),
            rows(part + ay * quarter + ax * eighth, eighth),
        )
        self.inside = (rows((1 - ay) * eighth, eighth), rows((1 - ax) * eighth, eighth))
        self.inside_keep = (rows(ay * eighth, eighth), rows(ax * eighth, eighth))
        self.one = [
            pltpu.make_async_remote_copy(
                src_ref=held.at[self.give_one[p]],
                dst_ref=from_one.at[p],
                send_sem=send.at[p],
                recv_sem=recv.at[p],
                device_id=peers["xy"[p]],
                device_id_type=MESH,
            )
            for p in (0, 1)
        ]
        self.two = [
            pltpu.make_async_remote_copy(
                src_ref=held.at[self.give_two[p]],
                dst_ref=from_two.at[p],
                send_sem=send.at[2 + p],
                recv_sem=recv.at[2 + p],
                device_id=peers["yx"[p]],
                device_id_type=MESH,
            )
            for p in (0, 1)
        ]

    def step_core(self, own):
        for spans in (self.give_one, self.keep_one):
            for p in (0, 1):
                span = spans[p]
                self.held[span] = plus(own[span], self.from_core[span])
            if spans is self.give_one:
                for copy in self.one:
                    copy.start()

    def step_one(self):
        for copy in self.one:
            copy.wait_recv()
        for p in (0, 1):
            self.held[self.give_two[p]] = plus(self.held[self.give_two[p]], self.from_one[p, self.inside[p]])
            self.two[p].start()
        for p in (0, 1):
            self.held[self.keep_two[p]] = plus(self.held[self.keep_two[p]], self.from_one[p, self.inside_keep[p]])

    def step_two(self, result):
        for p in (0, 1):
            self.two[p].wait_recv()
            result[p * self.eighth : (p + 1) * self.eighth] = plus(self.held[self.keep_two[p]], self.from_two[p])

    def drain(self):
        for copy in self.one + self.two:
            copy.wait_send()


class Everyone:
    def __init__(self, total, landing, send, recv, peer_list):
        self.total, self.landing = total, landing
        self.copies = [
            pltpu.make_async_remote_copy(
                src_ref=total.at[step],
                dst_ref=landing.at[step],
                send_sem=send.at[step],
                recv_sem=recv.at[step],
                device_id=peer,
                device_id_type=MESH,
            )
            for step, peer in enumerate(peer_list)
        ]

    def start(self, step):
        self.copies[step].start()

    def finish(self, step):
        self.copies[step].wait_recv()
        self.total[step + 1] = self.total[step] + self.landing[step]

    def drain(self):
        for copy in self.copies:
            copy.wait_send()


DIMS = {"NN": ((1,), (0,)), "NT": ((1,), (1,)), "TN": ((0,), (0,))}
SCALING = 1.0 / math.sqrt(HEAD_DIM)


def dot(left, right, form="NN"):
    return lax.dot_general(left, right, (DIMS[form], ((), ())), preferred_element_type=F32)


def column_sum(values):
    return jnp.sum(values, axis=0, keepdims=True)


def row_mean(values):
    return jnp.mean(values, axis=-1, keepdims=True)


def chunks(count, size, body):
    def run(step, carry):
        body(rows(step * size, size))
        return carry

    lax.fori_loop(0, count // size, run, 0)


def block_body(
    outer,
    x_hbm, cot_hbm, seg_ref, pad_ref, vec_ref, own_a, own_b, own_c,
    out_hbm, grad_in_hbm, summed_out, small_out,
    weights, x_ref, cot, masks, vecs, qkv, ctx, probs, norm_one, scale_one, hidden_low, act, slope,
    acc, d_norm, d_low, d_ctx,
    grads, from_core, from_one, from_two, zone, from_z, outer_in, totals, landing,
    gz_send, gz_recv, g_send, g_recv, v_send, v_recv, local_sem,
    csend, crecv, fsend, frecv, zsend, zrecv, asend, arecv, osend, orecv, ssend, srecv, credit,
):
    dp, z, core, ax, ay, peers = places()
    others = outer_peers(dp, z, outer)
    everyone = [peers[name] for name in ("c", "x", "y", 1, 2)] + others
    tokens, width = x_ref.shape
    side = own_a.shape[0]
    half = side // 2
    eighth = half // 8
    cols = side // 4
    heads = cols // HEAD_DIM
    row_count = tokens // SEQ
    shard_of = {0: z, 1: peers[1]["tensor"], 2: peers[2]["tensor"], 3: peers[3]["tensor"]}
    own_refs = [own_a, own_b, own_c]

    local_copies = [
        pltpu.make_async_copy(x_hbm, x_ref, local_sem.at[0]),
        pltpu.make_async_copy(own_a, weights.at[0, 0], local_sem.at[1]),
        pltpu.make_async_copy(vec_ref, vecs.at[0], local_sem.at[2]),
        pltpu.make_async_copy(own_b, weights.at[1, 0], local_sem.at[3]),
        pltpu.make_async_copy(own_c, weights.at[2, 0], local_sem.at[4]),
        pltpu.make_async_copy(cot_hbm, cot, local_sem.at[5]),
    ]
    for copy in local_copies:
        copy.start()
    greet([peers[name] for name in ("c", "x", "y", 1, 2, 3)] + others)

    spreads, crossing, vec_copies = {}, {}, {}
    gathered = [(k, j) for k in range(3) for j in (1, 2, 3)]
    for k, j in gathered:
        spreads[k, j] = Spread(weights.at[k, j], half, g_send.at[k, j - 1], g_recv.at[k, j - 1])
        crossing[k, j] = [
            pltpu.make_async_remote_copy(
                src_ref=own_refs[k].at[span],
                dst_ref=weights.at[k, j, span],
                send_sem=gz_send.at[k, j - 1, piece],
                recv_sem=gz_recv.at[k, j - 1, piece],
                device_id=peers[j],
                device_id_type=MESH,
            )
            for piece, span in enumerate(spreads[k, j].own)
        ]
    for j in (1, 2, 3):
        vec_copies[j] = pltpu.make_async_remote_copy(
            src_ref=vec_ref,
            dst_ref=vecs.at[j],
            send_sem=v_send.at[j - 1],
            recv_sem=v_recv.at[j - 1],
            device_id=peers[j],
            device_id_type=MESH,
        )
    for k, j in gathered:
        for copy in crossing[k, j]:
            copy.start()
        if k == 0:
            vec_copies[j].start()

    def gather_turn(turn):
        total = len(gathered)
        if turn < total:
            item = gathered[turn]
            for copy in crossing[item]:
                copy.wait_recv()
            spreads[item].start(0)
        for lag in (1, 2):
            if 0 <= turn - lag < total:
                item = gathered[turn - lag]
                spreads[item].finish(lag - 1)
                spreads[item].start(lag)
        if 0 <= turn - 3 < total:
            spreads[gathered[turn - 3]].finish(2)

    def vector(row, slot=0):
        return vecs[slot, row : row + 1, :].astype(F32)

    def build_masks():
        for r in range(row_count):
            place = pl.ds(z * row_count + r, 1)
            seg = jnp.broadcast_to(seg_ref[place, :].astype(F32), (SEQ, SEQ))
            pad = jnp.broadcast_to(pad_ref[place, :], (SEQ, SEQ))
            allowed = (seg == seg.T) & (pad == 1)
            masks[r] = jnp.where(allowed, 0.0, MASKED)

    def project(j):
        bias = vector(0, j)[:, : 3 * cols]
        qkv[j] = (dot(x_ref[...], weights[0, j, : 3 * cols], "NT") + bias).astype(BF)

    def attend(j):
        def one(r, carry):
            span = rows(r * SEQ, SEQ)
            joined = qkv[j, span]
            found = []
            for h in range(heads):
                q, k, v = (joined[:, i * cols + h * HEAD_DIM : i * cols + (h + 1) * HEAD_DIM] for i in range(3))
                scores = dot(q, k, "NT") * SCALING + masks[r]
                weight = jnp.exp(scores - jnp.max(scores, axis=-1, keepdims=True))
                prob = (weight * (1.0 / jnp.sum(weight, axis=-1, keepdims=True))).astype(BF)
                probs[j, r, h] = prob
                found.append(dot(prob, v).astype(BF))
            ctx[j, span] = jnp.concatenate(found, axis=1)
            return carry

        lax.fori_loop(0, row_count, one, 0)

    def project_out():
        total = dot(ctx[0], weights[0, 0, 3 * cols :])
        for j in (1, 2, 3):
            total = total + dot(ctx[j], weights[0, j, 3 * cols :])
        acc[...] = total

    def norm_first():
        b_out, gain, shift = vector(2), vector(3), vector(4)

        def body(span):
            value = acc[span] + b_out + x_ref[span].astype(F32)
            center = value - row_mean(value)
            scale = lax.rsqrt(row_mean(center * center) + EPSILON)
            normal = center * scale
            norm_one[span] = normal
            scale_one[span] = scale
            hidden_low[span] = (normal * gain + shift).astype(BF)

        chunks(tokens, 128, body)

    def feed_in(j):
        bias = vector(1, j)

        def body(span):
            pre = dot(hidden_low[span], weights[1, j]) + bias
            cumulative = 0.5 + 0.5 * lax.erf(pre * (1.0 / math.sqrt(2.0)))
            density = jnp.exp(pre * pre * -0.5) * (1.0 / math.sqrt(2.0 * math.pi))
            act[j, span] = (pre * cumulative).astype(BF)
            slope[j, span] = (cumulative + pre * density).astype(BF)

        chunks(tokens, 128, body)

    def feed_out(j):
        part = dot(act[j], weights[2, j])
        acc[...] = part if j == 0 else acc[...] + part

    def small_add(row, value):
        totals[0, pl.ds(row, 1), : value.shape[1]] += value

    def norm_second():
        gain_a, shift_a, b_outer = vector(3), vector(4), vector(5)
        gain, shift = vector(6), vector(7)

        def body(span):
            value = acc[span] + b_outer + (norm_one[span] * gain_a + shift_a)
            center = value - row_mean(value)
            scale = lax.rsqrt(row_mean(center * center) + EPSILON)
            normal = center * scale
            given = cot[span].astype(F32)
            cot[span] = (normal * gain + shift).astype(BF)
            pulled = given * gain
            grad = scale * (pulled - row_mean(pulled) - normal * row_mean(pulled * normal))
            d_norm[span] = grad
            d_low[span] = grad.astype(BF)
            small_add(3, column_sum(grad))
            small_add(4, column_sum(given * normal))
            small_add(5, column_sum(given))

        chunks(tokens, 128, body)

    def feed_out_back(j):
        def body(span):
            grad = (dot(d_low[span], weights[2, j], "NT") * slope[j, span].astype(F32)).astype(BF)
            act[j, span] = grad
            small_add(12 + shard_of[j], column_sum(grad.astype(F32)))

        chunks(tokens, 256, body)

    def feed_in_back(j, first):
        part = dot(act[j], weights[1, j], "NT")
        acc[...] = part if first else acc[...] + part

    def norm_first_back():
        gain = vector(3)

        def body(span):
            given = acc[span] + d_norm[span]
            normal = norm_one[span]
            pulled = given * gain
            grad = scale_one[span] * (pulled - row_mean(pulled) - normal * row_mean(pulled * normal))
            d_norm[span] = grad
            d_low[span] = grad.astype(BF)
            small_add(0, column_sum(grad))
            small_add(1, column_sum(given * normal))
            small_add(2, column_sum(given))

        chunks(tokens, 128, body)

    def attend_back(j):
        d_ctx[...] = dot(d_low[...], weights[0, j, 3 * cols :], "NT").astype(BF)

        def one(r, carry):
            span = rows(r * SEQ, SEQ)
            joined = qkv[j, span]
            given = d_ctx[span]
            found = [[], [], []]
            for h in range(heads):
                q, k, v = (joined[:, i * cols + h * HEAD_DIM : i * cols + (h + 1) * HEAD_DIM] for i in range(3))
                d_out = given[:, h * HEAD_DIM : (h + 1) * HEAD_DIM]
                prob = probs[j, r, h]
                wide = prob.astype(F32)
                d_prob = dot(d_out, v, "NT")
                inner = jnp.sum(d_prob * wide, axis=-1, keepdims=True)
                d_score = (wide * (d_prob - inner)).astype(BF)
                found[0].append((dot(d_score, k) * SCALING).astype(BF))
                found[1].append((dot(d_score, q, "TN") * SCALING).astype(BF))
                found[2].append(dot(prob, d_out, "TN").astype(BF))
            joined_grad = jnp.concatenate(found[0] + found[1] + found[2], axis=1)
            qkv[j, span] = joined_grad
            small_add(8 + shard_of[j], column_sum(joined_grad.astype(F32)))
            return carry

        lax.fori_loop(0, row_count, one, 0)

    def input_back(j):
        d_norm[...] = d_norm[...] + dot(qkv[j], weights[0, j, : 3 * cols])

    mine, theirs = rows(core * half, half), rows((1 - core) * half, half)
    mine_cols = pl.ds(pl.multiple_of(core * half, 128), half)
    their_cols = pl.ds(pl.multiple_of((1 - core) * half, 128), half)
    order = [(k, j) for k in range(3) for j in (1, 2, 3, 0)]
    swaps = {
        (k, j): pltpu.make_async_remote_copy(
            src_ref=grads.at[k % 2, j, theirs],
            dst_ref=from_core.at[k % 2, j],
            send_sem=csend.at[k, j],
            recv_sem=crecv.at[k, j],
            device_id=peers["c"],
            device_id_type=MESH,
        )
        for k, j in order
    }
    folds = {
        (k, j): Fold(
            grads.at[k % 2, j, mine], from_core.at[k % 2, j], from_one.at[k, j], from_two.at[k, j],
            fsend.at[k, j], frecv.at[k, j],
        )
        for k, j in order
    }
    over = {
        (k, j): pltpu.make_async_remote_copy(
            src_ref=zone.at[k, j],
            dst_ref=from_z.at[k, j - 1],
            send_sem=zsend.at[k, j - 1],
            recv_sem=zrecv.at[k, j - 1],
            device_id=peers[j],
            device_id_type=MESH,
        )
        for k, j in order
        if j
    }
    sums = [Spread(summed_out.at[k], half, asend.at[k], arecv.at[k]) for k in range(3)]
    tiny = Everyone(totals, landing, ssend, srecv, everyone)

    def settle(k):
        for j in (1, 2, 3):
            over[k, j].wait_recv()
        summed = zone[k, 0].astype(F32)
        for j in (1, 2, 3):
            summed = summed + from_z[k, j - 1].astype(F32)
        for step, peer in enumerate(others):
            outer_in[k, step, 0] = summed.astype(BF)
            copy = pltpu.make_async_remote_copy(
                src_ref=outer_in.at[k, step, 0],
                dst_ref=outer_in.at[k, step, 1],
                send_sem=osend.at[k, step],
                recv_sem=orecv.at[k, step],
                device_id=peer,
                device_id_type=MESH,
            )
            copy.start()
            copy.wait()
            summed = outer_in[k, step, 0].astype(F32) + outer_in[k, step, 1].astype(F32)
        for p in (0, 1):
            summed_out[k, sums[k].own[p]] = summed[p * eighth : (p + 1) * eighth].astype(BF)
        sums[k].start(0)

    def drain(item):
        swaps[item].wait_send()
        folds[item].drain()

    def grad_block(k, j):
        if k == 0:
            for span, picked in ((theirs, their_cols), (mine, mine_cols)):
                grads[0, j, span] = dot(act[j, :, picked], d_low[...], "TN").astype(BF)
                if span is theirs:
                    swaps[k, j].start()
        elif k == 1:
            for span, picked in ((theirs, their_cols), (mine, mine_cols)):
                grads[1, j, span] = dot(hidden_low[:, picked], act[j], "TN").astype(BF)
                if span is theirs:
                    swaps[k, j].start()
        else:
            drain((0, j))
            pl.semaphore_wait(credit.at[j], 1)
            grads[0, j, : 3 * cols] = dot(qkv[j], x_ref[...], "TN").astype(BF)
            grads[0, j, 3 * cols :] = dot(ctx[j], d_low[...], "TN").astype(BF)
            swaps[k, j].start()

    def reduce_turn(turn):
        total = len(order)
        if turn < total:
            item = order[turn]
            swaps[item].wait_recv()
            folds[item].step_core(grads.at[item[0] % 2, item[1], mine])
            if item[0] == 0:
                pl.semaphore_signal(credit.at[item[1]], inc=1, device_id=peers["c"], device_id_type=MESH)
        if 0 <= turn - 1 < total:
            folds[order[turn - 1]].step_one()
        if 0 <= turn - 2 < total:
            item = order[turn - 2]
            folds[item].step_two(zone.at[item[0], item[1]])
            if item[1]:
                over[item].start()
        if turn - 3 >= 0 and (turn - 3) % 4 == 3 and turn - 3 < total:
            settle((turn - 3) // 4)
        for step in (0, 1, 2):
            back = turn - 4 - step
            if back >= 0 and back % 4 == 3 and back < total:
                k = back // 4
                sums[k].finish(step)
                if step < 2:
                    sums[k].start(step + 1)

    local_copies[0].wait()
    local_copies[1].wait()
    local_copies[2].wait()
    build_masks()
    totals[0] = jnp.zeros_like(totals[0])
    project(0)
    gather_turn(0)
    attend(0)
    gather_turn(1)
    gather_turn(2)
    for j in (1, 2, 3):
        gather_turn(2 + j)
        if j == 1:
            for i in (1, 2, 3):
                vec_copies[i].wait_recv()
        project(j)
        attend(j)
    project_out()
    norm_first()
    local_copies[3].wait()
    feed_in(0)
    for j in (1, 2, 3):
        gather_turn(5 + j)
        feed_in(j)
    local_copies[4].wait()
    feed_out(0)
    for j in (1, 2, 3):
        gather_turn(8 + j)
        feed_out(j)
    local_copies[5].wait()
    norm_second()
    out_copy = pltpu.make_async_copy(cot, out_hbm, local_sem.at[0])
    out_copy.start()

    for turn, (k, j) in enumerate(order):
        if k == 2:
            if j == 1:
                norm_first_back()
            attend_back(j)
        grad_block(k, j)
        if k == 0:
            feed_out_back(j)
        elif k == 1:
            feed_in_back(j, j == 1)
        else:
            input_back(j)
        reduce_turn(turn)
    grad_in_copy = pltpu.make_async_copy(d_norm, grad_in_hbm, local_sem.at[1])
    grad_in_copy.start()
    tiny.start(0)
    for extra in range(6):
        if extra < len(everyone):
            tiny.finish(extra)
            if extra + 1 < len(everyone):
                tiny.start(extra + 1)
        reduce_turn(len(order) + extra)
    for extra in range(6, len(everyone)):
        tiny.finish(extra)
        if extra + 1 < len(everyone):
            tiny.start(extra + 1)
    small_out[...] = totals[len(everyone)]

    for item in gathered:
        for copy in crossing[item]:
            copy.wait_send()
        spreads[item].drain()
    for j in (1, 2, 3):
        vec_copies[j].wait_send()
    for item in order:
        if item[0]:
            drain(item)
        if item[1]:
            over[item].wait_send()
    for spread in sums:
        spread.drain()
    tiny.drain()
    out_copy.wait()
    grad_in_copy.wait()


def block(outer, x, cot, seg, pad, vec, own_a, own_b, own_c):
    tokens, width = x.shape
    side = own_a.shape[0]
    half, cols = side // 2, side // 4
    heads = cols // HEAD_DIM
    row_count = tokens // SEQ
    steps = 5 + int(math.log2(outer))
    more = max(steps - 5, 1)
    outer_rows = half // 4 if outer > 1 else 16
    dma = pltpu.SemaphoreType.DMA
    vmem = pltpu.VMEM
    any_space = pl.BlockSpec(memory_space=pl.ANY)
    in_vmem = pl.BlockSpec(memory_space=pltpu.VMEM)
    return pl.pallas_call(
        functools.partial(block_body, outer),
        out_shape=(
            jax.ShapeDtypeStruct((tokens, width), BF),
            jax.ShapeDtypeStruct((tokens, width), F32),
            jax.ShapeDtypeStruct((3, side, width), BF),
            jax.ShapeDtypeStruct((16, width), F32),
        ),
        in_specs=[any_space, any_space, in_vmem, in_vmem, any_space, any_space, any_space, any_space],
        out_specs=(any_space, any_space, in_vmem, in_vmem),
        scratch_shapes=[
            vmem((3, 4, side, width), BF),
            vmem((tokens, width), BF),
            vmem((tokens, width), BF),
            vmem((row_count, SEQ, SEQ), F32),
            vmem((4, 16, width), BF),
            vmem((4, tokens, 3 * cols), BF),
            vmem((4, tokens, cols), BF),
            vmem((4, row_count, heads, SEQ, SEQ), BF),
            vmem((tokens, width), F32),
            vmem((tokens, 1), F32),
            vmem((tokens, width), BF),
            vmem((4, tokens, side), BF),
            vmem((4, tokens, side), BF),
            vmem((tokens, width), F32),
            vmem((tokens, width), F32),
            vmem((tokens, width), BF),
            vmem((tokens, cols), BF),
            vmem((2, 4, side, width), BF),
            vmem((2, 4, half, width), BF),
            vmem((3, 4, 2, half // 4, width), BF),
            vmem((3, 4, 2, half // 8, width), BF),
            vmem((3, 4, half // 4, width), BF),
            vmem((3, 3, half // 4, width), BF),
            vmem((3, more, 2, outer_rows, width), BF),
            vmem((steps + 1, 16, width), F32),
            vmem((steps, 16, width), F32),
            dma((3, 3, 2)), dma((3, 3, 2)), dma((3, 3, 5)), dma((3, 3, 5)), dma((3,)), dma((3,)), dma((6,)),
            dma((3, 4)), dma((3, 4)), dma((3, 4, 4)), dma((3, 4, 4)), dma((3, 3)), dma((3, 3)),
            dma((3, 5)), dma((3, 5)), dma((3, more)), dma((3, more)), dma((steps,)), dma((steps,)),
            pltpu.SemaphoreType.REGULAR((4,)),
        ],
        compiler_params=pltpu.CompilerParams(
            collective_id=0, has_side_effects=True, vmem_limit_bytes=67043328
        ),
        name="block",
    )(x, cot, seg, pad, vec, own_a, own_b, own_c)


def local(
    outer, block_input, cotangent, segment_ids, pad_mask,
    w_query, b_query, w_key, w_value, b_value, w_out, b_out, gain_one, shift_one,
    w_inner, b_inner, w_outer, b_outer, gain_two, shift_two,
):
    tokens, width = block_input.shape
    cols = w_query.shape[1]
    z = lax.axis_index("tensor")
    own_a = jnp.concatenate([w_query.T, w_key.T, w_value.T, w_out], axis=0)
    zero = jnp.zeros((cols,), BF)
    vec = jnp.pad(
        jnp.stack(
            [
                jnp.concatenate([b_query, zero, b_value, zero]), b_inner,
                b_out, gain_one, shift_one, b_outer, gain_two, shift_two,
            ]
        ),
        ((0, 8), (0, 0)),
    )
    output, grad_input, summed, small = block(
        outer, block_input, cotangent, segment_ids.reshape(-1, SEQ), pad_mask.reshape(-1, SEQ),
        vec, own_a, w_inner, w_outer,
    )
    summed = summed.astype(F32)
    own = lax.dynamic_slice(small, (8 + z, 0), (1, width))[0]
    own_inner = lax.dynamic_slice(small, (12 + z, 0), (1, width))[0]
    return (
        output,
        grad_input,
        summed[2, :cols].T,
        own[:cols],
        summed[2, cols : 2 * cols].T,
        summed[2, 2 * cols : 3 * cols].T,
        own[2 * cols : 3 * cols],
        summed[2, 3 * cols :],
        small[0],
        small[1],
        small[2],
        summed[1],
        own_inner,
        summed[0],
        small[3],
        small[4],
        small[5],
    )


def solution(mesh):
    outer = mesh.shape["dp"] // GROUP
    row, col, both, rep = P("tensor", None), P(None, "tensor"), P(("dp", "tensor"), None), P()
    part = P("tensor")
    return jax.shard_map(
        functools.partial(local, outer),
        mesh=mesh,
        in_specs=(
            both, both, P("dp"), P("dp"), col, part, col, col, part, row, rep, rep, rep,
            col, part, row, rep, rep, rep,
        ),
        out_specs=(
            both, both, col, part, col, col, part, row, rep, rep, rep, col, part, row, rep, rep, rep,
        ),
        check_vma=False,
    )
```

```python
import functools
import math

import jax
import jax.numpy as jnp
from jax import lax
from jax.experimental import pallas as pl
from jax.experimental.pallas import tpu as pltpu
from jax.sharding import PartitionSpec as P

HEAD_DIM = 64
SEQ = 128
EPSILON = 1e-05
MASKED = -1e30
BF = jnp.bfloat16
F32 = jnp.float32
MESH = pl.DeviceIdType.MESH
GROUP = 8
WIDE = (2,)


def places():
    dp = lax.axis_index("dp")
    z = lax.axis_index("tensor")
    core = dp % 2
    along_x = (dp // 2) % 2
    along_y = (dp // 4) % 2
    peers = {
        "c": {"dp": dp + 1 - 2 * core, "tensor": z},
        "x": {"dp": dp + 2 - 4 * along_x, "tensor": z},
        "y": {"dp": dp + 4 - 8 * along_y, "tensor": z},
        1: {"dp": dp, "tensor": z + 1 - 2 * (z % 2)},
        2: {"dp": dp, "tensor": (z + 2) % 4},
        3: {"dp": dp, "tensor": 3 - z},
    }
    return dp, z, core, along_x, along_y, peers


def line_order(z):
    low, high = z % 2, z // 2
    middle = low + high - 2 * low * high
    shards = (z, z + 1 - 2 * low, (1 - middle) * ((z + 2) % 4) + middle * (3 - z), middle * ((z + 2) % 4) + (1 - middle) * (3 - z))
    return middle, shards, (0, 1, 3 - middle, 3 - middle)


def outer_peers(dp, z, outer):
    found = []
    weight = GROUP
    while weight < GROUP * outer:
        bit = (dp // weight) % 2
        found.append({"dp": dp + weight - 2 * weight * bit, "tensor": z})
        weight *= 2
    return found


def rows(start, size):
    return pl.ds(pl.multiple_of(start, 16), size)


class Spread:
    def __init__(self, block, half, send, recv, wide=False):
        _, _, core, ax, ay, peers = places()
        base = core * half
        part = half // 2
        quarter = part // 2
        eighth = quarter // 2
        first = base + ax * quarter
        second = base + part + ay * quarter
        self.steps = []
        plan = (
            ((rows(first + ay * eighth, eighth), "y"), (rows(second + ax * eighth, eighth), "x")),
            ((rows(first, quarter), "x"), (rows(second, quarter), "y")),
            ((rows(base, half), "c"),),
        )
        place = 0
        for number, step in enumerate(plan):
            copies = []
            for span, name in () if wide and number == 0 else step:
                copies.append(
                    pltpu.make_async_remote_copy(
                        src_ref=block.at[span],
                        dst_ref=block.at[span],
                        send_sem=send.at[place],
                        recv_sem=recv.at[place],
                        device_id=peers[name],
                        device_id_type=MESH,
                    )
                )
                place += 1
            self.steps.append(copies)
        self.own = (rows(first + ay * eighth, eighth), rows(second + ax * eighth, eighth))
        if wide:
            self.own = (rows(first, quarter), rows(second, quarter))

    def start(self, step):
        for copy in self.steps[step]:
            copy.start()

    def finish(self, step):
        for copy in self.steps[step]:
            copy.wait_recv()

    def drain(self):
        for step in self.steps:
            for copy in step:
                copy.wait_send()


def plus(left, right):
    return (left.astype(F32) + right.astype(F32)).astype(BF)


class Fold:
    def __init__(self, held, from_core, from_one, from_two, send, recv):
        _, _, core, ax, ay, peers = places()
        half = held.shape[0]
        part, quarter, eighth = half // 2, half // 4, half // 8
        self.held = held
        self.from_core = from_core
        self.from_one = from_one
        self.from_two = from_two
        self.quarter, self.eighth = quarter, eighth
        self.give_one = (rows((1 - ax) * quarter, quarter), rows(part + (1 - ay) * quarter, quarter))
        self.keep_one = (rows(ax * quarter, quarter), rows(part + ay * quarter, quarter))
        self.give_two = (
            rows(ax * quarter + (1 - ay) * eighth, eighth),
            rows(part + ay * quarter + (1 - ax) * eighth, eighth),
        )
        self.keep_two = (
            rows(ax * quarter + ay * eighth, eighth),
            rows(part + ay * quarter + ax * eighth, eighth),
        )
        self.inside = (rows((1 - ay) * eighth, eighth), rows((1 - ax) * eighth, eighth))
        self.inside_keep = (rows(ay * eighth, eighth), rows(ax * eighth, eighth))
        self.one = [
            pltpu.make_async_remote_copy(
                src_ref=held.at[self.give_one[p]],
                dst_ref=from_one.at[p],
                send_sem=send.at[p],
                recv_sem=recv.at[p],
                device_id=peers["xy"[p]],
                device_id_type=MESH,
            )
            for p in (0, 1)
        ]
        self.two = [
            pltpu.make_async_remote_copy(
                src_ref=held.at[self.give_two[p]],
                dst_ref=from_two.at[p],
                send_sem=send.at[2 + p],
                recv_sem=recv.at[2 + p],
                device_id=peers["yx"[p]],
                device_id_type=MESH,
            )
            for p in (0, 1)
        ]

    def step_core(self, own):
        for spans in (self.give_one, self.keep_one):
            for p in (0, 1):
                span = spans[p]
                self.held[span] = plus(own[span], self.from_core[span])
            if spans is self.give_one:
                for copy in self.one:
                    copy.start()

    def step_one(self):
        for copy in self.one:
            copy.wait_recv()
        for p in (0, 1):
            self.held[self.give_two[p]] = plus(self.held[self.give_two[p]], self.from_one[p, self.inside[p]])
            self.two[p].start()
        for p in (0, 1):
            self.held[self.keep_two[p]] = plus(self.held[self.keep_two[p]], self.from_one[p, self.inside_keep[p]])

    def step_two(self, result):
        for p in (0, 1):
            self.two[p].wait_recv()
            result[p * self.eighth : (p + 1) * self.eighth] = plus(self.held[self.keep_two[p]], self.from_two[p])

    def drain(self):
        for copy in self.one + self.two:
            copy.wait_send()


class Everyone:
    def __init__(self, total, landing, send, recv, peer_list):
        self.total, self.landing = total, landing
        self.copies = [
            pltpu.make_async_remote_copy(
                src_ref=total.at[step],
                dst_ref=landing.at[step],
                send_sem=send.at[step],
                recv_sem=recv.at[step],
                device_id=peer,
                device_id_type=MESH,
            )
            for step, peer in enumerate(peer_list)
        ]

    def start(self, step):
        self.copies[step].start()

    def finish(self, step):
        self.copies[step].wait_recv()
        self.total[step + 1] = self.total[step] + self.landing[step]

    def drain(self):
        for copy in self.copies:
            copy.wait_send()


DIMS = {"NN": ((1,), (0,)), "NT": ((1,), (1,)), "TN": ((0,), (0,))}
SCALING = 1.0 / math.sqrt(HEAD_DIM)


def dot(left, right, form="NN"):
    return lax.dot_general(left, right, (DIMS[form], ((), ())), preferred_element_type=F32)


def column_sum(values):
    return jnp.sum(values, axis=0, keepdims=True)


def row_mean(values):
    return jnp.mean(values, axis=-1, keepdims=True)


def chunks(count, size, body):
    def run(step, carry):
        body(rows(step * size, size))
        return carry

    lax.fori_loop(0, count // size, run, 0)


def block_body(
    outer,
    x_hbm, cot_hbm, seg_ref, pad_ref, w_query, w_key, w_value, w_out, own_b, own_c,
    b_query, b_value, b_inner, b_out, gain_one, shift_one, b_outer, gain_two, shift_two,
    out_hbm, grad_in_hbm, summed_hbm, small_hbm,
    weights, x_ref, cot, masks, vecs, qkv, ctx, probs, norm_one, scale_one, hidden_low, act, shared,
    acc, d_norm, d_low, d_ctx,
    grads, from_core, from_one, from_two, zone, from_z, outer_in, totals, landing,
    gz_send, gz_recv, g_send, g_recv, v_send, v_recv, local_sem, early_sem,
    csend, crecv, fsend, frecv, zsend, zrecv, asend, arecv, osend, orecv, ssend, srecv, credit,
):
    dp, z, core, ax, ay, peers = places()
    others = outer_peers(dp, z, outer)
    everyone = [peers[name] for name in ("c", "x", "y", 1, 2)] + others
    tokens, width = x_ref.shape
    side = own_b.shape[0]
    half = side // 2
    eighth = half // 8
    cols = side // 4
    heads = cols // HEAD_DIM
    row_count = tokens // SEQ
    slope = [shared.at[u * tokens : (u + 1) * tokens] for u in range(4)]
    summed_out = [shared.at[k * side : (k + 1) * side] for k in range(3)]
    middle, shard_of, landing_place = line_order(z)
    line = {u: {"dp": dp, "tensor": shard_of[u]} for u in (1, 2, 3)}

    local_copies = [
        pltpu.make_async_copy(x_hbm, x_ref, local_sem.at[0]),
        pltpu.make_async_copy(w_out, weights.at[0, 0, 3 * cols :], local_sem.at[1]),
        pltpu.make_async_copy(own_b, weights.at[1, 0], local_sem.at[2]),
        pltpu.make_async_copy(own_c, weights.at[2, 0], local_sem.at[3]),
        pltpu.make_async_copy(cot_hbm, cot, local_sem.at[4]),
    ] + [
        pltpu.make_async_copy(ref, weights.at[0, 0, part * cols : (part + 1) * cols], local_sem.at[5 + part])
        for part, ref in enumerate((w_query, w_key, w_value))
    ]
    for number in (5, 6, 7, 1, 0, 2, 3, 4):
        local_copies[number].start()
    barrier = pltpu.get_barrier_semaphore()
    greeted = [peers[name] for name in ("c", "x", "y", 1, 2, 3)] + others
    for peer in greeted:
        pl.semaphore_signal(barrier, inc=1, device_id=peer, device_id_type=MESH)

    spreads, arrivals, vec_copies = {}, {}, {}
    gathered = [(k, u) for k in range(3) for u in (1, 2, 3)]

    def hop(k, source, target, peer):
        found = []
        for piece, span in enumerate(spreads[k, target].own):
            src = weights.at[k, source, span]
            if source == 0 and k:
                src = (None, own_b, own_c)[k].at[span]
            found.append(
                pltpu.make_async_remote_copy(
                    src_ref=src,
                    dst_ref=weights.at[k, target, span],
                    send_sem=gz_send.at[k, target - 1, 0 if peer is peers[1] else 1, piece],
                    recv_sem=gz_recv.at[k, target - 1, piece],
                    device_id=peer,
                    device_id_type=MESH,
                )
            )
        return found

    for k, u in gathered:
        spreads[k, u] = Spread(weights.at[k, u], half, g_send.at[k, u - 1], g_recv.at[k, u - 1], k in WIDE)
    near = {k: hop(k, 0, 1, peers[1]) for k in range(3)}
    across = {(k, 2): hop(k, 0, 2, peers[3]) for k in range(3)}
    across.update({(k, 3): hop(k, 1, 3, peers[3]) for k in range(3)})
    onward = {(k, u): hop(k, u, u, peers[1]) for k in range(3) for u in (2, 3)}
    for u in (1, 2, 3):
        vec_copies[u] = pltpu.make_async_remote_copy(
            src_ref=vecs.at[0],
            dst_ref=vecs.at[landing_place[u]],
            send_sem=v_send.at[u - 1],
            recv_sem=v_recv.at[landing_place[u] - 1],
            device_id=line[u],
            device_id_type=MESH,
        )

    def begin(copies):
        for copy in copies:
            copy.start()

    def send_own(k):
        begin(near[k])
        pl.when(middle == 1)(lambda: begin(across[k, 2]))

    def line_turn(turn):
        if turn >= len(gathered):
            return
        k, u = gathered[turn]
        for copy in {1: near[k], 2: across[k, 2], 3: across[k, 3]}[u]:
            copy.wait_recv()

        def further():
            if u == 1:
                begin(across[k, 3])
            else:
                begin(onward[k, u])

        pl.when(middle == 1)(further)
        if u == 2 and k < 2:
            send_own(k + 1)

    def gather_turn(turn):
        total = len(gathered)
        if turn == 0:
            line_turn(0)
        if turn == 1:
            line_turn(1)
        if turn < total:
            spreads[gathered[turn]].start(1 if gathered[turn][0] in WIDE else 0)
        for lag in (1, 2):
            if 0 <= turn - lag < total:
                item = gathered[turn - lag]
                if lag == 1 and item[0] in WIDE:
                    spreads[item].finish(1)
                    spreads[item].start(2)
                elif item[0] not in WIDE:
                    spreads[item].finish(lag - 1)
                    spreads[item].start(lag)
        line_turn(turn + 1 if turn else 9)
        back = turn - 3
        if 0 <= back < total and gathered[back][0] not in WIDE:
            spreads[gathered[back]].finish(2)
        back = turn - 2
        if 0 <= back < total and gathered[back][0] in WIDE:
            spreads[gathered[back]].finish(2)

    def vector(row, slot=0):
        return vecs[slot, row : row + 1, :]

    def build_masks():
        for r in range(row_count):
            place = pl.ds(z * row_count + r, 1)
            seg = jnp.broadcast_to(seg_ref[place, :].astype(F32), (SEQ, SEQ))
            pad = jnp.broadcast_to(pad_ref[place, :], (SEQ, SEQ))
            allowed = (seg == seg.T) & (pad == 1)
            masks[r] = jnp.where(allowed, 0.0, MASKED)

    def project(j):
        bias = vector(0, j)[:, : 3 * cols]

        def body(span):
            qkv[j, span] = (dot(x_ref[span], weights[0, j, : 3 * cols], "NT") + bias).astype(BF)

        chunks(tokens, 256, body)

    def head(joined, part, h):
        return joined[:, part * cols + h * HEAD_DIM : part * cols + (h + 1) * HEAD_DIM]

    units = [(r, h) for r in range(row_count) for h in range(heads)]

    def spans(r):
        return slice(r * SEQ, (r + 1) * SEQ)

    def attend(j):
        joined = [qkv[j, spans(r)] for r in range(row_count)]
        scores = [
            dot(head(joined[r], 0, h), head(joined[r], 1, h), "NT") * SCALING + masks[r] for r, h in units
        ]
        found = []
        for (r, h), score in zip(units, scores):
            weight = jnp.exp(score - jnp.max(score, axis=-1, keepdims=True))
            found.append((weight * (1.0 / jnp.sum(weight, axis=-1, keepdims=True))).astype(BF))
        mixed = []
        for (r, h), prob in zip(units, found):
            probs[j, r, h] = prob
            mixed.append(dot(prob, head(joined[r], 2, h)).astype(BF))
        for r in range(row_count):
            ctx[j, spans(r)] = jnp.concatenate(mixed[r * heads : (r + 1) * heads], axis=1)

    def project_out():
        total = dot(ctx[0], weights[0, 0, 3 * cols :])
        for j in (1, 2, 3):
            total = total + dot(ctx[j], weights[0, j, 3 * cols :])
        acc[...] = total

    def norm_first():
        b_out, gain, shift = vector(2), vector(3), vector(4)

        def body(span):
            value = acc[span] + b_out + x_ref[span].astype(F32)
            center = value - row_mean(value)
            scale = lax.rsqrt(row_mean(center * center) + EPSILON)
            normal = center * scale
            norm_one[span] = normal
            scale_one[span] = scale
            hidden_low[span] = (normal * gain + shift).astype(BF)

        chunks(tokens, 128, body)

    def feed_in(j):
        bias = vector(1, j)

        def body(span):
            pre = dot(hidden_low[span], weights[1, j]) + bias
            cumulative = 0.5 + 0.5 * lax.erf(pre * (1.0 / math.sqrt(2.0)))
            density = jnp.exp(pre * pre * -0.5) * (1.0 / math.sqrt(2.0 * math.pi))
            act[j, span] = (pre * cumulative).astype(BF)
            slope[j][span] = (cumulative + pre * density).astype(BF)

        chunks(tokens, 128, body)

    def feed_out(j):
        part = dot(act[j], weights[2, j])
        acc[...] = part if j == 0 else acc[...] + part

    def small_add(row, value):
        totals[0, pl.ds(row, 1), : value.shape[1]] += value

    def norm_second():
        gain_a, shift_a, b_outer = vector(3), vector(4), vector(5)
        gain, shift = vector(6), vector(7)

        def body(span):
            value = acc[span] + b_outer + (norm_one[span] * gain_a + shift_a)
            center = value - row_mean(value)
            scale = lax.rsqrt(row_mean(center * center) + EPSILON)
            normal = center * scale
            given = cot[span].astype(F32)
            cot[span] = (normal * gain + shift).astype(BF)
            pulled = given * gain
            grad = scale * (pulled - row_mean(pulled) - normal * row_mean(pulled * normal))
            d_norm[span] = grad
            d_low[span] = grad.astype(BF)
            small_add(3, column_sum(grad))
            small_add(4, column_sum(given * normal))
            small_add(5, column_sum(given))

        chunks(tokens, 128, body)

    def feed_out_back(j):
        def body(span):
            grad = (dot(d_low[span], weights[2, j], "NT") * slope[j][span].astype(F32)).astype(BF)
            act[j, span] = grad
            small_add(12 + shard_of[j], column_sum(grad.astype(F32)))

        chunks(tokens, 256, body)

    def feed_in_back(j, first):
        def body(span):
            part = dot(act[j, span], weights[1, j], "NT")
            acc[span] = part if first else acc[span] + part

        chunks(tokens, 256, body)

    def norm_first_back():
        gain = vector(3)

        def body(span):
            given = acc[span] + d_norm[span]
            normal = norm_one[span]
            pulled = given * gain
            grad = scale_one[span] * (pulled - row_mean(pulled) - normal * row_mean(pulled * normal))
            d_norm[span] = grad
            d_low[span] = grad.astype(BF)
            small_add(0, column_sum(grad))
            small_add(1, column_sum(given * normal))
            small_add(2, column_sum(given))

        chunks(tokens, 128, body)

    def attend_back(j):
        d_ctx[...] = dot(d_low[...], weights[0, j, 3 * cols :], "NT").astype(BF)
        joined = [qkv[j, spans(r)] for r in range(row_count)]
        given = [d_ctx[spans(r)] for r in range(row_count)]
        d_outs = [given[r][:, h * HEAD_DIM : (h + 1) * HEAD_DIM] for r, h in units]
        d_probs = [dot(d_out, head(joined[r], 2, h), "NT") for (r, h), d_out in zip(units, d_outs)]
        prob_list = [probs[j, r, h] for r, h in units]
        d_scores = []
        for d_prob, prob in zip(d_probs, prob_list):
            wide = prob.astype(F32)
            inner = jnp.sum(d_prob * wide, axis=-1, keepdims=True)
            d_scores.append((wide * (d_prob - inner)).astype(BF))
        d_values = [dot(prob, d_out, "TN").astype(BF) for prob, d_out in zip(prob_list, d_outs)]
        d_queries = [(dot(ds, head(joined[r], 1, h)) * SCALING).astype(BF) for (r, h), ds in zip(units, d_scores)]
        d_keys = [(dot(ds, head(joined[r], 0, h), "TN") * SCALING).astype(BF) for (r, h), ds in zip(units, d_scores)]
        total = jnp.zeros((1, 3 * cols), F32)
        for r in range(row_count):
            mine_heads = slice(r * heads, (r + 1) * heads)
            joined_grad = jnp.concatenate(d_queries[mine_heads] + d_keys[mine_heads] + d_values[mine_heads], axis=1)
            qkv[j, spans(r)] = joined_grad
            total = total + column_sum(joined_grad.astype(F32))
        small_add(8 + shard_of[j], total)

    def input_back(j):
        def body(span):
            d_norm[span] = d_norm[span] + dot(qkv[j, span], weights[0, j, : 3 * cols])

        chunks(tokens, 256, body)

    mine, theirs = rows(core * half, half), rows((1 - core) * half, half)
    mine_cols = pl.ds(pl.multiple_of(core * half, 128), half)
    their_cols = pl.ds(pl.multiple_of((1 - core) * half, 128), half)
    order = [(k, j) for k in range(3) for j in (1, 2, 3, 0)]
    swaps = {
        (k, j): pltpu.make_async_remote_copy(
            src_ref=grads.at[k % 2, j, theirs],
            dst_ref=from_core.at[k % 2, j],
            send_sem=csend.at[k, j],
            recv_sem=crecv.at[k, j],
            device_id=peers["c"],
            device_id_type=MESH,
        )
        for k, j in order
    }
    folds = {
        (k, j): Fold(
            grads.at[k % 2, j, mine], from_core.at[k % 2, j], from_one.at[k, j], from_two.at[k, j],
            fsend.at[k, j], frecv.at[k, j],
        )
        for k, j in order
    }
    over = {
        (k, j): pltpu.make_async_remote_copy(
            src_ref=zone.at[k, j],
            dst_ref=from_z.at[k, landing_place[j] - 1],
            send_sem=zsend.at[k, j - 1],
            recv_sem=zrecv.at[k, landing_place[j] - 1],
            device_id=line[j],
            device_id_type=MESH,
        )
        for k, j in order
        if j
    }
    sums = [Spread(summed_out[k], half, asend.at[k], arecv.at[k]) for k in range(3)]
    tiny = Everyone(totals, landing, ssend, srecv, everyone)

    def settle(k):
        for place in range(3):
            pltpu.make_async_remote_copy(
                src_ref=zone.at[k, 1],
                dst_ref=from_z.at[k, place],
                send_sem=zsend.at[k, place],
                recv_sem=zrecv.at[k, place],
                device_id=peers[1],
                device_id_type=MESH,
            ).wait_recv()
        summed = zone[k, 0].astype(F32)
        for j in (1, 2, 3):
            summed = summed + from_z[k, j - 1].astype(F32)
        for step, peer in enumerate(others):
            outer_in[k, step, 0] = summed.astype(BF)
            copy = pltpu.make_async_remote_copy(
                src_ref=outer_in.at[k, step, 0],
                dst_ref=outer_in.at[k, step, 1],
                send_sem=osend.at[k, step],
                recv_sem=orecv.at[k, step],
                device_id=peer,
                device_id_type=MESH,
            )
            copy.start()
            copy.wait()
            summed = outer_in[k, step, 0].astype(F32) + outer_in[k, step, 1].astype(F32)
        for p in (0, 1):
            summed_out[k][sums[k].own[p]] = summed[p * eighth : (p + 1) * eighth].astype(BF)
        sums[k].start(0)

    def drain(item):
        swaps[item].wait_send()
        folds[item].drain()

    def grad_block(k, j):
        if k == 0:
            for span, picked in ((theirs, their_cols), (mine, mine_cols)):
                grads[0, j, span] = dot(act[j, :, picked], d_low[...], "TN").astype(BF)
                if span is theirs and j:
                    swaps[k, j].start()
            feed_out_back(j)
            if j == 0:
                swaps[k, j].start()
        elif k == 1:
            for span, picked in ((theirs, their_cols), (mine, mine_cols)):
                grads[1, j, span] = dot(hidden_low[:, picked], act[j], "TN").astype(BF)
                if span is theirs:
                    swaps[k, j].start()
        else:
            drain((0, j))
            pl.semaphore_wait(credit.at[j], 1)
            grads[0, j, : 3 * cols] = dot(qkv[j], x_ref[...], "TN").astype(BF)
            grads[0, j, 3 * cols :] = dot(ctx[j], d_low[...], "TN").astype(BF)
            swaps[k, j].start()

    def reduce_turn(turn):
        total = len(order)
        if turn < total:
            item = order[turn]
            swaps[item].wait_recv()
            folds[item].step_core(grads.at[item[0] % 2, item[1], mine])
            if item[0] == 0:
                pl.semaphore_signal(credit.at[item[1]], inc=1, device_id=peers["c"], device_id_type=MESH)
        if 0 <= turn - 1 < total:
            folds[order[turn - 1]].step_one()
        if 0 <= turn - 2 < total:
            item = order[turn - 2]
            folds[item].step_two(zone.at[item[0], item[1]])
            if item[1]:
                over[item].start()
        if turn - 3 >= 0 and (turn - 3) % 4 == 3 and turn - 3 < total:
            settle((turn - 3) // 4)
        for step in (0, 1, 2):
            back = turn - 4 - step
            if back >= 0 and back % 4 == 3 and back < total:
                k = back // 4
                sums[k].finish(step)
                if step < 2:
                    sums[k].start(step + 1)
                elif k < 2:
                    copy = pltpu.make_async_copy(summed_out[k], summed_hbm.at[k], early_sem.at[k])
                    copy.start()
                    early_copies.append(copy)

    early_copies = []

    vecs[0] = jnp.zeros_like(vecs[0])
    for row, start, ref in (
        (0, 0, b_query), (0, 2 * cols, b_value), (1, 0, b_inner), (2, 0, b_out), (3, 0, gain_one),
        (4, 0, shift_one), (5, 0, b_outer), (6, 0, gain_two), (7, 0, shift_two),
    ):
        size = ref.shape[0]
        vecs[0, row : row + 1, start : start + size] = ref[...].astype(F32).reshape(1, size)
    for number in (1, 5, 6, 7):
        local_copies[number].wait()
    pl.semaphore_wait(barrier, len(greeted))
    send_own(0)
    for u in (1, 2, 3):
        vec_copies[u].start()
    build_masks()
    totals[0] = jnp.zeros_like(totals[0])
    local_copies[0].wait()
    project(0)
    gather_turn(0)
    attend(0)
    gather_turn(1)
    gather_turn(2)
    for j in (1, 2, 3):
        gather_turn(2 + j)
        if j == 1:
            for place in range(3):
                pltpu.make_async_remote_copy(
                    src_ref=vecs.at[0],
                    dst_ref=vecs.at[place + 1],
                    send_sem=v_send.at[place],
                    recv_sem=v_recv.at[place],
                    device_id=peers[1],
                    device_id_type=MESH,
                ).wait_recv()
        project(j)
        attend(j)
    project_out()
    norm_first()
    local_copies[2].wait()
    feed_in(0)
    for j in (1, 2, 3):
        gather_turn(5 + j)
        feed_in(j)
    local_copies[3].wait()
    feed_out(0)
    for j in (1, 2, 3):
        if j > 1 or 2 not in WIDE:
            gather_turn(8 + j - (2 in WIDE))
        feed_out(j)
    local_copies[4].wait()
    norm_second()
    out_copy = pltpu.make_async_copy(cot, out_hbm, local_sem.at[0])
    out_copy.start()

    for turn, (k, j) in enumerate(order):
        if k == 2:
            if j == 1:
                norm_first_back()
            attend_back(j)
        grad_block(k, j)
        if k == 1:
            feed_in_back(j, j == 1)
        elif k == 2:
            input_back(j)
        reduce_turn(turn)
    grad_in_copy = pltpu.make_async_copy(d_norm, grad_in_hbm, local_sem.at[1])
    grad_in_copy.start()
    tiny.start(0)
    for extra in range(6):
        if extra < len(everyone):
            tiny.finish(extra)
            if extra + 1 < len(everyone):
                tiny.start(extra + 1)
        reduce_turn(len(order) + extra)
    for extra in range(6, len(everyone)):
        tiny.finish(extra)
        if extra + 1 < len(everyone):
            tiny.start(extra + 1)
    small_copy = pltpu.make_async_copy(totals.at[len(everyone)], small_hbm, local_sem.at[2])
    small_copy.start()
    last_copy = pltpu.make_async_copy(summed_out[2], summed_hbm.at[2], local_sem.at[3])
    last_copy.start()

    def settled(copies):
        for copy in copies:
            copy.wait_send()

    for k in range(3):
        settled(near[k])
        for u in (2, 3):
            pl.when(middle == 1)(lambda k=k, u=u: settled(across[k, u] + onward[k, u]))
    for item in gathered:
        spreads[item].drain()
    for j in (1, 2, 3):
        vec_copies[j].wait_send()
    for item in order:
        if item[0]:
            drain(item)
        if item[1]:
            over[item].wait_send()
    for spread in sums:
        spread.drain()
    tiny.drain()
    for copy in [out_copy, grad_in_copy, small_copy, last_copy] + early_copies:
        copy.wait()


def block(outer, x, cot, seg, pad, *others):
    tokens, width = x.shape
    side = others[4].shape[0]
    half, cols = side // 2, side // 4
    heads = cols // HEAD_DIM
    row_count = tokens // SEQ
    steps = 5 + int(math.log2(outer))
    more = max(steps - 5, 1)
    outer_rows = half // 4 if outer > 1 else 16
    dma = pltpu.SemaphoreType.DMA
    vmem = pltpu.VMEM
    any_space = pl.BlockSpec(memory_space=pl.ANY)
    in_vmem = pl.BlockSpec(memory_space=pltpu.VMEM)
    return pl.pallas_call(
        functools.partial(block_body, outer),
        out_shape=(
            jax.ShapeDtypeStruct((tokens, width), BF),
            jax.ShapeDtypeStruct((tokens, width), F32),
            jax.ShapeDtypeStruct((3, side, width), BF),
            jax.ShapeDtypeStruct((16, width), F32),
        ),
        in_specs=[any_space] * 2 + [in_vmem] * 2 + [any_space] * 6 + [in_vmem] * 9,
        out_specs=(any_space,) * 4,
        scratch_shapes=[
            vmem((3, 4, side, width), BF),
            vmem((tokens, width), BF),
            vmem((tokens, width), BF),
            vmem((row_count, SEQ, SEQ), F32),
            vmem((4, 8, width), F32),
            vmem((4, tokens, 3 * cols), BF),
            vmem((4, tokens, cols), BF),
            vmem((4, row_count, heads, SEQ, SEQ), BF),
            vmem((tokens, width), F32),
            vmem((tokens, 1), F32),
            vmem((tokens, width), BF),
            vmem((4, tokens, side), BF),
            vmem((max(3 * side, 4 * tokens), side), BF),
            vmem((tokens, width), F32),
            vmem((tokens, width), F32),
            vmem((tokens, width), BF),
            vmem((tokens, cols), BF),
            vmem((2, 4, side, width), BF),
            vmem((2, 4, half, width), BF),
            vmem((3, 4, 2, half // 4, width), BF),
            vmem((3, 4, 2, half // 8, width), BF),
            vmem((3, 4, half // 4, width), BF),
            vmem((3, 3, half // 4, width), BF),
            vmem((3, more, 2, outer_rows, width), BF),
            vmem((steps + 1, 16, width), F32),
            vmem((steps, 16, width), F32),
            dma((3, 3, 2, 2)), dma((3, 3, 2)), dma((3, 3, 5)), dma((3, 3, 5)), dma((3,)), dma((3,)), dma((8,)), dma((2,)),
            dma((3, 4)), dma((3, 4)), dma((3, 4, 4)), dma((3, 4, 4)), dma((3, 3)), dma((3, 3)),
            dma((3, 5)), dma((3, 5)), dma((3, more)), dma((3, more)), dma((steps,)), dma((steps,)),
            pltpu.SemaphoreType.REGULAR((4,)),
        ],
        compiler_params=pltpu.CompilerParams(
            collective_id=0, has_side_effects=True, vmem_limit_bytes=67043328
        ),
        name="block",
    )(x, cot, seg, pad, *others)


def local(
    outer, block_input, cotangent, segment_ids, pad_mask,
    w_query, b_query, w_key, w_value, b_value, w_out, b_out, gain_one, shift_one,
    w_inner, b_inner, w_outer, b_outer, gain_two, shift_two,
):
    tokens, width = block_input.shape
    cols = w_query.shape[1]
    output, grad_input, summed, small = block(
        outer, block_input, cotangent, segment_ids.reshape(-1, SEQ), pad_mask.reshape(-1, SEQ),
        w_query.T, w_key.T, w_value.T, w_out, w_inner, w_outer,
        b_query, b_value, b_inner, b_out, gain_one, shift_one, b_outer, gain_two, shift_two,
    )
    outs = list(finish(output, grad_input, summed, small, cols))
    for place in (2, 4, 5):
        outs[place] = outs[place].T
    return tuple(outs)


def finish_body(
    out_hbm, grad_in_hbm, summed_hbm, small_ref,
    output, grad_input, g_query, gb_query, g_key, g_value, gb_value, g_out, gb_out, gg_one, gs_one,
    g_inner, gb_inner, g_outer, gb_outer, gg_two, gs_two,
    out_held, in_held, summed, wide, turned, flat, in_sem, out_sem,
):
    z = lax.axis_index("tensor")
    cols = gb_query.shape[0]
    reads = [pltpu.make_async_copy(summed_hbm.at[k], summed.at[k], in_sem.at[k]) for k in (0, 1, 2)]
    reads.append(pltpu.make_async_copy(grad_in_hbm, in_held, in_sem.at[3]))
    reads.append(pltpu.make_async_copy(out_hbm, out_held, in_sem.at[4]))
    for copy in reads:
        copy.start()
    for row, ref in ((0, gb_out), (1, gg_one), (2, gs_one), (3, gb_outer), (4, gg_two), (5, gs_two)):
        ref[...] = small_ref[row : row + 1, :].reshape(ref.shape)
    own = small_ref[pl.ds(8 + z, 1), :]
    gb_query[...] = own[:, :cols].reshape(gb_query.shape)
    gb_value[...] = own[:, 2 * cols : 3 * cols].reshape(gb_value.shape)
    gb_inner[...] = small_ref[pl.ds(12 + z, 1), :].reshape(gb_inner.shape)
    writes = []

    def write(source, target):
        copy = pltpu.make_async_copy(source, target, out_sem.at[len(writes)])
        copy.start()
        writes.append(copy)

    for k, target in ((0, g_outer), (1, g_inner)):
        reads[k].wait()
        wide[k] = summed[k].astype(F32)
        write(wide.at[k], target)
    reads[2].wait()
    for part, target in enumerate((g_query, g_key, g_value)):
        turned[part] = summed[2, part * cols : (part + 1) * cols].astype(F32)
        write(turned.at[part], target)
    flat[...] = summed[2, 3 * cols :].astype(F32)
    write(flat, g_out)
    reads[3].wait()
    write(in_held, grad_input)
    reads[4].wait()
    write(out_held, output)
    for copy in writes:
        copy.wait()


def finish(output, grad_input, summed, small, cols):
    (tokens, width), side = output.shape, summed.shape[1]
    shape = jax.ShapeDtypeStruct
    any_space = pl.BlockSpec(memory_space=pl.ANY)
    in_vmem = pl.BlockSpec(memory_space=pltpu.VMEM)
    line, short, flat, big = shape((width,), F32), shape((cols,), F32), shape((cols, width), F32), shape((side, width), F32)
    outs = (
        (shape((tokens, width), BF), 0), (shape((tokens, width), F32), 0), (flat, 0), (short, 1), (flat, 0), (flat, 0),
        (short, 1), (flat, 0), (line, 1), (line, 1), (line, 1), (big, 0), (line, 1), (big, 0),
        (line, 1), (line, 1), (line, 1),
    )
    dma = pltpu.SemaphoreType.DMA
    return pl.pallas_call(
        finish_body,
        out_shape=tuple(item for item, _ in outs),
        in_specs=[any_space, any_space, any_space, in_vmem],
        out_specs=tuple(in_vmem if held else any_space for _, held in outs),
        scratch_shapes=[
            pltpu.VMEM((tokens, width), BF),
            pltpu.VMEM((tokens, width), F32),
            pltpu.VMEM((3, side, width), BF),
            pltpu.VMEM((2, side, width), F32),
            pltpu.VMEM((3, cols, width), F32),
            pltpu.VMEM((cols, width), F32),
            dma((5,)), dma((8,)),
        ],
        compiler_params=pltpu.CompilerParams(vmem_limit_bytes=67043328),
        name="finish",
    )(output, grad_input, summed, small)


def solution(mesh):
    outer = mesh.shape["dp"] // GROUP
    row, col, both, rep = P("tensor", None), P(None, "tensor"), P(("dp", "tensor"), None), P()
    part = P("tensor")
    return jax.shard_map(
        functools.partial(local, outer),
        mesh=mesh,
        in_specs=(
            both, both, P("dp"), P("dp"), col, part, col, col, part, row, rep, rep, rep,
            col, part, row, rep, rep, rep,
        ),
        out_specs=(
            both, both, col, part, col, col, part, row, rep, rep, rep, col, part, row, rep, rep, rep,
        ),
        check_vma=False,
    )
```

```python
import functools
import math

import jax
import jax.numpy as jnp
from jax import lax
from jax.experimental import pallas as pl
from jax.experimental.pallas import tpu as pltpu
from jax.sharding import PartitionSpec as P

HEAD_DIM = 64
SEQ = 128
EPSILON = 1e-05
MASKED = -1e30
BF = jnp.bfloat16
F32 = jnp.float32
MESH = pl.DeviceIdType.MESH
GROUP = 8
WIDE = ((2, 1), (2, 3))
EARLY = ((1, 2, 3), (1,), (1,))
MERGE_TURN = (8, 8, 12)


def places():
    dp = lax.axis_index("dp")
    z = lax.axis_index("tensor")
    core = dp % 2
    along_x = (dp // 2) % 2
    along_y = (dp // 4) % 2
    peers = {
        "c": {"dp": dp + 1 - 2 * core, "tensor": z},
        "x": {"dp": dp + 2 - 4 * along_x, "tensor": z},
        "y": {"dp": dp + 4 - 8 * along_y, "tensor": z},
        1: {"dp": dp, "tensor": z + 1 - 2 * (z % 2)},
        2: {"dp": dp, "tensor": (z + 2) % 4},
        3: {"dp": dp, "tensor": 3 - z},
    }
    return dp, z, core, along_x, along_y, peers


def line_order(z):
    low, high = z % 2, z // 2
    middle = low + high - 2 * low * high
    shards = (z, z + 1 - 2 * low, (1 - middle) * ((z + 2) % 4) + middle * (3 - z), middle * ((z + 2) % 4) + (1 - middle) * (3 - z))
    return middle, shards, (0, 1, 3 - middle, 3 - middle)


def outer_peers(dp, z, outer):
    found = []
    weight = GROUP
    while weight < GROUP * outer:
        bit = (dp // weight) % 2
        found.append({"dp": dp + weight - 2 * weight * bit, "tensor": z})
        weight *= 2
    return found


def rows(start, size):
    return pl.ds(pl.multiple_of(start, 16), size)


class Spread:
    def __init__(self, block, half, send, recv, wide=False):
        _, _, core, ax, ay, peers = places()
        base = core * half
        part = half // 2
        quarter = part // 2
        eighth = quarter // 2
        first = base + ax * quarter
        second = base + part + ay * quarter
        self.steps = []
        plan = (
            ((rows(first + ay * eighth, eighth), "y"), (rows(second + ax * eighth, eighth), "x")),
            ((rows(first, quarter), "x"), (rows(second, quarter), "y")),
            ((rows(base, half), "c"),),
        )
        place = 0
        for number, step in enumerate(plan):
            copies = []
            for span, name in () if wide and number == 0 else step:
                copies.append(
                    pltpu.make_async_remote_copy(
                        src_ref=block.at[span],
                        dst_ref=block.at[span],
                        send_sem=send.at[place],
                        recv_sem=recv.at[place],
                        device_id=peers[name],
                        device_id_type=MESH,
                    )
                )
                place += 1
            self.steps.append(copies)
        self.own = (rows(first + ay * eighth, eighth), rows(second + ax * eighth, eighth))
        if wide:
            self.own = (rows(first, quarter), rows(second, quarter))

    def start(self, step):
        for copy in self.steps[step]:
            copy.start()

    def finish(self, step):
        for copy in self.steps[step]:
            copy.wait_recv()

    def drain(self):
        for step in self.steps:
            for copy in step:
                copy.wait_send()


def plus(left, right):
    return (left.astype(F32) + right.astype(F32)).astype(BF)


class Fold:
    def __init__(self, held, from_core, from_one, from_two, send, recv):
        _, _, core, ax, ay, peers = places()
        half = held.shape[0]
        part, quarter, eighth = half // 2, half // 4, half // 8
        self.held = held
        self.from_core = from_core
        self.from_one = from_one
        self.from_two = from_two
        self.quarter, self.eighth = quarter, eighth
        self.give_one = (rows((1 - ax) * quarter, quarter), rows(part + (1 - ay) * quarter, quarter))
        self.keep_one = (rows(ax * quarter, quarter), rows(part + ay * quarter, quarter))
        self.give_two = (
            rows(ax * quarter + (1 - ay) * eighth, eighth),
            rows(part + ay * quarter + (1 - ax) * eighth, eighth),
        )
        self.keep_two = (
            rows(ax * quarter + ay * eighth, eighth),
            rows(part + ay * quarter + ax * eighth, eighth),
        )
        self.inside = (rows((1 - ay) * eighth, eighth), rows((1 - ax) * eighth, eighth))
        self.inside_keep = (rows(ay * eighth, eighth), rows(ax * eighth, eighth))
        self.one = [
            pltpu.make_async_remote_copy(
                src_ref=held.at[self.give_one[p]],
                dst_ref=from_one.at[p],
                send_sem=send.at[p],
                recv_sem=recv.at[p],
                device_id=peers["xy"[p]],
                device_id_type=MESH,
            )
            for p in (0, 1)
        ]
        self.two = [
            pltpu.make_async_remote_copy(
                src_ref=held.at[self.give_two[p]],
                dst_ref=from_two.at[p],
                send_sem=send.at[2 + p],
                recv_sem=recv.at[2 + p],
                device_id=peers["yx"[p]],
                device_id_type=MESH,
            )
            for p in (0, 1)
        ]

    def step_core(self, own):
        for spans in (self.give_one, self.keep_one):
            for p in (0, 1):
                span = spans[p]
                self.held[span] = plus(own[span], self.from_core[span])
            if spans is self.give_one:
                for copy in self.one:
                    copy.start()

    def step_one(self):
        for copy in self.one:
            copy.wait_recv()

    def combine(self, parts, send):
        for spans, insides in ((self.give_two, self.inside), (self.keep_two, self.inside_keep)):
            for p in (0, 1):
                total = self.held[spans[p]].astype(F32)
                for part in parts:
                    total = total + part[p, insides[p]].astype(F32)
                self.held[spans[p]] = total.astype(BF)
                if send and spans is self.give_two:
                    self.two[p].start()

    def step_two(self, result):
        for p in (0, 1):
            self.two[p].wait_recv()
            result[p * self.eighth : (p + 1) * self.eighth] = plus(self.held[self.keep_two[p]], self.from_two[p])

    def drain(self, halved):
        for copy in self.one + (self.two if halved else []):
            copy.wait_send()


class Everyone:
    def __init__(self, total, landing, send, recv, peer_list):
        self.total, self.landing = total, landing
        self.copies = [
            pltpu.make_async_remote_copy(
                src_ref=total.at[step],
                dst_ref=landing.at[step],
                send_sem=send.at[step],
                recv_sem=recv.at[step],
                device_id=peer,
                device_id_type=MESH,
            )
            for step, peer in enumerate(peer_list)
        ]

    def start(self, step):
        self.copies[step].start()

    def finish(self, step):
        self.copies[step].wait_recv()
        self.total[step + 1] = self.total[step] + self.landing[step]

    def drain(self):
        for copy in self.copies:
            copy.wait_send()


DIMS = {"NN": ((1,), (0,)), "NT": ((1,), (1,)), "TN": ((0,), (0,))}
SCALING = 1.0 / math.sqrt(HEAD_DIM)


def dot(left, right, form="NN"):
    return lax.dot_general(left, right, (DIMS[form], ((), ())), preferred_element_type=F32)


def column_sum(values):
    return jnp.sum(values, axis=0, keepdims=True)


def row_mean(values):
    return jnp.mean(values, axis=-1, keepdims=True)


def chunks(count, size, body):
    def run(step, carry):
        body(rows(step * size, size))
        return carry

    lax.fori_loop(0, count // size, run, 0)


def block_body(
    outer,
    x_hbm, cot_hbm, seg_ref, pad_ref, w_query, w_key, w_value, w_out, own_b, own_c,
    b_query, b_value, b_inner, b_out, gain_one, shift_one, b_outer, gain_two, shift_two,
    out_hbm, grad_in_hbm, summed_hbm, small_hbm,
    weights, x_ref, cot, masks, vecs, qkv, ctx, probs, norm_one, scale_one, hidden_low, act, shared,
    acc, d_norm, d_low, d_ctx,
    grads, from_core, from_one, from_two, zone, from_z, from_early, outer_in, totals, landing,
    gz_send, gz_recv, g_send, g_recv, v_send, v_recv, local_sem, early_sem,
    csend, crecv, fsend, frecv, zsend, zrecv, esend, erecv, asend, arecv, osend, orecv, ssend, srecv, credit,
):
    dp, z, core, ax, ay, peers = places()
    others = outer_peers(dp, z, outer)
    everyone = [peers[name] for name in ("c", "x", "y", 1, 2)] + others
    tokens, width = x_ref.shape
    side = own_b.shape[0]
    half = side // 2
    eighth = half // 8
    cols = side // 4
    heads = cols // HEAD_DIM
    row_count = tokens // SEQ
    slope = [shared.at[u * tokens : (u + 1) * tokens] for u in range(4)]
    summed_out = [shared.at[k * side : (k + 1) * side] for k in range(3)]
    middle, shard_of, landing_place = line_order(z)
    line = {u: {"dp": dp, "tensor": shard_of[u]} for u in (1, 2, 3)}

    local_copies = [
        pltpu.make_async_copy(x_hbm, x_ref, local_sem.at[0]),
        pltpu.make_async_copy(w_out, weights.at[0, 0, 3 * cols :], local_sem.at[1]),
        pltpu.make_async_copy(own_b, weights.at[1, 0], local_sem.at[2]),
        pltpu.make_async_copy(own_c, weights.at[2, 0], local_sem.at[3]),
        pltpu.make_async_copy(cot_hbm, cot, local_sem.at[4]),
    ] + [
        pltpu.make_async_copy(ref, weights.at[0, 0, part * cols : (part + 1) * cols], local_sem.at[5 + part])
        for part, ref in enumerate((w_query, w_key, w_value))
    ]
    for number in (5, 6, 7, 1, 0, 2, 3, 4):
        local_copies[number].start()
    barrier = pltpu.get_barrier_semaphore()
    greeted = [peers[name] for name in ("c", "x", "y", 1, 2, 3)] + others
    for peer in greeted:
        pl.semaphore_signal(barrier, inc=1, device_id=peer, device_id_type=MESH)

    spreads, arrivals, vec_copies = {}, {}, {}
    gathered = [(k, u) for k in range(3) for u in (1, 2, 3)]

    def hop(k, source, target, peer):
        found = []
        for piece, span in enumerate(spreads[k, target].own):
            src = weights.at[k, source, span]
            if source == 0 and k:
                src = (None, own_b, own_c)[k].at[span]
            found.append(
                pltpu.make_async_remote_copy(
                    src_ref=src,
                    dst_ref=weights.at[k, target, span],
                    send_sem=gz_send.at[k, target - 1, 0 if peer is peers[1] else 1, piece],
                    recv_sem=gz_recv.at[k, target - 1, piece],
                    device_id=peer,
                    device_id_type=MESH,
                )
            )
        return found

    for k, u in gathered:
        spreads[k, u] = Spread(weights.at[k, u], half, g_send.at[k, u - 1], g_recv.at[k, u - 1], (k, u) in WIDE)
    near = {k: hop(k, 0, 1, peers[1]) for k in range(3)}
    across = {(k, 2): hop(k, 0, 2, peers[3]) for k in range(3)}
    across.update({(k, 3): hop(k, 1, 3, peers[3]) for k in range(3)})
    onward = {(k, u): hop(k, u, u, peers[1]) for k in range(3) for u in (2, 3)}
    for u in (1, 2, 3):
        vec_copies[u] = pltpu.make_async_remote_copy(
            src_ref=vecs.at[0],
            dst_ref=vecs.at[landing_place[u]],
            send_sem=v_send.at[u - 1],
            recv_sem=v_recv.at[landing_place[u] - 1],
            device_id=line[u],
            device_id_type=MESH,
        )

    def begin(copies):
        for copy in copies:
            copy.start()

    def send_own(k):
        begin(near[k])
        pl.when(middle == 1)(lambda: begin(across[k, 2]))

    landed = {}
    for k in range(3):
        landed.update({(k, 1): near[k], (k, 2): across[k, 2], (k, 3): across[k, 3]})

    def arrive(item):
        for copy in landed[item]:
            copy.wait_recv()

    def ahead(turn):
        k, u = gathered[turn]

        def forward():
            arrive((k, u))
            begin(across[k, 3] if u == 1 else onward[k, u])

        pl.when(middle == 1)(forward)
        if u == 2 and k < 2:
            send_own(k + 1)

    def gather_turn(turn):
        total = len(gathered)
        if turn == 0:
            ahead(0)
        if turn < total:
            item = gathered[turn]
            pl.when(middle == 0)(lambda: arrive(item))
            spreads[item].start(1 if item in WIDE else 0)
        for lag in (1, 2, 3):
            if 0 <= turn - lag < total:
                item = gathered[turn - lag]
                step = lag - 1 + (item in WIDE)
                if step < 3:
                    spreads[item].finish(step)
                if step < 2:
                    spreads[item].start(step + 1)
            if lag < 3:
                for later in {(0, 1): (1,), (1, 1): (2,), (1, 2): (3,), (2, 2): (4,), (3, 1): (5,), (3, 2): (6,), (4, 2): (7,), (5, 2): (8,)}.get(
                    (turn, lag), ()
                ):
                    ahead(later)

    def vector(row, slot=0):
        return vecs[slot, row : row + 1, :]

    def build_masks():
        for r in range(row_count):
            place = pl.ds(z * row_count + r, 1)
            seg = jnp.broadcast_to(seg_ref[place, :].astype(F32), (SEQ, SEQ))
            pad = jnp.broadcast_to(pad_ref[place, :], (SEQ, SEQ))
            allowed = (seg == seg.T) & (pad == 1)
            masks[r] = jnp.where(allowed, 0.0, MASKED)

    def project(j):
        bias = vector(0, j)[:, : 3 * cols]

        def body(span):
            qkv[j, span] = (dot(x_ref[span], weights[0, j, : 3 * cols], "NT") + bias).astype(BF)

        chunks(tokens, 256, body)

    def head(joined, part, h):
        return joined[:, part * cols + h * HEAD_DIM : part * cols + (h + 1) * HEAD_DIM]

    units = [(r, h) for r in range(row_count) for h in range(heads)]

    def spans(r):
        return slice(r * SEQ, (r + 1) * SEQ)

    def attend(j):
        joined = [qkv[j, spans(r)] for r in range(row_count)]
        scores = [
            dot(head(joined[r], 0, h), head(joined[r], 1, h), "NT") * SCALING + masks[r] for r, h in units
        ]
        found = []
        for (r, h), score in zip(units, scores):
            weight = jnp.exp(score - jnp.max(score, axis=-1, keepdims=True))
            found.append((weight * (1.0 / jnp.sum(weight, axis=-1, keepdims=True))).astype(BF))
        mixed = []
        for (r, h), prob in zip(units, found):
            probs[j, r, h] = prob
            mixed.append(dot(prob, head(joined[r], 2, h)).astype(BF))
        for r in range(row_count):
            ctx[j, spans(r)] = jnp.concatenate(mixed[r * heads : (r + 1) * heads], axis=1)

    def project_out():
        total = dot(ctx[0], weights[0, 0, 3 * cols :])
        for j in (1, 2, 3):
            total = total + dot(ctx[j], weights[0, j, 3 * cols :])
        acc[...] = total

    def norm_first():
        b_out, gain, shift = vector(2), vector(3), vector(4)

        def body(span):
            value = acc[span] + b_out + x_ref[span].astype(F32)
            center = value - row_mean(value)
            scale = lax.rsqrt(row_mean(center * center) + EPSILON)
            normal = center * scale
            norm_one[span] = normal
            scale_one[span] = scale
            hidden_low[span] = (normal * gain + shift).astype(BF)

        chunks(tokens, 128, body)

    def feed_in(j):
        bias = vector(1, j)

        def body(span):
            pre = dot(hidden_low[span], weights[1, j]) + bias
            cumulative = 0.5 + 0.5 * lax.erf(pre * (1.0 / math.sqrt(2.0)))
            density = jnp.exp(pre * pre * -0.5) * (1.0 / math.sqrt(2.0 * math.pi))
            act[j, span] = (pre * cumulative).astype(BF)
            slope[j][span] = (cumulative + pre * density).astype(BF)

        chunks(tokens, 128, body)

    def feed_out(j):
        part = dot(act[j], weights[2, j])
        acc[...] = part if j == 0 else acc[...] + part

    def small_add(row, value):
        totals[0, pl.ds(row, 1), : value.shape[1]] += value

    def norm_second():
        gain_a, shift_a, b_outer = vector(3), vector(4), vector(5)
        gain, shift = vector(6), vector(7)

        def body(span):
            value = acc[span] + b_outer + (norm_one[span] * gain_a + shift_a)
            center = value - row_mean(value)
            scale = lax.rsqrt(row_mean(center * center) + EPSILON)
            normal = center * scale
            given = cot[span].astype(F32)
            cot[span] = (normal * gain + shift).astype(BF)
            pulled = given * gain
            grad = scale * (pulled - row_mean(pulled) - normal * row_mean(pulled * normal))
            d_norm[span] = grad
            d_low[span] = grad.astype(BF)
            small_add(3, column_sum(grad))
            small_add(4, column_sum(given * normal))
            small_add(5, column_sum(given))

        chunks(tokens, 128, body)

    def feed_out_back(j):
        def body(span):
            grad = (dot(d_low[span], weights[2, j], "NT") * slope[j][span].astype(F32)).astype(BF)
            act[j, span] = grad
            small_add(12 + shard_of[j], column_sum(grad.astype(F32)))

        chunks(tokens, 256, body)

    def feed_in_back(j, first):
        def body(span):
            part = dot(act[j, span], weights[1, j], "NT")
            acc[span] = part if first else acc[span] + part

        chunks(tokens, 256, body)

    def norm_first_back():
        gain = vector(3)

        def body(span):
            given = acc[span] + d_norm[span]
            normal = norm_one[span]
            pulled = given * gain
            grad = scale_one[span] * (pulled - row_mean(pulled) - normal * row_mean(pulled * normal))
            d_norm[span] = grad
            d_low[span] = grad.astype(BF)
            small_add(0, column_sum(grad))
            small_add(1, column_sum(given * normal))
            small_add(2, column_sum(given))

        chunks(tokens, 128, body)

    def attend_back(j):
        d_ctx[...] = dot(d_low[...], weights[0, j, 3 * cols :], "NT").astype(BF)
        joined = [qkv[j, spans(r)] for r in range(row_count)]
        given = [d_ctx[spans(r)] for r in range(row_count)]
        d_outs = [given[r][:, h * HEAD_DIM : (h + 1) * HEAD_DIM] for r, h in units]
        d_probs = [dot(d_out, head(joined[r], 2, h), "NT") for (r, h), d_out in zip(units, d_outs)]
        prob_list = [probs[j, r, h] for r, h in units]
        d_scores = []
        for d_prob, prob in zip(d_probs, prob_list):
            wide = prob.astype(F32)
            inner = jnp.sum(d_prob * wide, axis=-1, keepdims=True)
            d_scores.append((wide * (d_prob - inner)).astype(BF))
        d_values = [dot(prob, d_out, "TN").astype(BF) for prob, d_out in zip(prob_list, d_outs)]
        d_queries = [(dot(ds, head(joined[r], 1, h)) * SCALING).astype(BF) for (r, h), ds in zip(units, d_scores)]
        d_keys = [(dot(ds, head(joined[r], 0, h), "TN") * SCALING).astype(BF) for (r, h), ds in zip(units, d_scores)]
        total = jnp.zeros((1, 3 * cols), F32)
        for r in range(row_count):
            mine_heads = slice(r * heads, (r + 1) * heads)
            joined_grad = jnp.concatenate(d_queries[mine_heads] + d_keys[mine_heads] + d_values[mine_heads], axis=1)
            qkv[j, spans(r)] = joined_grad
            total = total + column_sum(joined_grad.astype(F32))
        small_add(8 + shard_of[j], total)

    def input_back(j):
        def body(span):
            d_norm[span] = d_norm[span] + dot(qkv[j, span], weights[0, j, : 3 * cols])

        chunks(tokens, 256, body)

    mine, theirs = rows(core * half, half), rows((1 - core) * half, half)
    mine_cols = pl.ds(pl.multiple_of(core * half, 128), half)
    their_cols = pl.ds(pl.multiple_of((1 - core) * half, 128), half)
    order = [(k, j) for k in range(3) for j in (1, 2, 3, 0)]
    swaps = {
        (k, j): pltpu.make_async_remote_copy(
            src_ref=grads.at[k % 2, j, theirs],
            dst_ref=from_core.at[k % 2, j],
            send_sem=csend.at[k, j],
            recv_sem=crecv.at[k, j],
            device_id=peers["c"],
            device_id_type=MESH,
        )
        for k, j in order
    }
    folds = {
        (k, j): Fold(
            grads.at[k % 2, j, mine], from_core.at[k % 2, j], from_one.at[k, j], from_two.at[k, j],
            fsend.at[k, j], frecv.at[k, j],
        )
        for k, j in order
    }
    over = {
        (k, j): pltpu.make_async_remote_copy(
            src_ref=zone.at[k, j],
            dst_ref=from_z.at[k, landing_place[j] - 1],
            send_sem=zsend.at[k, j - 1],
            recv_sem=zrecv.at[k, landing_place[j] - 1],
            device_id=line[j],
            device_id_type=MESH,
        )
        for k, j in order
        if j and j not in EARLY[k]
    }
    early_slots = [(k, j) for k, j in order if j in EARLY[k]]
    early_base = {k: early_slots.index((k, 1)) for k in range(3)}

    def early_pair(k, place, item):
        found = []
        for p in (0, 1):
            found.append(
                pltpu.make_async_remote_copy(
                    src_ref=grads.at[k % 2, item[1], mine].at[folds[item].keep_one[p]],
                    dst_ref=from_early.at[early_base[k] + place, p],
                    send_sem=esend.at[early_slots.index(item), p],
                    recv_sem=erecv.at[early_base[k] + place, p],
                    device_id=line[item[1]],
                    device_id_type=MESH,
                )
            )
        return found

    early = {(k, j): early_pair(k, landing_place[j] - 1, (k, j)) for k, j in early_slots}

    def merge(k, first):
        parts = [first] if first is not None else []
        for place in range(len(EARLY[k])):
            for copy in early_pair(k, place, (k, 1)):
                copy.wait_recv()
            parts.append(from_early.at[early_base[k] + place])
        folds[k, 0].combine(parts, True)

    sums = [Spread(summed_out[k], half, asend.at[k], arecv.at[k]) for k in range(3)]
    tiny = Everyone(totals, landing, ssend, srecv, everyone)

    def settle(k):
        for place in range(len(EARLY[k]), 3):
            pltpu.make_async_remote_copy(
                src_ref=zone.at[k, 1],
                dst_ref=from_z.at[k, place],
                send_sem=zsend.at[k, place],
                recv_sem=zrecv.at[k, place],
                device_id=peers[1],
                device_id_type=MESH,
            ).wait_recv()
        summed = zone[k, 0].astype(F32)
        for place in range(len(EARLY[k]), 3):
            summed = summed + from_z[k, place].astype(F32)
        for step, peer in enumerate(others):
            outer_in[k, step, 0] = summed.astype(BF)
            copy = pltpu.make_async_remote_copy(
                src_ref=outer_in.at[k, step, 0],
                dst_ref=outer_in.at[k, step, 1],
                send_sem=osend.at[k, step],
                recv_sem=orecv.at[k, step],
                device_id=peer,
                device_id_type=MESH,
            )
            copy.start()
            copy.wait()
            summed = outer_in[k, step, 0].astype(F32) + outer_in[k, step, 1].astype(F32)
        for p in (0, 1):
            summed_out[k][sums[k].own[p]] = summed[p * eighth : (p + 1) * eighth].astype(BF)
        sums[k].start(0)

    def drain(item):
        swaps[item].wait_send()
        folds[item].drain(item not in early)
        for copy in early.get(item, ()):
            copy.wait_send()

    def grad_block(k, j):
        if k == 0:
            for span, picked in ((theirs, their_cols), (mine, mine_cols)):
                grads[0, j, span] = dot(act[j, :, picked], d_low[...], "TN").astype(BF)
                if span is theirs and j:
                    swaps[k, j].start()
            if j == 0:
                feed_out_back(j)
                swaps[k, j].start()
        elif k == 1:
            for span, picked in ((theirs, their_cols), (mine, mine_cols)):
                grads[1, j, span] = dot(hidden_low[:, picked], act[j], "TN").astype(BF)
                if span is theirs:
                    swaps[k, j].start()
        else:
            drain((0, j))
            pl.semaphore_wait(credit.at[j], 1)
            grads[0, j, : 3 * cols] = dot(qkv[j], x_ref[...], "TN").astype(BF)
            grads[0, j, 3 * cols :] = dot(ctx[j], d_low[...], "TN").astype(BF)
            swaps[k, j].start()

    def reduce_turn(turn):
        total = len(order)
        if turn < total:
            item = order[turn]
            swaps[item].wait_recv()
            folds[item].step_core(grads.at[item[0] % 2, item[1], mine])
            if item[0] == 0:
                pl.semaphore_signal(credit.at[item[1]], inc=1, device_id=peers["c"], device_id_type=MESH)
        if 0 <= turn - 1 < total:
            item = k, j = order[turn - 1]
            folds[item].step_one()
            if j == 0 and MERGE_TURN[k] == turn:
                merge(k, from_one.at[item])
            else:
                folds[item].combine([from_one.at[item]], j and item not in early)
                for copy in early.get(item, ()):
                    copy.start()
        for k in range(3):
            if MERGE_TURN[k] == turn and order[turn - 1] != (k, 0):
                merge(k, None)
        if 0 <= turn - 2 < total:
            item = order[turn - 2]
            if item[1] and item not in early:
                folds[item].step_two(zone.at[item[0], item[1]])
                over[item].start()
        for k in range(3):
            if turn == MERGE_TURN[k] + 1:
                folds[k, 0].step_two(zone.at[k, 0])
            if turn == MERGE_TURN[k] + 2:
                settle(k)
            step = turn - MERGE_TURN[k] - 3
            if 0 <= step < 3:
                sums[k].finish(step)
                if step < 2:
                    sums[k].start(step + 1)
                elif k < 2:
                    copy = pltpu.make_async_copy(summed_out[k], summed_hbm.at[k], early_sem.at[k])
                    copy.start()
                    early_copies.append(copy)

    early_copies = []

    vecs[0] = jnp.zeros_like(vecs[0])
    for row, start, ref in (
        (0, 0, b_query), (0, 2 * cols, b_value), (1, 0, b_inner), (2, 0, b_out), (3, 0, gain_one),
        (4, 0, shift_one), (5, 0, b_outer), (6, 0, gain_two), (7, 0, shift_two),
    ):
        size = ref.shape[0]
        vecs[0, row : row + 1, start : start + size] = ref[...].astype(F32).reshape(1, size)
    for number in (1, 5, 6, 7):
        local_copies[number].wait()
    pl.semaphore_wait(barrier, len(greeted))
    send_own(0)
    for u in (1, 2, 3):
        vec_copies[u].start()
    build_masks()
    totals[0] = jnp.zeros_like(totals[0])
    local_copies[0].wait()
    project(0)
    gather_turn(0)
    attend(0)
    gather_turn(1)
    gather_turn(2)
    for j in (1, 2, 3):
        gather_turn(2 + j)
        if j == 1:
            for place in range(3):
                pltpu.make_async_remote_copy(
                    src_ref=vecs.at[0],
                    dst_ref=vecs.at[place + 1],
                    send_sem=v_send.at[place],
                    recv_sem=v_recv.at[place],
                    device_id=peers[1],
                    device_id_type=MESH,
                ).wait_recv()
        project(j)
        attend(j)
    gather_turn(6)
    project_out()
    norm_first()
    gather_turn(7)
    local_copies[2].wait()
    feed_in(0)
    feed_in(1)
    gather_turn(8)
    feed_in(2)
    feed_in(3)
    gather_turn(9)
    local_copies[3].wait()
    feed_out(0)
    feed_out(1)
    for j in (2, 3):
        spreads[2, j].finish(2)
        feed_out(j)
    local_copies[4].wait()
    norm_second()
    out_copy = pltpu.make_async_copy(cot, out_hbm, local_sem.at[0])
    out_copy.start()

    grad_block(0, 1)
    grad_block(0, 2)
    reduce_turn(0)
    grad_block(0, 3)
    feed_out_back(1)
    feed_out_back(2)
    reduce_turn(1)
    feed_out_back(3)
    grad_block(0, 0)
    feed_in_back(1, True)
    reduce_turn(2)
    for j in (2, 3, 0):
        feed_in_back(j, False)
    norm_first_back()
    grad_block(1, 1)
    reduce_turn(3)
    for place, j in enumerate((2, 3, 0)):
        grad_block(1, j)
        attend_back((1, 2, 3)[place])
        reduce_turn(4 + place)
    attend_back(0)
    for place, j in enumerate((1, 2, 3, 0)):
        grad_block(2, j)
        if place:
            input_back(order[7 + place][1])
        reduce_turn(7 + place)
    input_back(0)
    reduce_turn(11)
    grad_in_copy = pltpu.make_async_copy(d_norm, grad_in_hbm, local_sem.at[1])
    grad_in_copy.start()
    tiny.start(0)
    for extra in range(6):
        if extra < len(everyone):
            tiny.finish(extra)
            if extra + 1 < len(everyone):
                tiny.start(extra + 1)
        reduce_turn(len(order) + extra)
    for extra in range(6, len(everyone)):
        tiny.finish(extra)
        if extra + 1 < len(everyone):
            tiny.start(extra + 1)
    small_copy = pltpu.make_async_copy(totals.at[len(everyone)], small_hbm, local_sem.at[2])
    small_copy.start()
    last_copy = pltpu.make_async_copy(summed_out[2], summed_hbm.at[2], local_sem.at[3])
    last_copy.start()

    def settled(copies):
        for copy in copies:
            copy.wait_send()

    for k in range(3):
        settled(near[k])
        for u in (2, 3):
            pl.when(middle == 1)(lambda k=k, u=u: settled(across[k, u] + onward[k, u]))
    for item in gathered:
        spreads[item].drain()
    for j in (1, 2, 3):
        vec_copies[j].wait_send()
    for item in order:
        if item[0]:
            drain(item)
        if item in over:
            over[item].wait_send()
    for spread in sums:
        spread.drain()
    tiny.drain()
    for copy in [out_copy, grad_in_copy, small_copy, last_copy] + early_copies:
        copy.wait()


def block(outer, x, cot, seg, pad, *others):
    tokens, width = x.shape
    side = others[4].shape[0]
    half, cols = side // 2, side // 4
    heads = cols // HEAD_DIM
    row_count = tokens // SEQ
    steps = 5 + int(math.log2(outer))
    more = max(steps - 5, 1)
    outer_rows = half // 4 if outer > 1 else 16
    early = sum(len(slots) for slots in EARLY)
    dma = pltpu.SemaphoreType.DMA
    vmem = pltpu.VMEM
    any_space = pl.BlockSpec(memory_space=pl.ANY)
    in_vmem = pl.BlockSpec(memory_space=pltpu.VMEM)
    return pl.pallas_call(
        functools.partial(block_body, outer),
        out_shape=(
            jax.ShapeDtypeStruct((tokens, width), BF),
            jax.ShapeDtypeStruct((tokens, width), F32),
            jax.ShapeDtypeStruct((3, side, width), BF),
            jax.ShapeDtypeStruct((16, width), F32),
        ),
        in_specs=[any_space] * 2 + [in_vmem] * 2 + [any_space] * 6 + [in_vmem] * 9,
        out_specs=(any_space,) * 4,
        scratch_shapes=[
            vmem((3, 4, side, width), BF),
            vmem((tokens, width), BF),
            vmem((tokens, width), BF),
            vmem((row_count, SEQ, SEQ), F32),
            vmem((4, 8, width), F32),
            vmem((4, tokens, 3 * cols), BF),
            vmem((4, tokens, cols), BF),
            vmem((4, row_count, heads, SEQ, SEQ), BF),
            vmem((tokens, width), F32),
            vmem((tokens, 1), F32),
            vmem((tokens, width), BF),
            vmem((4, tokens, side), BF),
            vmem((max(3 * side, 4 * tokens), side), BF),
            vmem((tokens, width), F32),
            vmem((tokens, width), F32),
            vmem((tokens, width), BF),
            vmem((tokens, cols), BF),
            vmem((2, 4, side, width), BF),
            vmem((2, 4, half, width), BF),
            vmem((3, 4, 2, half // 4, width), BF),
            vmem((3, 4, 2, half // 8, width), BF),
            vmem((3, 4, half // 4, width), BF),
            vmem((3, 3, half // 4, width), BF),
            vmem((early, 2, half // 4, width), BF),
            vmem((3, more, 2, outer_rows, width), BF),
            vmem((steps + 1, 16, width), F32),
            vmem((steps, 16, width), F32),
            dma((3, 3, 2, 2)), dma((3, 3, 2)), dma((3, 3, 5)), dma((3, 3, 5)), dma((3,)), dma((3,)), dma((8,)), dma((2,)),
            dma((3, 4)), dma((3, 4)), dma((3, 4, 4)), dma((3, 4, 4)), dma((3, 3)), dma((3, 3)), dma((early, 2)), dma((early, 2)),
            dma((3, 5)), dma((3, 5)), dma((3, more)), dma((3, more)), dma((steps,)), dma((steps,)),
            pltpu.SemaphoreType.REGULAR((4,)),
        ],
        compiler_params=pltpu.CompilerParams(
            collective_id=0, has_side_effects=True, vmem_limit_bytes=67043328
        ),
        name="block",
    )(x, cot, seg, pad, *others)


def local(
    outer, block_input, cotangent, segment_ids, pad_mask,
    w_query, b_query, w_key, w_value, b_value, w_out, b_out, gain_one, shift_one,
    w_inner, b_inner, w_outer, b_outer, gain_two, shift_two,
):
    tokens, width = block_input.shape
    cols = w_query.shape[1]
    output, grad_input, summed, small = block(
        outer, block_input, cotangent, segment_ids.reshape(-1, SEQ), pad_mask.reshape(-1, SEQ),
        w_query.T, w_key.T, w_value.T, w_out, w_inner, w_outer,
        b_query, b_value, b_inner, b_out, gain_one, shift_one, b_outer, gain_two, shift_two,
    )
    outs = list(finish(output, grad_input, summed, small, cols))
    for place in (2, 4, 5):
        outs[place] = outs[place].T
    return tuple(outs)


def finish_body(
    out_hbm, grad_in_hbm, summed_hbm, small_ref,
    output, grad_input, g_query, gb_query, g_key, g_value, gb_value, g_out, gb_out, gg_one, gs_one,
    g_inner, gb_inner, g_outer, gb_outer, gg_two, gs_two,
    out_held, in_held, summed, wide, turned, flat, in_sem, out_sem,
):
    z = lax.axis_index("tensor")
    cols = gb_query.shape[0]
    reads = [pltpu.make_async_copy(summed_hbm.at[k], summed.at[k], in_sem.at[k]) for k in (0, 1, 2)]
    reads.append(pltpu.make_async_copy(grad_in_hbm, in_held, in_sem.at[3]))
    reads.append(pltpu.make_async_copy(out_hbm, out_held, in_sem.at[4]))
    for copy in reads:
        copy.start()
    for row, ref in ((0, gb_out), (1, gg_one), (2, gs_one), (3, gb_outer), (4, gg_two), (5, gs_two)):
        ref[...] = small_ref[row : row + 1, :].reshape(ref.shape)
    own = small_ref[pl.ds(8 + z, 1), :]
    gb_query[...] = own[:, :cols].reshape(gb_query.shape)
    gb_value[...] = own[:, 2 * cols : 3 * cols].reshape(gb_value.shape)
    gb_inner[...] = small_ref[pl.ds(12 + z, 1), :].reshape(gb_inner.shape)
    writes = []

    def write(source, target):
        copy = pltpu.make_async_copy(source, target, out_sem.at[len(writes)])
        copy.start()
        writes.append(copy)

    for k, target in ((0, g_outer), (1, g_inner)):
        reads[k].wait()
        wide[k] = summed[k].astype(F32)
        write(wide.at[k], target)
    reads[2].wait()
    for part, target in enumerate((g_query, g_key, g_value)):
        turned[part] = summed[2, part * cols : (part + 1) * cols].astype(F32)
        write(turned.at[part], target)
    flat[...] = summed[2, 3 * cols :].astype(F32)
    write(flat, g_out)
    reads[3].wait()
    write(in_held, grad_input)
    reads[4].wait()
    write(out_held, output)
    for copy in writes:
        copy.wait()


def finish(output, grad_input, summed, small, cols):
    (tokens, width), side = output.shape, summed.shape[1]
    shape = jax.ShapeDtypeStruct
    any_space = pl.BlockSpec(memory_space=pl.ANY)
    in_vmem = pl.BlockSpec(memory_space=pltpu.VMEM)
    line, short, flat, big = shape((width,), F32), shape((cols,), F32), shape((cols, width), F32), shape((side, width), F32)
    outs = (
        (shape((tokens, width), BF), 0), (shape((tokens, width), F32), 0), (flat, 0), (short, 1), (flat, 0), (flat, 0),
        (short, 1), (flat, 0), (line, 1), (line, 1), (line, 1), (big, 0), (line, 1), (big, 0),
        (line, 1), (line, 1), (line, 1),
    )
    dma = pltpu.SemaphoreType.DMA
    return pl.pallas_call(
        finish_body,
        out_shape=tuple(item for item, _ in outs),
        in_specs=[any_space, any_space, any_space, in_vmem],
        out_specs=tuple(in_vmem if held else any_space for _, held in outs),
        scratch_shapes=[
            pltpu.VMEM((tokens, width), BF),
            pltpu.VMEM((tokens, width), F32),
            pltpu.VMEM((3, side, width), BF),
            pltpu.VMEM((2, side, width), F32),
            pltpu.VMEM((3, cols, width), F32),
            pltpu.VMEM((cols, width), F32),
            dma((5,)), dma((8,)),
        ],
        compiler_params=pltpu.CompilerParams(vmem_limit_bytes=67043328),
        name="finish",
    )(output, grad_input, summed, small)


def solution(mesh):
    outer = mesh.shape["dp"] // GROUP
    row, col, both, rep = P("tensor", None), P(None, "tensor"), P(("dp", "tensor"), None), P()
    part = P("tensor")
    return jax.shard_map(
        functools.partial(local, outer),
        mesh=mesh,
        in_specs=(
            both, both, P("dp"), P("dp"), col, part, col, col, part, row, rep, rep, rep,
            col, part, row, rep, rep, rep,
        ),
        out_specs=(
            both, both, col, part, col, col, part, row, rep, rep, rep, col, part, row, rep, rep, rep,
        ),
        check_vma=False,
    )
```

```python
import functools
import math

import jax
import jax.numpy as jnp
from jax import lax
from jax.experimental import pallas as pl
from jax.experimental.pallas import tpu as pltpu
from jax.sharding import PartitionSpec as P

HEAD_DIM = 64
SEQ = 128
EPSILON = 1e-05
MASKED = -1e30
BF = jnp.bfloat16
F32 = jnp.float32
MESH = pl.DeviceIdType.MESH
GROUP = 8
WIDE = ((2, 1), (2, 3))
EARLY = ((1, 2, 3), (1,), (1,))
MERGE_TURN = (8, 8, 12)
SETTLE_TURN = (12, 13, 14)


def places():
    dp = lax.axis_index("dp")
    z = lax.axis_index("tensor")
    core = dp % 2
    along_x = (dp // 2) % 2
    along_y = (dp // 4) % 2
    peers = {
        "c": {"dp": dp + 1 - 2 * core, "tensor": z},
        "x": {"dp": dp + 2 - 4 * along_x, "tensor": z},
        "y": {"dp": dp + 4 - 8 * along_y, "tensor": z},
        1: {"dp": dp, "tensor": z + 1 - 2 * (z % 2)},
        2: {"dp": dp, "tensor": (z + 2) % 4},
        3: {"dp": dp, "tensor": 3 - z},
    }
    return dp, z, core, along_x, along_y, peers


def line_order(z):
    low, high = z % 2, z // 2
    middle = low + high - 2 * low * high
    shards = (z, z + 1 - 2 * low, (1 - middle) * ((z + 2) % 4) + middle * (3 - z), middle * ((z + 2) % 4) + (1 - middle) * (3 - z))
    return middle, shards, (0, 1, 3 - middle, 3 - middle)


def outer_peers(dp, z, outer):
    found = []
    weight = GROUP
    while weight < GROUP * outer:
        bit = (dp // weight) % 2
        found.append({"dp": dp + weight - 2 * weight * bit, "tensor": z})
        weight *= 2
    return found


def rows(start, size):
    return pl.ds(pl.multiple_of(start, 16), size)


class Spread:
    def __init__(self, block, half, send, recv, wide=False):
        _, _, core, ax, ay, peers = places()
        base = core * half
        part = half // 2
        quarter = part // 2
        eighth = quarter // 2
        first = base + ax * quarter
        second = base + part + ay * quarter
        self.steps = []
        plan = (
            ((rows(first + ay * eighth, eighth), "y"), (rows(second + ax * eighth, eighth), "x")),
            ((rows(first, quarter), "x"), (rows(second, quarter), "y")),
            ((rows(base, half), "c"),),
        )
        place = 0
        for number, step in enumerate(plan):
            copies = []
            for span, name in () if wide and number == 0 else step:
                copies.append(
                    pltpu.make_async_remote_copy(
                        src_ref=block.at[span],
                        dst_ref=block.at[span],
                        send_sem=send.at[place],
                        recv_sem=recv.at[place],
                        device_id=peers[name],
                        device_id_type=MESH,
                    )
                )
                place += 1
            self.steps.append(copies)
        self.own = (rows(first + ay * eighth, eighth), rows(second + ax * eighth, eighth))
        if wide:
            self.own = (rows(first, quarter), rows(second, quarter))

    def start(self, step):
        for copy in self.steps[step]:
            copy.start()

    def finish(self, step):
        for copy in self.steps[step]:
            copy.wait_recv()

    def drain(self):
        for step in self.steps:
            for copy in step:
                copy.wait_send()


def plus(left, right):
    return (left.astype(F32) + right.astype(F32)).astype(BF)


class Fold:
    def __init__(self, held, from_core, from_one, from_two, send, recv):
        _, _, core, ax, ay, peers = places()
        half = held.shape[0]
        part, quarter, eighth = half // 2, half // 4, half // 8
        self.held = held
        self.from_core = from_core
        self.from_one = from_one
        self.from_two = from_two
        self.quarter, self.eighth = quarter, eighth
        self.give_one = (rows((1 - ax) * quarter, quarter), rows(part + (1 - ay) * quarter, quarter))
        self.keep_one = (rows(ax * quarter, quarter), rows(part + ay * quarter, quarter))
        self.give_two = (
            rows(ax * quarter + (1 - ay) * eighth, eighth),
            rows(part + ay * quarter + (1 - ax) * eighth, eighth),
        )
        self.keep_two = (
            rows(ax * quarter + ay * eighth, eighth),
            rows(part + ay * quarter + ax * eighth, eighth),
        )
        self.inside = (rows((1 - ay) * eighth, eighth), rows((1 - ax) * eighth, eighth))
        self.inside_keep = (rows(ay * eighth, eighth), rows(ax * eighth, eighth))
        self.one = [
            pltpu.make_async_remote_copy(
                src_ref=held.at[self.give_one[p]],
                dst_ref=from_one.at[p],
                send_sem=send.at[p],
                recv_sem=recv.at[p],
                device_id=peers["xy"[p]],
                device_id_type=MESH,
            )
            for p in (0, 1)
        ]
        self.two = [
            pltpu.make_async_remote_copy(
                src_ref=held.at[self.give_two[p]],
                dst_ref=from_two.at[p],
                send_sem=send.at[2 + p],
                recv_sem=recv.at[2 + p],
                device_id=peers["yx"[p]],
                device_id_type=MESH,
            )
            for p in (0, 1)
        ]

    def step_core(self, own):
        for spans in (self.give_one, self.keep_one):
            for p in (0, 1):
                span = spans[p]
                self.held[span] = plus(own[span], self.from_core[span])
            if spans is self.give_one:
                for copy in self.one:
                    copy.start()

    def step_one(self):
        for copy in self.one:
            copy.wait_recv()

    def combine(self, parts, send):
        for spans, insides in ((self.give_two, self.inside), (self.keep_two, self.inside_keep)):
            for p in (0, 1):
                total = self.held[spans[p]].astype(F32)
                for part in parts:
                    total = total + part[p, insides[p]].astype(F32)
                self.held[spans[p]] = total.astype(BF)
                if send and spans is self.give_two:
                    self.two[p].start()

    def step_two(self, result):
        for p in (0, 1):
            self.two[p].wait_recv()
            result[p * self.eighth : (p + 1) * self.eighth] = plus(self.held[self.keep_two[p]], self.from_two[p])

    def drain(self, halved):
        for copy in self.one + (self.two if halved else []):
            copy.wait_send()


class Everyone:
    def __init__(self, total, landing, send, recv, peer_list):
        self.total, self.landing = total, landing
        self.copies = [
            pltpu.make_async_remote_copy(
                src_ref=total.at[step],
                dst_ref=landing.at[step],
                send_sem=send.at[step],
                recv_sem=recv.at[step],
                device_id=peer,
                device_id_type=MESH,
            )
            for step, peer in enumerate(peer_list)
        ]

    def start(self, step):
        self.copies[step].start()

    def finish(self, step):
        self.copies[step].wait_recv()
        self.total[step + 1] = self.total[step] + self.landing[step]

    def drain(self):
        for copy in self.copies:
            copy.wait_send()


DIMS = {"NN": ((1,), (0,)), "NT": ((1,), (1,)), "TN": ((0,), (0,))}
SCALING = 1.0 / math.sqrt(HEAD_DIM)


def dot(left, right, form="NN"):
    return lax.dot_general(left, right, (DIMS[form], ((), ())), preferred_element_type=F32)


def column_sum(values):
    return jnp.sum(values, axis=0, keepdims=True)


def row_mean(values):
    return jnp.mean(values, axis=-1, keepdims=True)


def chunks(count, size, body):
    def run(step, carry):
        body(rows(step * size, size))
        return carry

    lax.fori_loop(0, count // size, run, 0)


def block_body(
    outer,
    x_hbm, cot_hbm, seg_ref, pad_ref, w_query, w_key, w_value, w_out, own_b, own_c,
    b_query, b_value, b_inner, b_out, gain_one, shift_one, b_outer, gain_two, shift_two,
    out_hbm, grad_in_hbm, summed_hbm, small_hbm,
    weights, x_ref, cot, masks, vecs, qkv, ctx, probs, norm_one, scale_one, hidden_low, act, shared,
    acc, d_norm, d_low, d_ctx,
    grads, from_core, from_one, from_two, zone, from_z, from_early, outer_in, totals, landing,
    gz_send, gz_recv, g_send, g_recv, v_send, v_recv, local_sem, early_sem,
    csend, crecv, fsend, frecv, zsend, zrecv, esend, erecv, asend, arecv, osend, orecv, ssend, srecv, credit,
):
    dp, z, core, ax, ay, peers = places()
    others = outer_peers(dp, z, outer)
    everyone = [peers[name] for name in ("c", "x", "y", 1, 2)] + others
    tokens, width = x_ref.shape
    side = own_b.shape[0]
    half = side // 2
    eighth = half // 8
    cols = side // 4
    heads = cols // HEAD_DIM
    row_count = tokens // SEQ
    slope = [shared.at[u * tokens : (u + 1) * tokens] for u in range(4)]
    summed_out = [shared.at[k * side : (k + 1) * side] for k in range(3)]
    middle, shard_of, landing_place = line_order(z)
    line = {u: {"dp": dp, "tensor": shard_of[u]} for u in (1, 2, 3)}

    local_copies = [
        pltpu.make_async_copy(x_hbm, x_ref, local_sem.at[0]),
        pltpu.make_async_copy(w_out, weights.at[0, 0, 3 * cols :], local_sem.at[1]),
        pltpu.make_async_copy(own_b, weights.at[1, 0], local_sem.at[2]),
        pltpu.make_async_copy(own_c, weights.at[2, 0], local_sem.at[3]),
        pltpu.make_async_copy(cot_hbm, cot, local_sem.at[4]),
    ] + [
        pltpu.make_async_copy(ref, weights.at[0, 0, part * cols : (part + 1) * cols], local_sem.at[5 + part])
        for part, ref in enumerate((w_query, w_key, w_value))
    ]
    for number in (5, 6, 7, 1, 0, 2, 3, 4):
        local_copies[number].start()
    barrier = pltpu.get_barrier_semaphore()
    greeted = [peers[name] for name in ("c", "x", "y", 1, 2, 3)] + others
    for peer in greeted:
        pl.semaphore_signal(barrier, inc=1, device_id=peer, device_id_type=MESH)

    spreads, arrivals, vec_copies = {}, {}, {}
    gathered = [(k, u) for k in range(3) for u in (1, 2, 3)]

    def hop(k, source, target, peer):
        found = []
        for piece, span in enumerate(spreads[k, target].own):
            src = weights.at[k, source, span]
            if source == 0 and k:
                src = (None, own_b, own_c)[k].at[span]
            found.append(
                pltpu.make_async_remote_copy(
                    src_ref=src,
                    dst_ref=weights.at[k, target, span],
                    send_sem=gz_send.at[k, target - 1, 0 if peer is peers[1] else 1, piece],
                    recv_sem=gz_recv.at[k, target - 1, piece],
                    device_id=peer,
                    device_id_type=MESH,
                )
            )
        return found

    for k, u in gathered:
        spreads[k, u] = Spread(weights.at[k, u], half, g_send.at[k, u - 1], g_recv.at[k, u - 1], (k, u) in WIDE)
    near = {k: hop(k, 0, 1, peers[1]) for k in range(3)}
    across = {(k, 2): hop(k, 0, 2, peers[3]) for k in range(3)}
    across.update({(k, 3): hop(k, 1, 3, peers[3]) for k in range(3)})
    onward = {(k, u): hop(k, u, u, peers[1]) for k in range(3) for u in (2, 3)}
    for u in (1, 2, 3):
        vec_copies[u] = pltpu.make_async_remote_copy(
            src_ref=vecs.at[0],
            dst_ref=vecs.at[landing_place[u]],
            send_sem=v_send.at[u - 1],
            recv_sem=v_recv.at[landing_place[u] - 1],
            device_id=line[u],
            device_id_type=MESH,
        )

    def begin(copies):
        for copy in copies:
            copy.start()

    def send_own(k):
        begin(near[k])
        pl.when(middle == 1)(lambda: begin(across[k, 2]))

    landed = {}
    for k in range(3):
        landed.update({(k, 1): near[k], (k, 2): across[k, 2], (k, 3): across[k, 3]})

    def arrive(item):
        for copy in landed[item]:
            copy.wait_recv()

    def ahead(turn):
        k, u = gathered[turn]

        def forward():
            arrive((k, u))
            begin(across[k, 3] if u == 1 else onward[k, u])

        pl.when(middle == 1)(forward)
        if u == 2 and k < 2:
            send_own(k + 1)

    def gather_turn(turn):
        total = len(gathered)
        if turn == 0:
            ahead(0)
        if turn < total:
            item = gathered[turn]
            pl.when(middle == 0)(lambda: arrive(item))
            spreads[item].start(1 if item in WIDE else 0)
        for lag in (1, 2, 3):
            if 0 <= turn - lag < total:
                item = gathered[turn - lag]
                step = lag - 1 + (item in WIDE)
                if step < 3:
                    spreads[item].finish(step)
                if step < 2:
                    spreads[item].start(step + 1)
            if lag < 3:
                for later in {(0, 1): (1,), (1, 1): (2,), (1, 2): (3,), (2, 2): (4,), (3, 1): (5,), (3, 2): (6,), (4, 2): (7,), (5, 2): (8,)}.get(
                    (turn, lag), ()
                ):
                    ahead(later)

    def vector(row, slot=0):
        return vecs[slot, row : row + 1, :]

    def build_masks():
        for r in range(row_count):
            place = pl.ds(z * row_count + r, 1)
            seg = jnp.broadcast_to(seg_ref[place, :].astype(F32), (SEQ, SEQ))
            pad = jnp.broadcast_to(pad_ref[place, :], (SEQ, SEQ))
            allowed = (seg == seg.T) & (pad == 1)
            masks[r] = jnp.where(allowed, 0.0, MASKED)

    def project(j):
        bias = vector(0, j)[:, : 3 * cols]

        def body(span):
            qkv[j, span] = (dot(x_ref[span], weights[0, j, : 3 * cols], "NT") + bias).astype(BF)

        chunks(tokens, 256, body)

    def head(joined, part, h):
        return joined[:, part * cols + h * HEAD_DIM : part * cols + (h + 1) * HEAD_DIM]

    units = [(r, h) for r in range(row_count) for h in range(heads)]

    def spans(r):
        return slice(r * SEQ, (r + 1) * SEQ)

    def attend(j):
        joined = [qkv[j, spans(r)] for r in range(row_count)]
        scores = [
            dot(head(joined[r], 0, h), head(joined[r], 1, h), "NT") * SCALING + masks[r] for r, h in units
        ]
        found = []
        for (r, h), score in zip(units, scores):
            weight = jnp.exp(score - jnp.max(score, axis=-1, keepdims=True))
            found.append((weight * (1.0 / jnp.sum(weight, axis=-1, keepdims=True))).astype(BF))
        mixed = []
        for (r, h), prob in zip(units, found):
            probs[j, r, h] = prob
            mixed.append(dot(prob, head(joined[r], 2, h)).astype(BF))
        for r in range(row_count):
            ctx[j, spans(r)] = jnp.concatenate(mixed[r * heads : (r + 1) * heads], axis=1)

    def project_out():
        total = dot(ctx[0], weights[0, 0, 3 * cols :])
        for j in (1, 2, 3):
            total = total + dot(ctx[j], weights[0, j, 3 * cols :])
        acc[...] = total

    def norm_first():
        b_out, gain, shift = vector(2), vector(3), vector(4)

        def body(span):
            value = acc[span] + b_out + x_ref[span].astype(F32)
            center = value - row_mean(value)
            scale = lax.rsqrt(row_mean(center * center) + EPSILON)
            normal = center * scale
            norm_one[span] = normal
            scale_one[span] = scale
            hidden_low[span] = (normal * gain + shift).astype(BF)

        chunks(tokens, 128, body)

    def feed_in(j):
        bias = vector(1, j)

        def body(span):
            pre = dot(hidden_low[span], weights[1, j]) + bias
            cumulative = 0.5 + 0.5 * lax.erf(pre * (1.0 / math.sqrt(2.0)))
            density = jnp.exp(pre * pre * -0.5) * (1.0 / math.sqrt(2.0 * math.pi))
            act[j, span] = (pre * cumulative).astype(BF)
            slope[j][span] = (cumulative + pre * density).astype(BF)

        chunks(tokens, 128, body)

    def feed_out(j):
        part = dot(act[j], weights[2, j])
        acc[...] = part if j == 0 else acc[...] + part

    def small_add(row, value):
        totals[0, pl.ds(row, 1), : value.shape[1]] += value

    def norm_second():
        gain_a, shift_a, b_outer = vector(3), vector(4), vector(5)
        gain, shift = vector(6), vector(7)

        def body(span):
            value = acc[span] + b_outer + (norm_one[span] * gain_a + shift_a)
            center = value - row_mean(value)
            scale = lax.rsqrt(row_mean(center * center) + EPSILON)
            normal = center * scale
            given = cot[span].astype(F32)
            cot[span] = (normal * gain + shift).astype(BF)
            pulled = given * gain
            grad = scale * (pulled - row_mean(pulled) - normal * row_mean(pulled * normal))
            d_norm[span] = grad
            d_low[span] = grad.astype(BF)
            small_add(3, column_sum(grad))
            small_add(4, column_sum(given * normal))
            small_add(5, column_sum(given))

        chunks(tokens, 128, body)

    def feed_out_back(j):
        def body(span):
            grad = (dot(d_low[span], weights[2, j], "NT") * slope[j][span].astype(F32)).astype(BF)
            act[j, span] = grad
            small_add(12 + shard_of[j], column_sum(grad.astype(F32)))

        chunks(tokens, 256, body)

    def feed_in_back(j, first):
        def body(span):
            part = dot(act[j, span], weights[1, j], "NT")
            acc[span] = part if first else acc[span] + part

        chunks(tokens, 256, body)

    def norm_first_back():
        gain = vector(3)

        def body(span):
            given = acc[span] + d_norm[span]
            normal = norm_one[span]
            pulled = given * gain
            grad = scale_one[span] * (pulled - row_mean(pulled) - normal * row_mean(pulled * normal))
            d_norm[span] = grad
            d_low[span] = grad.astype(BF)
            small_add(0, column_sum(grad))
            small_add(1, column_sum(given * normal))
            small_add(2, column_sum(given))

        chunks(tokens, 128, body)

    def attend_back(j):
        d_ctx[...] = dot(d_low[...], weights[0, j, 3 * cols :], "NT").astype(BF)
        joined = [qkv[j, spans(r)] for r in range(row_count)]
        given = [d_ctx[spans(r)] for r in range(row_count)]
        d_outs = [given[r][:, h * HEAD_DIM : (h + 1) * HEAD_DIM] for r, h in units]
        d_probs = [dot(d_out, head(joined[r], 2, h), "NT") for (r, h), d_out in zip(units, d_outs)]
        prob_list = [probs[j, r, h] for r, h in units]
        d_scores = []
        for d_prob, prob in zip(d_probs, prob_list):
            wide = prob.astype(F32)
            inner = jnp.sum(d_prob * wide, axis=-1, keepdims=True)
            d_scores.append((wide * (d_prob - inner)).astype(BF))
        d_values = [dot(prob, d_out, "TN").astype(BF) for prob, d_out in zip(prob_list, d_outs)]
        d_queries = [(dot(ds, head(joined[r], 1, h)) * SCALING).astype(BF) for (r, h), ds in zip(units, d_scores)]
        d_keys = [(dot(ds, head(joined[r], 0, h), "TN") * SCALING).astype(BF) for (r, h), ds in zip(units, d_scores)]
        total = jnp.zeros((1, 3 * cols), F32)
        for r in range(row_count):
            mine_heads = slice(r * heads, (r + 1) * heads)
            joined_grad = jnp.concatenate(d_queries[mine_heads] + d_keys[mine_heads] + d_values[mine_heads], axis=1)
            qkv[j, spans(r)] = joined_grad
            total = total + column_sum(joined_grad.astype(F32))
        small_add(8 + shard_of[j], total)

    def input_back(j):
        def body(span):
            d_norm[span] = d_norm[span] + dot(qkv[j, span], weights[0, j, : 3 * cols])

        chunks(tokens, 256, body)

    mine, theirs = rows(core * half, half), rows((1 - core) * half, half)
    mine_cols = pl.ds(pl.multiple_of(core * half, 128), half)
    their_cols = pl.ds(pl.multiple_of((1 - core) * half, 128), half)
    order = [(k, j) for k in range(3) for j in (1, 2, 3, 0)]
    swaps = {
        (k, j): pltpu.make_async_remote_copy(
            src_ref=grads.at[k % 2, j, theirs],
            dst_ref=from_core.at[k % 2, j],
            send_sem=csend.at[k, j],
            recv_sem=crecv.at[k, j],
            device_id=peers["c"],
            device_id_type=MESH,
        )
        for k, j in order
    }
    folds = {
        (k, j): Fold(
            grads.at[k % 2, j, mine], from_core.at[k % 2, j], from_one.at[k, j], from_two.at[k, j],
            fsend.at[k, j], frecv.at[k, j],
        )
        for k, j in order
    }
    over = {
        (k, j): pltpu.make_async_remote_copy(
            src_ref=zone.at[k, j],
            dst_ref=from_z.at[k, landing_place[j] - 1],
            send_sem=zsend.at[k, j - 1],
            recv_sem=zrecv.at[k, landing_place[j] - 1],
            device_id=line[j],
            device_id_type=MESH,
        )
        for k, j in order
        if j and j not in EARLY[k]
    }
    early_slots = [(k, j) for k, j in order if j in EARLY[k]]
    early_base = {k: early_slots.index((k, 1)) for k in range(3)}

    def early_pair(k, place, item):
        found = []
        for p in (0, 1):
            found.append(
                pltpu.make_async_remote_copy(
                    src_ref=grads.at[k % 2, item[1], mine].at[folds[item].keep_one[p]],
                    dst_ref=from_early.at[early_base[k] + place, p],
                    send_sem=esend.at[early_slots.index(item), p],
                    recv_sem=erecv.at[early_base[k] + place, p],
                    device_id=line[item[1]],
                    device_id_type=MESH,
                )
            )
        return found

    early = {(k, j): early_pair(k, landing_place[j] - 1, (k, j)) for k, j in early_slots}

    def merge(k, first):
        parts = [first] if first is not None else []
        for place in range(len(EARLY[k])):
            for copy in early_pair(k, place, (k, 1)):
                copy.wait_recv()
            parts.append(from_early.at[early_base[k] + place])
        folds[k, 0].combine(parts, True)

    sums = [Spread(summed_out[k], half, asend.at[k], arecv.at[k]) for k in range(3)]
    tiny = Everyone(totals, landing, ssend, srecv, everyone)

    def settle(k):
        for place in range(len(EARLY[k]), 3):
            pltpu.make_async_remote_copy(
                src_ref=zone.at[k, 1],
                dst_ref=from_z.at[k, place],
                send_sem=zsend.at[k, place],
                recv_sem=zrecv.at[k, place],
                device_id=peers[1],
                device_id_type=MESH,
            ).wait_recv()
        summed = zone[k, 0].astype(F32)
        for place in range(len(EARLY[k]), 3):
            summed = summed + from_z[k, place].astype(F32)
        for step, peer in enumerate(others):
            outer_in[k, step, 0] = summed.astype(BF)
            copy = pltpu.make_async_remote_copy(
                src_ref=outer_in.at[k, step, 0],
                dst_ref=outer_in.at[k, step, 1],
                send_sem=osend.at[k, step],
                recv_sem=orecv.at[k, step],
                device_id=peer,
                device_id_type=MESH,
            )
            copy.start()
            copy.wait()
            summed = outer_in[k, step, 0].astype(F32) + outer_in[k, step, 1].astype(F32)
        for p in (0, 1):
            summed_out[k][sums[k].own[p]] = summed[p * eighth : (p + 1) * eighth].astype(BF)
        sums[k].start(0)

    def drain(item):
        swaps[item].wait_send()
        folds[item].drain(item not in early)
        for copy in early.get(item, ()):
            copy.wait_send()

    def grad_block(k, j):
        if k == 0:
            for span, picked in ((theirs, their_cols), (mine, mine_cols)):
                grads[0, j, span] = dot(act[j, :, picked], d_low[...], "TN").astype(BF)
                if span is theirs and j:
                    swaps[k, j].start()
            if j == 0:
                feed_out_back(j)
                swaps[k, j].start()
        elif k == 1:
            for span, picked in ((theirs, their_cols), (mine, mine_cols)):
                grads[1, j, span] = dot(hidden_low[:, picked], act[j], "TN").astype(BF)
                if span is theirs:
                    swaps[k, j].start()
        else:
            drain((0, j))
            pl.semaphore_wait(credit.at[j], 1)
            grads[0, j, : 3 * cols] = dot(qkv[j], x_ref[...], "TN").astype(BF)
            grads[0, j, 3 * cols :] = dot(ctx[j], d_low[...], "TN").astype(BF)
            swaps[k, j].start()

    def reduce_turn(turn):
        total = len(order)
        if turn < total:
            item = order[turn]
            swaps[item].wait_recv()
            folds[item].step_core(grads.at[item[0] % 2, item[1], mine])
            if item[0] == 0:
                pl.semaphore_signal(credit.at[item[1]], inc=1, device_id=peers["c"], device_id_type=MESH)
        if 0 <= turn - 1 < total:
            item = k, j = order[turn - 1]
            folds[item].step_one()
            if j == 0 and MERGE_TURN[k] == turn:
                merge(k, from_one.at[item])
            else:
                folds[item].combine([from_one.at[item]], j and item not in early)
                for copy in early.get(item, ()):
                    copy.start()
        for k in range(3):
            if MERGE_TURN[k] == turn and order[turn - 1] != (k, 0):
                merge(k, None)
        if 0 <= turn - 2 < total:
            item = order[turn - 2]
            if item[1] and item not in early:
                folds[item].step_two(zone.at[item[0], item[1]])
                over[item].start()
        for k in range(3):
            if turn == MERGE_TURN[k] + 1:
                folds[k, 0].step_two(zone.at[k, 0])
        for k in (2, 1, 0):
            if turn == SETTLE_TURN[k]:
                settle(k)
            step = turn - SETTLE_TURN[k] - 1
            if 0 <= step < 3:
                sums[k].finish(step)
                if step < 2:
                    sums[k].start(step + 1)
                elif k < 2:
                    copy = pltpu.make_async_copy(summed_out[k], summed_hbm.at[k], early_sem.at[k])
                    copy.start()
                    early_copies.append(copy)

    early_copies = []

    vecs[0] = jnp.zeros_like(vecs[0])
    for row, start, ref in (
        (0, 0, b_query), (0, 2 * cols, b_value), (1, 0, b_inner), (2, 0, b_out), (3, 0, gain_one),
        (4, 0, shift_one), (5, 0, b_outer), (6, 0, gain_two), (7, 0, shift_two),
    ):
        size = ref.shape[0]
        vecs[0, row : row + 1, start : start + size] = ref[...].astype(F32).reshape(1, size)
    for number in (1, 5, 6, 7):
        local_copies[number].wait()
    pl.semaphore_wait(barrier, len(greeted))
    send_own(0)
    for u in (1, 2, 3):
        vec_copies[u].start()
    build_masks()
    totals[0] = jnp.zeros_like(totals[0])
    local_copies[0].wait()
    project(0)
    gather_turn(0)
    gather_turn(1)
    attend(0)
    gather_turn(2)
    for j in (1, 2, 3):
        gather_turn(2 + j)
        if j == 1:
            for place in range(3):
                pltpu.make_async_remote_copy(
                    src_ref=vecs.at[0],
                    dst_ref=vecs.at[place + 1],
                    send_sem=v_send.at[place],
                    recv_sem=v_recv.at[place],
                    device_id=peers[1],
                    device_id_type=MESH,
                ).wait_recv()
        project(j)
        attend(j)
    gather_turn(6)
    project_out()
    norm_first()
    gather_turn(7)
    local_copies[2].wait()
    feed_in(0)
    feed_in(1)
    gather_turn(8)
    feed_in(2)
    feed_in(3)
    gather_turn(9)
    local_copies[3].wait()
    feed_out(0)
    feed_out(1)
    for j in (2, 3):
        spreads[2, j].finish(2)
        feed_out(j)
    local_copies[4].wait()
    norm_second()
    out_copy = pltpu.make_async_copy(cot, out_hbm, local_sem.at[0])
    out_copy.start()

    grad_block(0, 1)
    grad_block(0, 2)
    reduce_turn(0)
    grad_block(0, 3)
    feed_out_back(1)
    feed_out_back(2)
    reduce_turn(1)
    feed_out_back(3)
    grad_block(0, 0)
    feed_in_back(1, True)
    reduce_turn(2)
    for j in (2, 3, 0):
        feed_in_back(j, False)
    norm_first_back()
    grad_block(1, 1)
    reduce_turn(3)
    for place, j in enumerate((2, 3, 0)):
        grad_block(1, j)
        attend_back((1, 2, 3)[place])
        reduce_turn(4 + place)
    attend_back(0)
    for place, j in enumerate((1, 2, 3, 0)):
        grad_block(2, j)
        if place:
            input_back(order[7 + place][1])
        reduce_turn(7 + place)
    input_back(0)
    reduce_turn(11)
    grad_in_copy = pltpu.make_async_copy(d_norm, grad_in_hbm, local_sem.at[1])
    grad_in_copy.start()
    tiny.start(0)
    for extra in range(6):
        if extra < len(everyone):
            tiny.finish(extra)
            if extra + 1 < len(everyone):
                tiny.start(extra + 1)
        reduce_turn(len(order) + extra)
    for extra in range(6, len(everyone)):
        tiny.finish(extra)
        if extra + 1 < len(everyone):
            tiny.start(extra + 1)
    small_copy = pltpu.make_async_copy(totals.at[len(everyone)], small_hbm, local_sem.at[2])
    small_copy.start()
    last_copy = pltpu.make_async_copy(summed_out[2], summed_hbm.at[2], local_sem.at[3])
    last_copy.start()

    def settled(copies):
        for copy in copies:
            copy.wait_send()

    for k in range(3):
        settled(near[k])
        for u in (2, 3):
            pl.when(middle == 1)(lambda k=k, u=u: settled(across[k, u] + onward[k, u]))
    for item in gathered:
        spreads[item].drain()
    for j in (1, 2, 3):
        vec_copies[j].wait_send()
    for item in order:
        if item[0]:
            drain(item)
        if item in over:
            over[item].wait_send()
    for spread in sums:
        spread.drain()
    tiny.drain()
    for copy in [out_copy, grad_in_copy, small_copy, last_copy] + early_copies:
        copy.wait()


def block(outer, x, cot, seg, pad, *others):
    tokens, width = x.shape
    side = others[4].shape[0]
    half, cols = side // 2, side // 4
    heads = cols // HEAD_DIM
    row_count = tokens // SEQ
    steps = 5 + int(math.log2(outer))
    more = max(steps - 5, 1)
    outer_rows = half // 4 if outer > 1 else 16
    early = sum(len(slots) for slots in EARLY)
    dma = pltpu.SemaphoreType.DMA
    vmem = pltpu.VMEM
    any_space = pl.BlockSpec(memory_space=pl.ANY)
    in_vmem = pl.BlockSpec(memory_space=pltpu.VMEM)
    return pl.pallas_call(
        functools.partial(block_body, outer),
        out_shape=(
            jax.ShapeDtypeStruct((tokens, width), BF),
            jax.ShapeDtypeStruct((tokens, width), F32),
            jax.ShapeDtypeStruct((3, side, width), BF),
            jax.ShapeDtypeStruct((16, width), F32),
        ),
        in_specs=[any_space] * 2 + [in_vmem] * 2 + [any_space] * 6 + [in_vmem] * 9,
        out_specs=(any_space,) * 4,
        scratch_shapes=[
            vmem((3, 4, side, width), BF),
            vmem((tokens, width), BF),
            vmem((tokens, width), BF),
            vmem((row_count, SEQ, SEQ), F32),
            vmem((4, 8, width), F32),
            vmem((4, tokens, 3 * cols), BF),
            vmem((4, tokens, cols), BF),
            vmem((4, row_count, heads, SEQ, SEQ), BF),
            vmem((tokens, width), F32),
            vmem((tokens, 1), F32),
            vmem((tokens, width), BF),
            vmem((4, tokens, side), BF),
            vmem((max(3 * side, 4 * tokens), side), BF),
            vmem((tokens, width), F32),
            vmem((tokens, width), F32),
            vmem((tokens, width), BF),
            vmem((tokens, cols), BF),
            vmem((2, 4, side, width), BF),
            vmem((2, 4, half, width), BF),
            vmem((3, 4, 2, half // 4, width), BF),
            vmem((3, 4, 2, half // 8, width), BF),
            vmem((3, 4, half // 4, width), BF),
            vmem((3, 3, half // 4, width), BF),
            vmem((early, 2, half // 4, width), BF),
            vmem((3, more, 2, outer_rows, width), BF),
            vmem((steps + 1, 16, width), F32),
            vmem((steps, 16, width), F32),
            dma((3, 3, 2, 2)), dma((3, 3, 2)), dma((3, 3, 5)), dma((3, 3, 5)), dma((3,)), dma((3,)), dma((8,)), dma((2,)),
            dma((3, 4)), dma((3, 4)), dma((3, 4, 4)), dma((3, 4, 4)), dma((3, 3)), dma((3, 3)), dma((early, 2)), dma((early, 2)),
            dma((3, 5)), dma((3, 5)), dma((3, more)), dma((3, more)), dma((steps,)), dma((steps,)),
            pltpu.SemaphoreType.REGULAR((4,)),
        ],
        compiler_params=pltpu.CompilerParams(
            collective_id=0, has_side_effects=True, vmem_limit_bytes=67043328
        ),
        name="block",
    )(x, cot, seg, pad, *others)


def local(
    outer, block_input, cotangent, segment_ids, pad_mask,
    w_query, b_query, w_key, w_value, b_value, w_out, b_out, gain_one, shift_one,
    w_inner, b_inner, w_outer, b_outer, gain_two, shift_two,
):
    tokens, width = block_input.shape
    cols = w_query.shape[1]
    output, grad_input, summed, small = block(
        outer, block_input, cotangent, segment_ids.reshape(-1, SEQ), pad_mask.reshape(-1, SEQ),
        w_query.T, w_key.T, w_value.T, w_out, w_inner, w_outer,
        b_query, b_value, b_inner, b_out, gain_one, shift_one, b_outer, gain_two, shift_two,
    )
    outs = list(finish(output, grad_input, summed, small, cols))
    for place in (2, 4, 5):
        outs[place] = outs[place].T
    return tuple(outs)


def finish_body(
    out_hbm, grad_in_hbm, summed_hbm, small_ref,
    output, grad_input, g_query, gb_query, g_key, g_value, gb_value, g_out, gb_out, gg_one, gs_one,
    g_inner, gb_inner, g_outer, gb_outer, gg_two, gs_two,
    out_held, in_held, summed, wide, turned, flat, in_sem, out_sem,
):
    z = lax.axis_index("tensor")
    cols = gb_query.shape[0]
    reads = [pltpu.make_async_copy(summed_hbm.at[k], summed.at[k], in_sem.at[k]) for k in (0, 1, 2)]
    reads.append(pltpu.make_async_copy(grad_in_hbm, in_held, in_sem.at[3]))
    reads.append(pltpu.make_async_copy(out_hbm, out_held, in_sem.at[4]))
    for copy in reads:
        copy.start()
    for row, ref in ((0, gb_out), (1, gg_one), (2, gs_one), (3, gb_outer), (4, gg_two), (5, gs_two)):
        ref[...] = small_ref[row : row + 1, :].reshape(ref.shape)
    own = small_ref[pl.ds(8 + z, 1), :]
    gb_query[...] = own[:, :cols].reshape(gb_query.shape)
    gb_value[...] = own[:, 2 * cols : 3 * cols].reshape(gb_value.shape)
    gb_inner[...] = small_ref[pl.ds(12 + z, 1), :].reshape(gb_inner.shape)
    writes = []

    def write(source, target):
        copy = pltpu.make_async_copy(source, target, out_sem.at[len(writes)])
        copy.start()
        writes.append(copy)

    for k, target in ((0, g_outer), (1, g_inner)):
        reads[k].wait()
        wide[k] = summed[k].astype(F32)
        write(wide.at[k], target)
    reads[2].wait()
    for part, target in enumerate((g_query, g_key, g_value)):
        turned[part] = summed[2, part * cols : (part + 1) * cols].astype(F32)
        write(turned.at[part], target)
    flat[...] = summed[2, 3 * cols :].astype(F32)
    write(flat, g_out)
    reads[3].wait()
    write(in_held, grad_input)
    reads[4].wait()
    write(out_held, output)
    for copy in writes:
        copy.wait()


def finish(output, grad_input, summed, small, cols):
    (tokens, width), side = output.shape, summed.shape[1]
    shape = jax.ShapeDtypeStruct
    any_space = pl.BlockSpec(memory_space=pl.ANY)
    in_vmem = pl.BlockSpec(memory_space=pltpu.VMEM)
    line, short, flat, big = shape((width,), F32), shape((cols,), F32), shape((cols, width), F32), shape((side, width), F32)
    outs = (
        (shape((tokens, width), BF), 0), (shape((tokens, width), F32), 0), (flat, 0), (short, 1), (flat, 0), (flat, 0),
        (short, 1), (flat, 0), (line, 1), (line, 1), (line, 1), (big, 0), (line, 1), (big, 0),
        (line, 1), (line, 1), (line, 1),
    )
    dma = pltpu.SemaphoreType.DMA
    return pl.pallas_call(
        finish_body,
        out_shape=tuple(item for item, _ in outs),
        in_specs=[any_space, any_space, any_space, in_vmem],
        out_specs=tuple(in_vmem if held else any_space for _, held in outs),
        scratch_shapes=[
            pltpu.VMEM((tokens, width), BF),
            pltpu.VMEM((tokens, width), F32),
            pltpu.VMEM((3, side, width), BF),
            pltpu.VMEM((2, side, width), F32),
            pltpu.VMEM((3, cols, width), F32),
            pltpu.VMEM((cols, width), F32),
            dma((5,)), dma((8,)),
        ],
        compiler_params=pltpu.CompilerParams(vmem_limit_bytes=67043328),
        name="finish",
    )(output, grad_input, summed, small)


def solution(mesh):
    outer = mesh.shape["dp"] // GROUP
    row, col, both, rep = P("tensor", None), P(None, "tensor"), P(("dp", "tensor"), None), P()
    part = P("tensor")
    return jax.shard_map(
        functools.partial(local, outer),
        mesh=mesh,
        in_specs=(
            both, both, P("dp"), P("dp"), col, part, col, col, part, row, rep, rep, rep,
            col, part, row, rep, rep, rep,
        ),
        out_specs=(
            both, both, col, part, col, col, part, row, rep, rep, rep, col, part, row, rep, rep, rep,
        ),
        check_vma=False,
    )
```

```python
import functools
import math

import jax
import jax.numpy as jnp
from jax import lax
from jax.experimental import pallas as pl
from jax.experimental.pallas import tpu as pltpu
from jax.sharding import PartitionSpec as P

HEAD_DIM = 64
SEQ = 128
EPSILON = 1e-05
MASKED = -1e30
BF = jnp.bfloat16
F32 = jnp.float32
MESH = pl.DeviceIdType.MESH
GROUP = 8
WIDE = ((2, 1), (2, 3))
EARLY = ((1, 2, 3), (1,), (1,))
MERGE_TURN = (7, 8, 12)
SETTLE_TURN = (12, 13, 14)


def places():
    dp = lax.axis_index("dp")
    z = lax.axis_index("tensor")
    core = dp % 2
    along_x = (dp // 2) % 2
    along_y = (dp // 4) % 2
    peers = {
        "c": {"dp": dp + 1 - 2 * core, "tensor": z},
        "x": {"dp": dp + 2 - 4 * along_x, "tensor": z},
        "y": {"dp": dp + 4 - 8 * along_y, "tensor": z},
        1: {"dp": dp, "tensor": z + 1 - 2 * (z % 2)},
        2: {"dp": dp, "tensor": (z + 2) % 4},
        3: {"dp": dp, "tensor": 3 - z},
    }
    return dp, z, core, along_x, along_y, peers


def line_order(z):
    low, high = z % 2, z // 2
    middle = low + high - 2 * low * high
    shards = (z, z + 1 - 2 * low, (1 - middle) * ((z + 2) % 4) + middle * (3 - z), middle * ((z + 2) % 4) + (1 - middle) * (3 - z))
    return middle, shards, (0, 1, 3 - middle, 3 - middle)


def outer_peers(dp, z, outer):
    found = []
    weight = GROUP
    while weight < GROUP * outer:
        bit = (dp // weight) % 2
        found.append({"dp": dp + weight - 2 * weight * bit, "tensor": z})
        weight *= 2
    return found


def rows(start, size):
    return pl.ds(pl.multiple_of(start, 16), size)


class Spread:
    def __init__(self, block, half, send, recv, wide=False):
        _, _, core, ax, ay, peers = places()
        base = core * half
        part = half // 2
        quarter = part // 2
        eighth = quarter // 2
        first = base + ax * quarter
        second = base + part + ay * quarter
        self.steps = []
        plan = (
            ((rows(first + ay * eighth, eighth), "y"), (rows(second + ax * eighth, eighth), "x")),
            ((rows(first, quarter), "x"), (rows(second, quarter), "y")),
            ((rows(base, half), "c"),),
        )
        place = 0
        for number, step in enumerate(plan):
            copies = []
            for span, name in () if wide and number == 0 else step:
                copies.append(
                    pltpu.make_async_remote_copy(
                        src_ref=block.at[span],
                        dst_ref=block.at[span],
                        send_sem=send.at[place],
                        recv_sem=recv.at[place],
                        device_id=peers[name],
                        device_id_type=MESH,
                    )
                )
                place += 1
            self.steps.append(copies)
        self.own = (rows(first + ay * eighth, eighth), rows(second + ax * eighth, eighth))
        if wide:
            self.own = (rows(first, quarter), rows(second, quarter))

    def start(self, step):
        for copy in self.steps[step]:
            copy.start()

    def finish(self, step):
        for copy in self.steps[step]:
            copy.wait_recv()

    def drain(self):
        for step in self.steps:
            for copy in step:
                copy.wait_send()


def plus(left, right):
    return (left.astype(F32) + right.astype(F32)).astype(BF)


class Fold:
    def __init__(self, held, from_core, from_one, from_two, send, recv):
        _, _, core, ax, ay, peers = places()
        half = held.shape[0]
        part, quarter, eighth = half // 2, half // 4, half // 8
        self.held = held
        self.from_core = from_core
        self.from_one = from_one
        self.from_two = from_two
        self.quarter, self.eighth = quarter, eighth
        self.give_one = (rows((1 - ax) * quarter, quarter), rows(part + (1 - ay) * quarter, quarter))
        self.keep_one = (rows(ax * quarter, quarter), rows(part + ay * quarter, quarter))
        self.give_two = (
            rows(ax * quarter + (1 - ay) * eighth, eighth),
            rows(part + ay * quarter + (1 - ax) * eighth, eighth),
        )
        self.keep_two = (
            rows(ax * quarter + ay * eighth, eighth),
            rows(part + ay * quarter + ax * eighth, eighth),
        )
        self.inside = (rows((1 - ay) * eighth, eighth), rows((1 - ax) * eighth, eighth))
        self.inside_keep = (rows(ay * eighth, eighth), rows(ax * eighth, eighth))
        self.one = [
            pltpu.make_async_remote_copy(
                src_ref=held.at[self.give_one[p]],
                dst_ref=from_one.at[p],
                send_sem=send.at[p],
                recv_sem=recv.at[p],
                device_id=peers["xy"[p]],
                device_id_type=MESH,
            )
            for p in (0, 1)
        ]
        self.two = [
            pltpu.make_async_remote_copy(
                src_ref=held.at[self.give_two[p]],
                dst_ref=from_two.at[p],
                send_sem=send.at[2 + p],
                recv_sem=recv.at[2 + p],
                device_id=peers["yx"[p]],
                device_id_type=MESH,
            )
            for p in (0, 1)
        ]

    def step_core(self, own):
        for spans in (self.give_one, self.keep_one):
            for p in (0, 1):
                span = spans[p]
                self.held[span] = plus(own[span], self.from_core[span])
            if spans is self.give_one:
                for copy in self.one:
                    copy.start()

    def step_one(self):
        for copy in self.one:
            copy.wait_recv()

    def combine(self, parts, send):
        for spans, insides in ((self.give_two, self.inside), (self.keep_two, self.inside_keep)):
            for p in (0, 1):
                total = self.held[spans[p]].astype(F32)
                for part in parts:
                    total = total + part[p, insides[p]].astype(F32)
                self.held[spans[p]] = total.astype(BF)
                if send and spans is self.give_two:
                    self.two[p].start()

    def step_two(self, result):
        for p in (0, 1):
            self.two[p].wait_recv()
            result[p * self.eighth : (p + 1) * self.eighth] = plus(self.held[self.keep_two[p]], self.from_two[p])

    def drain(self, halved):
        for copy in self.one + (self.two if halved else []):
            copy.wait_send()


class Everyone:
    def __init__(self, total, landing, send, recv, peer_list):
        self.total, self.landing = total, landing
        self.copies = [
            pltpu.make_async_remote_copy(
                src_ref=total.at[step],
                dst_ref=landing.at[step],
                send_sem=send.at[step],
                recv_sem=recv.at[step],
                device_id=peer,
                device_id_type=MESH,
            )
            for step, peer in enumerate(peer_list)
        ]

    def start(self, step):
        self.copies[step].start()

    def finish(self, step):
        self.copies[step].wait_recv()
        self.total[step + 1] = self.total[step] + self.landing[step]

    def drain(self):
        for copy in self.copies:
            copy.wait_send()


DIMS = {"NN": ((1,), (0,)), "NT": ((1,), (1,)), "TN": ((0,), (0,))}
SCALING = 1.0 / math.sqrt(HEAD_DIM)


def dot(left, right, form="NN"):
    return lax.dot_general(left, right, (DIMS[form], ((), ())), preferred_element_type=F32)


def column_sum(values):
    return jnp.sum(values, axis=0, keepdims=True)


def row_mean(values):
    return jnp.mean(values, axis=-1, keepdims=True)


def chunks(count, size, body):
    def run(step, carry):
        body(rows(step * size, size))
        return carry

    lax.fori_loop(0, count // size, run, 0)


def block_body(
    outer,
    x_hbm, cot_hbm, seg_ref, pad_ref, w_query, w_key, w_value, w_out, own_b, own_c,
    b_query, b_value, b_inner, b_out, gain_one, shift_one, b_outer, gain_two, shift_two,
    out_hbm, grad_in_hbm, summed_hbm, small_hbm,
    weights, x_ref, cot, masks, vecs, qkv, ctx, probs, norm_one, scale_one, hidden_low, act, shared,
    acc, d_norm, d_low, d_ctx,
    grads, from_core, from_one, from_two, zone, from_z, from_early, outer_in, totals, landing,
    gz_send, gz_recv, g_send, g_recv, v_send, v_recv, local_sem, early_sem,
    csend, crecv, fsend, frecv, zsend, zrecv, esend, erecv, asend, arecv, osend, orecv, ssend, srecv, credit,
):
    dp, z, core, ax, ay, peers = places()
    others = outer_peers(dp, z, outer)
    everyone = [peers[name] for name in ("c", "x", "y", 1, 2)] + others
    tokens, width = x_ref.shape
    side = own_b.shape[0]
    half = side // 2
    eighth = half // 8
    cols = side // 4
    heads = cols // HEAD_DIM
    row_count = tokens // SEQ
    slope = [shared.at[u * tokens : (u + 1) * tokens] for u in range(4)]
    summed_out = [shared.at[k * side : (k + 1) * side] for k in range(3)]
    middle, shard_of, landing_place = line_order(z)
    line = {u: {"dp": dp, "tensor": shard_of[u]} for u in (1, 2, 3)}

    local_copies = [
        pltpu.make_async_copy(x_hbm, x_ref, local_sem.at[0]),
        pltpu.make_async_copy(w_out, weights.at[0, 0, 3 * cols :], local_sem.at[1]),
        pltpu.make_async_copy(own_b, weights.at[1, 0], local_sem.at[2]),
        pltpu.make_async_copy(own_c, weights.at[2, 0], local_sem.at[3]),
        pltpu.make_async_copy(cot_hbm, cot, local_sem.at[4]),
    ] + [
        pltpu.make_async_copy(ref, weights.at[0, 0, part * cols : (part + 1) * cols], local_sem.at[5 + part])
        for part, ref in enumerate((w_query, w_key, w_value))
    ]
    for number in (5, 6, 7, 1, 0, 2, 3, 4):
        local_copies[number].start()
    barrier = pltpu.get_barrier_semaphore()
    greeted = [peers[name] for name in ("c", "x", "y", 1, 2, 3)] + others
    for peer in greeted:
        pl.semaphore_signal(barrier, inc=1, device_id=peer, device_id_type=MESH)

    spreads, arrivals, vec_copies = {}, {}, {}
    gathered = [(k, u) for k in range(3) for u in (1, 2, 3)]

    def hop(k, source, target, peer):
        found = []
        for piece, span in enumerate(spreads[k, target].own):
            src = weights.at[k, source, span]
            if source == 0 and k:
                src = (None, own_b, own_c)[k].at[span]
            found.append(
                pltpu.make_async_remote_copy(
                    src_ref=src,
                    dst_ref=weights.at[k, target, span],
                    send_sem=gz_send.at[k, target - 1, 0 if peer is peers[1] else 1, piece],
                    recv_sem=gz_recv.at[k, target - 1, piece],
                    device_id=peer,
                    device_id_type=MESH,
                )
            )
        return found

    for k, u in gathered:
        spreads[k, u] = Spread(weights.at[k, u], half, g_send.at[k, u - 1], g_recv.at[k, u - 1], (k, u) in WIDE)
    near = {k: hop(k, 0, 1, peers[1]) for k in range(3)}
    across = {(k, 2): hop(k, 0, 2, peers[3]) for k in range(3)}
    across.update({(k, 3): hop(k, 1, 3, peers[3]) for k in range(3)})
    onward = {(k, u): hop(k, u, u, peers[1]) for k in range(3) for u in (2, 3)}
    for u in (1, 2, 3):
        vec_copies[u] = pltpu.make_async_remote_copy(
            src_ref=vecs.at[0],
            dst_ref=vecs.at[landing_place[u]],
            send_sem=v_send.at[u - 1],
            recv_sem=v_recv.at[landing_place[u] - 1],
            device_id=line[u],
            device_id_type=MESH,
        )

    def begin(copies):
        for copy in copies:
            copy.start()

    def send_own(k):
        begin(near[k])
        pl.when(middle == 1)(lambda: begin(across[k, 2]))

    landed = {}
    for k in range(3):
        landed.update({(k, 1): near[k], (k, 2): across[k, 2], (k, 3): across[k, 3]})

    def arrive(item):
        for copy in landed[item]:
            copy.wait_recv()

    def ahead(turn):
        k, u = gathered[turn]

        def forward():
            arrive((k, u))
            begin(across[k, 3] if u == 1 else onward[k, u])

        pl.when(middle == 1)(forward)
        if u == 2 and k < 2:
            send_own(k + 1)

    def gather_turn(turn):
        total = len(gathered)
        if turn == 0:
            ahead(0)
        if turn < total:
            item = gathered[turn]
            pl.when(middle == 0)(lambda: arrive(item))
            spreads[item].start(1 if item in WIDE else 0)
        for lag in (1, 2, 3):
            if 0 <= turn - lag < total:
                item = gathered[turn - lag]
                step = lag - 1 + (item in WIDE)
                if step < 3:
                    spreads[item].finish(step)
                if step < 2:
                    spreads[item].start(step + 1)
            if lag < 3:
                for later in {(0, 1): (1,), (1, 1): (2,), (1, 2): (3,), (2, 2): (4,), (3, 1): (5,), (3, 2): (6,), (4, 2): (7,), (5, 2): (8,)}.get(
                    (turn, lag), ()
                ):
                    ahead(later)

    def vector(row, slot=0):
        return vecs[slot, row : row + 1, :]

    def build_masks():
        for r in range(row_count):
            place = pl.ds(z * row_count + r, 1)
            seg = jnp.broadcast_to(seg_ref[place, :].astype(F32), (SEQ, SEQ))
            pad = jnp.broadcast_to(pad_ref[place, :], (SEQ, SEQ))
            allowed = (seg == seg.T) & (pad == 1)
            masks[r] = jnp.where(allowed, 0.0, MASKED)

    def project(j):
        bias = vector(0, j)[:, : 3 * cols]

        def body(span):
            qkv[j, span] = (dot(x_ref[span], weights[0, j, : 3 * cols], "NT") + bias).astype(BF)

        chunks(tokens, 256, body)

    def head(joined, part, h):
        return joined[:, part * cols + h * HEAD_DIM : part * cols + (h + 1) * HEAD_DIM]

    units = [(r, h) for r in range(row_count) for h in range(heads)]

    def spans(r):
        return slice(r * SEQ, (r + 1) * SEQ)

    def attend(j):
        joined = [qkv[j, spans(r)] for r in range(row_count)]
        scores = [
            dot(head(joined[r], 0, h), head(joined[r], 1, h), "NT") * SCALING + masks[r] for r, h in units
        ]
        found = []
        for (r, h), score in zip(units, scores):
            weight = jnp.exp(score - jnp.max(score, axis=-1, keepdims=True))
            found.append((weight * (1.0 / jnp.sum(weight, axis=-1, keepdims=True))).astype(BF))
        mixed = []
        for (r, h), prob in zip(units, found):
            probs[j, r, h] = prob
            mixed.append(dot(prob, head(joined[r], 2, h)).astype(BF))
        for r in range(row_count):
            ctx[j, spans(r)] = jnp.concatenate(mixed[r * heads : (r + 1) * heads], axis=1)

    def project_out():
        total = dot(ctx[0], weights[0, 0, 3 * cols :])
        for j in (1, 2, 3):
            total = total + dot(ctx[j], weights[0, j, 3 * cols :])
        acc[...] = total

    def norm_first():
        b_out, gain, shift = vector(2), vector(3), vector(4)

        def body(span):
            value = acc[span] + b_out + x_ref[span].astype(F32)
            center = value - row_mean(value)
            scale = lax.rsqrt(row_mean(center * center) + EPSILON)
            normal = center * scale
            norm_one[span] = normal
            scale_one[span] = scale
            hidden_low[span] = (normal * gain + shift).astype(BF)

        chunks(tokens, 128, body)

    def feed_in(j):
        bias = vector(1, j)

        def body(span):
            pre = dot(hidden_low[span], weights[1, j]) + bias
            cumulative = 0.5 + 0.5 * lax.erf(pre * (1.0 / math.sqrt(2.0)))
            density = jnp.exp(pre * pre * -0.5) * (1.0 / math.sqrt(2.0 * math.pi))
            act[j, span] = (pre * cumulative).astype(BF)
            slope[j][span] = (cumulative + pre * density).astype(BF)

        chunks(tokens, 128, body)

    def feed_out(j):
        part = dot(act[j], weights[2, j])
        acc[...] = part if j == 0 else acc[...] + part

    def small_add(row, value):
        totals[0, pl.ds(row, 1), : value.shape[1]] += value

    def norm_second():
        gain_a, shift_a, b_outer = vector(3), vector(4), vector(5)
        gain, shift = vector(6), vector(7)

        def body(span):
            value = acc[span] + b_outer + (norm_one[span] * gain_a + shift_a)
            center = value - row_mean(value)
            scale = lax.rsqrt(row_mean(center * center) + EPSILON)
            normal = center * scale
            given = cot[span].astype(F32)
            cot[span] = (normal * gain + shift).astype(BF)
            pulled = given * gain
            grad = scale * (pulled - row_mean(pulled) - normal * row_mean(pulled * normal))
            d_norm[span] = grad
            d_low[span] = grad.astype(BF)
            small_add(3, column_sum(grad))
            small_add(4, column_sum(given * normal))
            small_add(5, column_sum(given))

        chunks(tokens, 128, body)

    def feed_out_back(j):
        def body(span):
            grad = (dot(d_low[span], weights[2, j], "NT") * slope[j][span].astype(F32)).astype(BF)
            act[j, span] = grad
            small_add(12 + shard_of[j], column_sum(grad.astype(F32)))

        chunks(tokens, 256, body)

    def feed_in_back(j, first):
        def body(span):
            part = dot(act[j, span], weights[1, j], "NT")
            acc[span] = part if first else acc[span] + part

        chunks(tokens, 256, body)

    def norm_first_back():
        gain = vector(3)

        def body(span):
            given = acc[span] + d_norm[span]
            normal = norm_one[span]
            pulled = given * gain
            grad = scale_one[span] * (pulled - row_mean(pulled) - normal * row_mean(pulled * normal))
            d_norm[span] = grad
            d_low[span] = grad.astype(BF)
            small_add(0, column_sum(grad))
            small_add(1, column_sum(given * normal))
            small_add(2, column_sum(given))

        chunks(tokens, 128, body)

    def attend_back(j):
        d_ctx[...] = dot(d_low[...], weights[0, j, 3 * cols :], "NT").astype(BF)
        joined = [qkv[j, spans(r)] for r in range(row_count)]
        given = [d_ctx[spans(r)] for r in range(row_count)]
        d_outs = [given[r][:, h * HEAD_DIM : (h + 1) * HEAD_DIM] for r, h in units]
        d_probs = [dot(d_out, head(joined[r], 2, h), "NT") for (r, h), d_out in zip(units, d_outs)]
        prob_list = [probs[j, r, h] for r, h in units]
        d_scores = []
        for d_prob, prob in zip(d_probs, prob_list):
            wide = prob.astype(F32)
            inner = jnp.sum(d_prob * wide, axis=-1, keepdims=True)
            d_scores.append((wide * (d_prob - inner)).astype(BF))
        d_values = [dot(prob, d_out, "TN").astype(BF) for prob, d_out in zip(prob_list, d_outs)]
        d_queries = [(dot(ds, head(joined[r], 1, h)) * SCALING).astype(BF) for (r, h), ds in zip(units, d_scores)]
        d_keys = [(dot(ds, head(joined[r], 0, h), "TN") * SCALING).astype(BF) for (r, h), ds in zip(units, d_scores)]
        total = jnp.zeros((1, 3 * cols), F32)
        for r in range(row_count):
            mine_heads = slice(r * heads, (r + 1) * heads)
            joined_grad = jnp.concatenate(d_queries[mine_heads] + d_keys[mine_heads] + d_values[mine_heads], axis=1)
            qkv[j, spans(r)] = joined_grad
            total = total + column_sum(joined_grad.astype(F32))
        small_add(8 + shard_of[j], total)

    def input_back(j):
        def body(span):
            d_norm[span] = d_norm[span] + dot(qkv[j, span], weights[0, j, : 3 * cols])

        chunks(tokens, 256, body)

    mine, theirs = rows(core * half, half), rows((1 - core) * half, half)
    mine_cols = pl.ds(pl.multiple_of(core * half, 128), half)
    their_cols = pl.ds(pl.multiple_of((1 - core) * half, 128), half)
    order = [(k, j) for k in range(3) for j in (1, 2, 3, 0)]
    swaps = {
        (k, j): pltpu.make_async_remote_copy(
            src_ref=grads.at[k % 2, j, theirs],
            dst_ref=from_core.at[k % 2, j],
            send_sem=csend.at[k, j],
            recv_sem=crecv.at[k, j],
            device_id=peers["c"],
            device_id_type=MESH,
        )
        for k, j in order
    }
    folds = {
        (k, j): Fold(
            grads.at[k % 2, j, mine], from_core.at[k % 2, j], from_one.at[k, j], from_two.at[k, j],
            fsend.at[k, j], frecv.at[k, j],
        )
        for k, j in order
    }
    over = {
        (k, j): pltpu.make_async_remote_copy(
            src_ref=zone.at[k, j],
            dst_ref=from_z.at[k, landing_place[j] - 1],
            send_sem=zsend.at[k, j - 1],
            recv_sem=zrecv.at[k, landing_place[j] - 1],
            device_id=line[j],
            device_id_type=MESH,
        )
        for k, j in order
        if j and j not in EARLY[k]
    }
    early_slots = [(k, j) for k, j in order if j in EARLY[k]]
    early_base = {k: early_slots.index((k, 1)) for k in range(3)}

    def early_pair(k, place, item):
        found = []
        for p in (0, 1):
            found.append(
                pltpu.make_async_remote_copy(
                    src_ref=grads.at[k % 2, item[1], mine].at[folds[item].keep_one[p]],
                    dst_ref=from_early.at[early_base[k] + place, p],
                    send_sem=esend.at[early_slots.index(item), p],
                    recv_sem=erecv.at[early_base[k] + place, p],
                    device_id=line[item[1]],
                    device_id_type=MESH,
                )
            )
        return found

    early = {(k, j): early_pair(k, landing_place[j] - 1, (k, j)) for k, j in early_slots}

    def merge(k, first):
        parts = [first] if first is not None else []
        for place in range(len(EARLY[k])):
            for copy in early_pair(k, place, (k, 1)):
                copy.wait_recv()
            parts.append(from_early.at[early_base[k] + place])
        folds[k, 0].combine(parts, True)

    sums = [Spread(summed_out[k], half, asend.at[k], arecv.at[k]) for k in range(3)]
    tiny = Everyone(totals, landing, ssend, srecv, everyone)

    def settle(k):
        for place in range(len(EARLY[k]), 3):
            pltpu.make_async_remote_copy(
                src_ref=zone.at[k, 1],
                dst_ref=from_z.at[k, place],
                send_sem=zsend.at[k, place],
                recv_sem=zrecv.at[k, place],
                device_id=peers[1],
                device_id_type=MESH,
            ).wait_recv()
        summed = zone[k, 0].astype(F32)
        for place in range(len(EARLY[k]), 3):
            summed = summed + from_z[k, place].astype(F32)
        for step, peer in enumerate(others):
            outer_in[k, step, 0] = summed.astype(BF)
            copy = pltpu.make_async_remote_copy(
                src_ref=outer_in.at[k, step, 0],
                dst_ref=outer_in.at[k, step, 1],
                send_sem=osend.at[k, step],
                recv_sem=orecv.at[k, step],
                device_id=peer,
                device_id_type=MESH,
            )
            copy.start()
            copy.wait()
            summed = outer_in[k, step, 0].astype(F32) + outer_in[k, step, 1].astype(F32)
        for p in (0, 1):
            summed_out[k][sums[k].own[p]] = summed[p * eighth : (p + 1) * eighth].astype(BF)
        sums[k].start(0)

    def drain(item):
        swaps[item].wait_send()
        folds[item].drain(item not in early)
        for copy in early.get(item, ()):
            copy.wait_send()

    def grad_block(k, j):
        if k == 0:
            for span, picked in ((theirs, their_cols), (mine, mine_cols)):
                grads[0, j, span] = dot(act[j, :, picked], d_low[...], "TN").astype(BF)
                if span is theirs and j:
                    swaps[k, j].start()
            if j == 0:
                feed_out_back(j)
                swaps[k, j].start()
        elif k == 1:
            for span, picked in ((theirs, their_cols), (mine, mine_cols)):
                grads[1, j, span] = dot(hidden_low[:, picked], act[j], "TN").astype(BF)
                if span is theirs:
                    swaps[k, j].start()
        else:
            drain((0, j))
            pl.semaphore_wait(credit.at[j], 1)
            grads[0, j, : 3 * cols] = dot(qkv[j], x_ref[...], "TN").astype(BF)
            grads[0, j, 3 * cols :] = dot(ctx[j], d_low[...], "TN").astype(BF)
            swaps[k, j].start()

    def reduce_turn(turn):
        total = len(order)
        if turn < total:
            item = order[turn]
            swaps[item].wait_recv()
            folds[item].step_core(grads.at[item[0] % 2, item[1], mine])
            if item[0] == 0:
                pl.semaphore_signal(credit.at[item[1]], inc=1, device_id=peers["c"], device_id_type=MESH)
        if 0 <= turn - 1 < total:
            item = k, j = order[turn - 1]
            folds[item].step_one()
            if j == 0 and MERGE_TURN[k] == turn:
                merge(k, from_one.at[item])
            else:
                folds[item].combine([from_one.at[item]], j and item not in early)
                for copy in early.get(item, ()):
                    copy.start()
        for k in range(3):
            if MERGE_TURN[k] == turn and order[turn - 1] != (k, 0):
                merge(k, None)
        if 0 <= turn - 2 < total:
            item = order[turn - 2]
            if item[1] and item not in early:
                folds[item].step_two(zone.at[item[0], item[1]])
                over[item].start()
        for k in range(3):
            if turn == MERGE_TURN[k] + 1:
                folds[k, 0].step_two(zone.at[k, 0])
        for k in (2, 1, 0):
            if turn == SETTLE_TURN[k]:
                settle(k)
            step = turn - SETTLE_TURN[k] - 1
            if 0 <= step < 3:
                sums[k].finish(step)
                if step < 2:
                    sums[k].start(step + 1)
                if k == 2 and step:
                    part = (None, mine, theirs)[step]
                    copy = pltpu.make_async_copy(summed_out[k].at[part], summed_hbm.at[k, part], early_sem.at[1 + step])
                    copy.start()
                    early_copies.append(copy)
                elif step == 2:
                    copy = pltpu.make_async_copy(summed_out[k], summed_hbm.at[k], early_sem.at[k])
                    copy.start()
                    early_copies.append(copy)

    early_copies = []

    vecs[0] = jnp.zeros_like(vecs[0])
    for row, start, ref in (
        (0, 0, b_query), (0, 2 * cols, b_value), (1, 0, b_inner), (2, 0, b_out), (3, 0, gain_one),
        (4, 0, shift_one), (5, 0, b_outer), (6, 0, gain_two), (7, 0, shift_two),
    ):
        size = ref.shape[0]
        vecs[0, row : row + 1, start : start + size] = ref[...].astype(F32).reshape(1, size)
    for number in (1, 5, 6, 7):
        local_copies[number].wait()
    pl.semaphore_wait(barrier, len(greeted))
    send_own(0)
    for u in (1, 2, 3):
        vec_copies[u].start()
    build_masks()
    totals[0] = jnp.zeros_like(totals[0])
    local_copies[0].wait()
    project(0)
    gather_turn(0)
    gather_turn(1)
    attend(0)
    gather_turn(2)
    for j in (1, 2, 3):
        gather_turn(2 + j)
        if j == 1:
            for place in range(3):
                pltpu.make_async_remote_copy(
                    src_ref=vecs.at[0],
                    dst_ref=vecs.at[place + 1],
                    send_sem=v_send.at[place],
                    recv_sem=v_recv.at[place],
                    device_id=peers[1],
                    device_id_type=MESH,
                ).wait_recv()
        project(j)
        attend(j)
    gather_turn(6)
    project_out()
    norm_first()
    gather_turn(7)
    local_copies[2].wait()
    feed_in(0)
    feed_in(1)
    gather_turn(8)
    feed_in(2)
    feed_in(3)
    gather_turn(9)
    local_copies[3].wait()
    feed_out(0)
    feed_out(1)
    for j in (2, 3):
        spreads[2, j].finish(2)
        feed_out(j)
    local_copies[4].wait()
    norm_second()
    out_copy = pltpu.make_async_copy(cot, out_hbm, local_sem.at[0])
    out_copy.start()

    grad_block(0, 1)
    grad_block(0, 2)
    reduce_turn(0)
    grad_block(0, 3)
    feed_out_back(1)
    feed_out_back(2)
    reduce_turn(1)
    feed_out_back(3)
    grad_block(0, 0)
    feed_in_back(1, True)
    reduce_turn(2)
    for j in (2, 3, 0):
        feed_in_back(j, False)
    norm_first_back()
    grad_block(1, 1)
    reduce_turn(3)
    for place, j in enumerate((2, 3, 0)):
        grad_block(1, j)
        attend_back((1, 2, 3)[place])
        reduce_turn(4 + place)
    attend_back(0)

    def tiny_turn(number):
        if number < len(everyone):
            tiny.finish(number)
            if number + 1 < len(everyone):
                tiny.start(number + 1)

    for place, j in enumerate((1, 2, 3, 0)):
        grad_block(2, j)
        if place:
            input_back(order[7 + place][1])
        reduce_turn(7 + place)
    input_back(0)
    grad_in_copy = pltpu.make_async_copy(d_norm, grad_in_hbm, local_sem.at[1])
    grad_in_copy.start()
    reduce_turn(11)
    tiny.start(0)
    for extra in range(6):
        tiny_turn(extra)
        reduce_turn(len(order) + extra)
    for extra in range(6, len(everyone)):
        tiny_turn(extra)
    small_copy = pltpu.make_async_copy(totals.at[len(everyone)], small_hbm, local_sem.at[2])
    small_copy.start()

    def settled(copies):
        for copy in copies:
            copy.wait_send()

    for k in range(3):
        settled(near[k])
        for u in (2, 3):
            pl.when(middle == 1)(lambda k=k, u=u: settled(across[k, u] + onward[k, u]))
    for item in gathered:
        spreads[item].drain()
    for j in (1, 2, 3):
        vec_copies[j].wait_send()
    for item in order:
        if item[0]:
            drain(item)
        if item in over:
            over[item].wait_send()
    for spread in sums:
        spread.drain()
    tiny.drain()
    for copy in [out_copy, grad_in_copy, small_copy] + early_copies:
        copy.wait()


def block(outer, x, cot, seg, pad, *others):
    tokens, width = x.shape
    side = others[4].shape[0]
    half, cols = side // 2, side // 4
    heads = cols // HEAD_DIM
    row_count = tokens // SEQ
    steps = 5 + int(math.log2(outer))
    more = max(steps - 5, 1)
    outer_rows = half // 4 if outer > 1 else 16
    early = sum(len(slots) for slots in EARLY)
    dma = pltpu.SemaphoreType.DMA
    vmem = pltpu.VMEM
    any_space = pl.BlockSpec(memory_space=pl.ANY)
    in_vmem = pl.BlockSpec(memory_space=pltpu.VMEM)
    return pl.pallas_call(
        functools.partial(block_body, outer),
        out_shape=(
            jax.ShapeDtypeStruct((tokens, width), BF),
            jax.ShapeDtypeStruct((tokens, width), F32),
            jax.ShapeDtypeStruct((3, side, width), BF),
            jax.ShapeDtypeStruct((16, width), F32),
        ),
        in_specs=[any_space] * 2 + [in_vmem] * 2 + [any_space] * 6 + [in_vmem] * 9,
        out_specs=(any_space,) * 4,
        scratch_shapes=[
            vmem((3, 4, side, width), BF),
            vmem((tokens, width), BF),
            vmem((tokens, width), BF),
            vmem((row_count, SEQ, SEQ), F32),
            vmem((4, 8, width), F32),
            vmem((4, tokens, 3 * cols), BF),
            vmem((4, tokens, cols), BF),
            vmem((4, row_count, heads, SEQ, SEQ), BF),
            vmem((tokens, width), F32),
            vmem((tokens, 1), F32),
            vmem((tokens, width), BF),
            vmem((4, tokens, side), BF),
            vmem((max(3 * side, 4 * tokens), side), BF),
            vmem((tokens, width), F32),
            vmem((tokens, width), F32),
            vmem((tokens, width), BF),
            vmem((tokens, cols), BF),
            vmem((2, 4, side, width), BF),
            vmem((2, 4, half, width), BF),
            vmem((3, 4, 2, half // 4, width), BF),
            vmem((3, 4, 2, half // 8, width), BF),
            vmem((3, 4, half // 4, width), BF),
            vmem((3, 3, half // 4, width), BF),
            vmem((early, 2, half // 4, width), BF),
            vmem((3, more, 2, outer_rows, width), BF),
            vmem((steps + 1, 16, width), F32),
            vmem((steps, 16, width), F32),
            dma((3, 3, 2, 2)), dma((3, 3, 2)), dma((3, 3, 5)), dma((3, 3, 5)), dma((3,)), dma((3,)), dma((8,)), dma((4,)),
            dma((3, 4)), dma((3, 4)), dma((3, 4, 4)), dma((3, 4, 4)), dma((3, 3)), dma((3, 3)), dma((early, 2)), dma((early, 2)),
            dma((3, 5)), dma((3, 5)), dma((3, more)), dma((3, more)), dma((steps,)), dma((steps,)),
            pltpu.SemaphoreType.REGULAR((4,)),
        ],
        compiler_params=pltpu.CompilerParams(
            collective_id=0, has_side_effects=True, vmem_limit_bytes=67043328
        ),
        name="block",
    )(x, cot, seg, pad, *others)


def local(
    outer, block_input, cotangent, segment_ids, pad_mask,
    w_query, b_query, w_key, w_value, b_value, w_out, b_out, gain_one, shift_one,
    w_inner, b_inner, w_outer, b_outer, gain_two, shift_two,
):
    tokens, width = block_input.shape
    cols = w_query.shape[1]
    output, grad_input, summed, small = block(
        outer, block_input, cotangent, segment_ids.reshape(-1, SEQ), pad_mask.reshape(-1, SEQ),
        w_query.T, w_key.T, w_value.T, w_out, w_inner, w_outer,
        b_query, b_value, b_inner, b_out, gain_one, shift_one, b_outer, gain_two, shift_two,
    )
    outs = list(finish(output, grad_input, summed, small, cols))
    for place in (2, 4, 5):
        outs[place] = outs[place].T
    return tuple(outs)


def finish_body(
    out_hbm, grad_in_hbm, summed_hbm, small_ref,
    output, grad_input, g_query, gb_query, g_key, g_value, gb_value, g_out, gb_out, gg_one, gs_one,
    g_inner, gb_inner, g_outer, gb_outer, gg_two, gs_two,
    out_held, in_held, summed, wide, turned, flat, in_sem, out_sem,
):
    z = lax.axis_index("tensor")
    cols = gb_query.shape[0]
    reads = [pltpu.make_async_copy(summed_hbm.at[k], summed.at[k], in_sem.at[k]) for k in (0, 1, 2)]
    reads.append(pltpu.make_async_copy(grad_in_hbm, in_held, in_sem.at[3]))
    reads.append(pltpu.make_async_copy(out_hbm, out_held, in_sem.at[4]))
    for copy in reads:
        copy.start()
    for row, ref in ((0, gb_out), (1, gg_one), (2, gs_one), (3, gb_outer), (4, gg_two), (5, gs_two)):
        ref[...] = small_ref[row : row + 1, :].reshape(ref.shape)
    own = small_ref[pl.ds(8 + z, 1), :]
    gb_query[...] = own[:, :cols].reshape(gb_query.shape)
    gb_value[...] = own[:, 2 * cols : 3 * cols].reshape(gb_value.shape)
    gb_inner[...] = small_ref[pl.ds(12 + z, 1), :].reshape(gb_inner.shape)
    writes = []

    def write(source, target):
        copy = pltpu.make_async_copy(source, target, out_sem.at[len(writes)])
        copy.start()
        writes.append(copy)

    for k, target in ((0, g_outer), (1, g_inner)):
        reads[k].wait()
        wide[k] = summed[k].astype(F32)
        write(wide.at[k], target)
    reads[2].wait()
    for part, target in enumerate((g_query, g_key, g_value)):
        turned[part] = summed[2, part * cols : (part + 1) * cols].astype(F32)
        write(turned.at[part], target)
    flat[...] = summed[2, 3 * cols :].astype(F32)
    write(flat, g_out)
    reads[3].wait()
    write(in_held, grad_input)
    reads[4].wait()
    write(out_held, output)
    for copy in writes:
        copy.wait()


def finish(output, grad_input, summed, small, cols):
    (tokens, width), side = output.shape, summed.shape[1]
    shape = jax.ShapeDtypeStruct
    any_space = pl.BlockSpec(memory_space=pl.ANY)
    in_vmem = pl.BlockSpec(memory_space=pltpu.VMEM)
    line, short, flat, big = shape((width,), F32), shape((cols,), F32), shape((cols, width), F32), shape((side, width), F32)
    outs = (
        (shape((tokens, width), BF), 0), (shape((tokens, width), F32), 0), (flat, 0), (short, 1), (flat, 0), (flat, 0),
        (short, 1), (flat, 0), (line, 1), (line, 1), (line, 1), (big, 0), (line, 1), (big, 0),
        (line, 1), (line, 1), (line, 1),
    )
    dma = pltpu.SemaphoreType.DMA
    return pl.pallas_call(
        finish_body,
        out_shape=tuple(item for item, _ in outs),
        in_specs=[any_space, any_space, any_space, in_vmem],
        out_specs=tuple(in_vmem if held else any_space for _, held in outs),
        scratch_shapes=[
            pltpu.VMEM((tokens, width), BF),
            pltpu.VMEM((tokens, width), F32),
            pltpu.VMEM((3, side, width), BF),
            pltpu.VMEM((2, side, width), F32),
            pltpu.VMEM((3, cols, width), F32),
            pltpu.VMEM((cols, width), F32),
            dma((5,)), dma((8,)),
        ],
        compiler_params=pltpu.CompilerParams(vmem_limit_bytes=67043328),
        name="finish",
    )(output, grad_input, summed, small)


def solution(mesh):
    outer = mesh.shape["dp"] // GROUP
    row, col, both, rep = P("tensor", None), P(None, "tensor"), P(("dp", "tensor"), None), P()
    part = P("tensor")
    return jax.shard_map(
        functools.partial(local, outer),
        mesh=mesh,
        in_specs=(
            both, both, P("dp"), P("dp"), col, part, col, col, part, row, rep, rep, rep,
            col, part, row, rep, rep, rep,
        ),
        out_specs=(
            both, both, col, part, col, col, part, row, rep, rep, rep, col, part, row, rep, rep, rep,
        ),
        check_vma=False,
    )
```

```python
import functools
import math

import jax
import jax.numpy as jnp
from jax import lax
from jax.experimental import pallas as pl
from jax.experimental.pallas import tpu as pltpu
from jax.sharding import PartitionSpec as P

HEAD_DIM = 64
SEQ = 128
EPSILON = 1e-05
MASKED = -1e30
BF = jnp.bfloat16
F32 = jnp.float32
MESH = pl.DeviceIdType.MESH
GROUP = 8
WIDE = ((2, 1), (2, 3))
EARLY = ((1, 2, 3), (1,), (1,))
MERGE_TURN = (6, 8, 12)
SETTLE_TURN = (12, 13, 14)


def places():
    dp = lax.axis_index("dp")
    z = lax.axis_index("tensor")
    core = dp % 2
    along_x = (dp // 2) % 2
    along_y = (dp // 4) % 2
    peers = {
        "c": {"dp": dp + 1 - 2 * core, "tensor": z},
        "x": {"dp": dp + 2 - 4 * along_x, "tensor": z},
        "y": {"dp": dp + 4 - 8 * along_y, "tensor": z},
        1: {"dp": dp, "tensor": z + 1 - 2 * (z % 2)},
        2: {"dp": dp, "tensor": (z + 2) % 4},
        3: {"dp": dp, "tensor": 3 - z},
    }
    return dp, z, core, along_x, along_y, peers


def line_order(z):
    low, high = z % 2, z // 2
    middle = low + high - 2 * low * high
    shards = (z, z + 1 - 2 * low, (1 - middle) * ((z + 2) % 4) + middle * (3 - z), middle * ((z + 2) % 4) + (1 - middle) * (3 - z))
    return middle, shards, (0, 1, 3 - middle, 3 - middle)


def outer_peers(dp, z, outer):
    found = []
    weight = GROUP
    while weight < GROUP * outer:
        bit = (dp // weight) % 2
        found.append({"dp": dp + weight - 2 * weight * bit, "tensor": z})
        weight *= 2
    return found


def rows(start, size):
    return pl.ds(pl.multiple_of(start, 16), size)


class Spread:
    def __init__(self, block, half, send, recv, wide=False):
        _, _, core, ax, ay, peers = places()
        base = core * half
        part = half // 2
        quarter = part // 2
        eighth = quarter // 2
        first = base + ax * quarter
        second = base + part + ay * quarter
        self.steps = []
        plan = (
            ((rows(first + ay * eighth, eighth), "y"), (rows(second + ax * eighth, eighth), "x")),
            ((rows(first, quarter), "x"), (rows(second, quarter), "y")),
            ((rows(base, half), "c"),),
        )
        place = 0
        for number, step in enumerate(plan):
            copies = []
            for span, name in () if wide and number == 0 else step:
                copies.append(
                    pltpu.make_async_remote_copy(
                        src_ref=block.at[span],
                        dst_ref=block.at[span],
                        send_sem=send.at[place],
                        recv_sem=recv.at[place],
                        device_id=peers[name],
                        device_id_type=MESH,
                    )
                )
                place += 1
            self.steps.append(copies)
        self.own = (rows(first + ay * eighth, eighth), rows(second + ax * eighth, eighth))
        if wide:
            self.own = (rows(first, quarter), rows(second, quarter))

    def start(self, step):
        for copy in self.steps[step]:
            copy.start()

    def finish(self, step):
        for copy in self.steps[step]:
            copy.wait_recv()

    def drain(self):
        for step in self.steps:
            for copy in step:
                copy.wait_send()


def plus(left, right):
    return (left.astype(F32) + right.astype(F32)).astype(BF)


class Fold:
    def __init__(self, held, from_core, from_one, from_two, send, recv):
        _, _, core, ax, ay, peers = places()
        half = held.shape[0]
        part, quarter, eighth = half // 2, half // 4, half // 8
        self.held = held
        self.from_core = from_core
        self.from_one = from_one
        self.from_two = from_two
        self.quarter, self.eighth = quarter, eighth
        self.give_one = (rows((1 - ax) * quarter, quarter), rows(part + (1 - ay) * quarter, quarter))
        self.keep_one = (rows(ax * quarter, quarter), rows(part + ay * quarter, quarter))
        self.give_two = (
            rows(ax * quarter + (1 - ay) * eighth, eighth),
            rows(part + ay * quarter + (1 - ax) * eighth, eighth),
        )
        self.keep_two = (
            rows(ax * quarter + ay * eighth, eighth),
            rows(part + ay * quarter + ax * eighth, eighth),
        )
        self.inside = (rows((1 - ay) * eighth, eighth), rows((1 - ax) * eighth, eighth))
        self.inside_keep = (rows(ay * eighth, eighth), rows(ax * eighth, eighth))
        self.one = [
            pltpu.make_async_remote_copy(
                src_ref=held.at[self.give_one[p]],
                dst_ref=from_one.at[p],
                send_sem=send.at[p],
                recv_sem=recv.at[p],
                device_id=peers["xy"[p]],
                device_id_type=MESH,
            )
            for p in (0, 1)
        ]
        self.two = [
            pltpu.make_async_remote_copy(
                src_ref=held.at[self.give_two[p]],
                dst_ref=from_two.at[p],
                send_sem=send.at[2 + p],
                recv_sem=recv.at[2 + p],
                device_id=peers["yx"[p]],
                device_id_type=MESH,
            )
            for p in (0, 1)
        ]

    def step_core(self, own):
        for spans in (self.give_one, self.keep_one):
            for p in (0, 1):
                span = spans[p]
                self.held[span] = plus(own[span], self.from_core[span])
            if spans is self.give_one:
                for copy in self.one:
                    copy.start()

    def step_one(self):
        for copy in self.one:
            copy.wait_recv()

    def combine(self, parts, send):
        for spans, insides in ((self.give_two, self.inside), (self.keep_two, self.inside_keep)):
            for p in (0, 1):
                total = self.held[spans[p]].astype(F32)
                for part in parts:
                    total = total + part[p, insides[p]].astype(F32)
                self.held[spans[p]] = total.astype(BF)
                if send and spans is self.give_two:
                    self.two[p].start()

    def step_two(self, result):
        for p in (0, 1):
            self.two[p].wait_recv()
            result[p * self.eighth : (p + 1) * self.eighth] = plus(self.held[self.keep_two[p]], self.from_two[p])

    def drain(self, halved):
        for copy in self.one + (self.two if halved else []):
            copy.wait_send()


class Everyone:
    def __init__(self, total, landing, send, recv, peer_list):
        self.total, self.landing = total, landing
        self.copies = [
            pltpu.make_async_remote_copy(
                src_ref=total.at[step],
                dst_ref=landing.at[step],
                send_sem=send.at[step],
                recv_sem=recv.at[step],
                device_id=peer,
                device_id_type=MESH,
            )
            for step, peer in enumerate(peer_list)
        ]

    def start(self, step):
        self.copies[step].start()

    def finish(self, step):
        self.copies[step].wait_recv()
        self.total[step + 1] = self.total[step] + self.landing[step]

    def drain(self):
        for copy in self.copies:
            copy.wait_send()


DIMS = {"NN": ((1,), (0,)), "NT": ((1,), (1,)), "TN": ((0,), (0,))}
SCALING = 1.0 / math.sqrt(HEAD_DIM)


def dot(left, right, form="NN"):
    return lax.dot_general(left, right, (DIMS[form], ((), ())), preferred_element_type=F32)


def column_sum(values):
    return jnp.sum(values, axis=0, keepdims=True)


def row_mean(values):
    return jnp.mean(values, axis=-1, keepdims=True)


def chunks(count, size, body):
    def run(step, carry):
        body(rows(step * size, size))
        return carry

    lax.fori_loop(0, count // size, run, 0)


def block_body(
    outer,
    x_hbm, cot_hbm, seg_ref, pad_ref, w_query, w_key, w_value, w_out, own_b, own_c,
    b_query, b_value, b_inner, b_out, gain_one, shift_one, b_outer, gain_two, shift_two,
    out_hbm, grad_in_hbm, summed_hbm, small_hbm,
    weights, x_ref, cot, masks, vecs, qkv, ctx, probs, norm_one, scale_one, hidden_low, act, shared,
    acc, d_norm, d_low, d_ctx,
    grads, from_core, from_one, from_two, zone, from_z, from_early, outer_in, totals, landing,
    gz_send, gz_recv, g_send, g_recv, v_send, v_recv, local_sem, early_sem,
    csend, crecv, fsend, frecv, zsend, zrecv, esend, erecv, asend, arecv, osend, orecv, ssend, srecv, credit,
):
    dp, z, core, ax, ay, peers = places()
    others = outer_peers(dp, z, outer)
    everyone = [peers[name] for name in ("c", "x", "y", 1, 2)] + others
    tokens, width = x_ref.shape
    side = own_b.shape[0]
    half = side // 2
    eighth = half // 8
    cols = side // 4
    heads = cols // HEAD_DIM
    row_count = tokens // SEQ
    slope = [shared.at[u * tokens : (u + 1) * tokens] for u in range(4)]
    summed_out = [shared.at[k * side : (k + 1) * side] for k in range(3)]
    middle, shard_of, landing_place = line_order(z)
    line = {u: {"dp": dp, "tensor": shard_of[u]} for u in (1, 2, 3)}

    local_copies = [
        pltpu.make_async_copy(x_hbm, x_ref, local_sem.at[0]),
        pltpu.make_async_copy(w_out, weights.at[0, 0, 3 * cols :], local_sem.at[1]),
        pltpu.make_async_copy(own_b, weights.at[1, 0], local_sem.at[2]),
        pltpu.make_async_copy(own_c, weights.at[2, 0], local_sem.at[3]),
        pltpu.make_async_copy(cot_hbm, cot, local_sem.at[4]),
    ] + [
        pltpu.make_async_copy(ref, weights.at[0, 0, part * cols : (part + 1) * cols], local_sem.at[5 + part])
        for part, ref in enumerate((w_query, w_key, w_value))
    ]
    for number in (5, 6, 7, 1, 0, 2, 3, 4):
        local_copies[number].start()
    barrier = pltpu.get_barrier_semaphore()
    greeted = [peers[name] for name in ("c", "x", "y", 1, 2, 3)] + others
    for peer in greeted:
        pl.semaphore_signal(barrier, inc=1, device_id=peer, device_id_type=MESH)

    spreads, arrivals, vec_copies = {}, {}, {}
    gathered = [(k, u) for k in range(3) for u in (1, 2, 3)]

    def hop(k, source, target, peer):
        found = []
        for piece, span in enumerate(spreads[k, target].own):
            src = weights.at[k, source, span]
            if source == 0 and k:
                src = (None, own_b, own_c)[k].at[span]
            found.append(
                pltpu.make_async_remote_copy(
                    src_ref=src,
                    dst_ref=weights.at[k, target, span],
                    send_sem=gz_send.at[k, target - 1, 0 if peer is peers[1] else 1, piece],
                    recv_sem=gz_recv.at[k, target - 1, piece],
                    device_id=peer,
                    device_id_type=MESH,
                )
            )
        return found

    for k, u in gathered:
        spreads[k, u] = Spread(weights.at[k, u], half, g_send.at[k, u - 1], g_recv.at[k, u - 1], (k, u) in WIDE)
    near = {k: hop(k, 0, 1, peers[1]) for k in range(3)}
    across = {(k, 2): hop(k, 0, 2, peers[3]) for k in range(3)}
    across.update({(k, 3): hop(k, 1, 3, peers[3]) for k in range(3)})
    onward = {(k, u): hop(k, u, u, peers[1]) for k in range(3) for u in (2, 3)}
    for u in (1, 2, 3):
        vec_copies[u] = pltpu.make_async_remote_copy(
            src_ref=vecs.at[0],
            dst_ref=vecs.at[landing_place[u]],
            send_sem=v_send.at[u - 1],
            recv_sem=v_recv.at[landing_place[u] - 1],
            device_id=line[u],
            device_id_type=MESH,
        )

    def begin(copies):
        for copy in copies:
            copy.start()

    def send_own(k):
        begin(near[k])
        pl.when(middle == 1)(lambda: begin(across[k, 2]))

    landed = {}
    for k in range(3):
        landed.update({(k, 1): near[k], (k, 2): across[k, 2], (k, 3): across[k, 3]})

    def arrive(item):
        for copy in landed[item]:
            copy.wait_recv()

    def ahead(turn):
        k, u = gathered[turn]

        def forward():
            arrive((k, u))
            begin(across[k, 3] if u == 1 else onward[k, u])

        pl.when(middle == 1)(forward)
        if u == 2 and k < 2:
            send_own(k + 1)

    def gather_turn(turn):
        total = len(gathered)
        if turn == 0:
            ahead(0)
        if turn < total:
            item = gathered[turn]
            pl.when(middle == 0)(lambda: arrive(item))
            spreads[item].start(1 if item in WIDE else 0)
        for lag in (1, 2, 3):
            if 0 <= turn - lag < total:
                item = gathered[turn - lag]
                step = lag - 1 + (item in WIDE)
                if step < 3:
                    spreads[item].finish(step)
                if step < 2:
                    spreads[item].start(step + 1)
            if lag < 3:
                for later in {(0, 1): (1,), (1, 1): (2,), (1, 2): (3,), (2, 2): (4,), (3, 1): (5,), (3, 2): (6,), (4, 2): (7,), (5, 2): (8,)}.get(
                    (turn, lag), ()
                ):
                    ahead(later)

    def vector(row, slot=0):
        return vecs[slot, row : row + 1, :]

    def build_masks():
        for r in range(row_count):
            place = pl.ds(z * row_count + r, 1)
            seg = jnp.broadcast_to(seg_ref[place, :].astype(F32), (SEQ, SEQ))
            pad = jnp.broadcast_to(pad_ref[place, :], (SEQ, SEQ))
            allowed = (seg == seg.T) & (pad == 1)
            masks[r] = jnp.where(allowed, 0.0, MASKED)

    def project(j):
        bias = vector(0, j)[:, : 3 * cols]

        def body(span):
            qkv[j, span] = (dot(x_ref[span], weights[0, j, : 3 * cols], "NT") + bias).astype(BF)

        chunks(tokens, 256, body)

    def head(joined, part, h):
        return joined[:, part * cols + h * HEAD_DIM : part * cols + (h + 1) * HEAD_DIM]

    units = [(r, h) for r in range(row_count) for h in range(heads)]

    def spans(r):
        return slice(r * SEQ, (r + 1) * SEQ)

    def attend(j):
        joined = [qkv[j, spans(r)] for r in range(row_count)]
        scores = [
            dot(head(joined[r], 0, h), head(joined[r], 1, h), "NT") * SCALING + masks[r] for r, h in units
        ]
        found = []
        for (r, h), score in zip(units, scores):
            weight = jnp.exp(score - jnp.max(score, axis=-1, keepdims=True))
            found.append((weight * (1.0 / jnp.sum(weight, axis=-1, keepdims=True))).astype(BF))
        mixed = []
        for (r, h), prob in zip(units, found):
            probs[j, r, h] = prob
            mixed.append(dot(prob, head(joined[r], 2, h)).astype(BF))
        for r in range(row_count):
            ctx[j, spans(r)] = jnp.concatenate(mixed[r * heads : (r + 1) * heads], axis=1)

    def project_out():
        total = dot(ctx[0], weights[0, 0, 3 * cols :])
        for j in (1, 2, 3):
            total = total + dot(ctx[j], weights[0, j, 3 * cols :])
        acc[...] = total

    def norm_first():
        b_out, gain, shift = vector(2), vector(3), vector(4)

        def body(span):
            value = acc[span] + b_out + x_ref[span].astype(F32)
            center = value - row_mean(value)
            scale = lax.rsqrt(row_mean(center * center) + EPSILON)
            normal = center * scale
            norm_one[span] = normal
            scale_one[span] = scale
            hidden_low[span] = (normal * gain + shift).astype(BF)

        chunks(tokens, 128, body)

    def feed_in(j):
        bias = vector(1, j)

        def body(span):
            pre = dot(hidden_low[span], weights[1, j]) + bias
            cumulative = 0.5 + 0.5 * lax.erf(pre * (1.0 / math.sqrt(2.0)))
            density = jnp.exp(pre * pre * -0.5) * (1.0 / math.sqrt(2.0 * math.pi))
            act[j, span] = (pre * cumulative).astype(BF)
            slope[j][span] = (cumulative + pre * density).astype(BF)

        chunks(tokens, 128, body)

    def feed_out(j):
        part = dot(act[j], weights[2, j])
        acc[...] = part if j == 0 else acc[...] + part

    def small_add(row, value):
        totals[0, pl.ds(row, 1), : value.shape[1]] += value

    def norm_second():
        gain_a, shift_a, b_outer = vector(3), vector(4), vector(5)
        gain, shift = vector(6), vector(7)

        def body(span):
            value = acc[span] + b_outer + (norm_one[span] * gain_a + shift_a)
            center = value - row_mean(value)
            scale = lax.rsqrt(row_mean(center * center) + EPSILON)
            normal = center * scale
            given = cot[span].astype(F32)
            cot[span] = (normal * gain + shift).astype(BF)
            pulled = given * gain
            grad = scale * (pulled - row_mean(pulled) - normal * row_mean(pulled * normal))
            d_norm[span] = grad
            d_low[span] = grad.astype(BF)
            small_add(3, column_sum(grad))
            small_add(4, column_sum(given * normal))
            small_add(5, column_sum(given))

        chunks(tokens, 128, body)

    def feed_out_back(j):
        def body(span):
            grad = (dot(d_low[span], weights[2, j], "NT") * slope[j][span].astype(F32)).astype(BF)
            act[j, span] = grad
            small_add(12 + shard_of[j], column_sum(grad.astype(F32)))

        chunks(tokens, 256, body)

    def feed_in_back(j, first):
        def body(span):
            part = dot(act[j, span], weights[1, j], "NT")
            acc[span] = part if first else acc[span] + part

        chunks(tokens, 256, body)

    def norm_first_back():
        gain = vector(3)

        def body(span):
            given = acc[span] + d_norm[span]
            normal = norm_one[span]
            pulled = given * gain
            grad = scale_one[span] * (pulled - row_mean(pulled) - normal * row_mean(pulled * normal))
            d_norm[span] = grad
            d_low[span] = grad.astype(BF)
            small_add(0, column_sum(grad))
            small_add(1, column_sum(given * normal))
            small_add(2, column_sum(given))

        chunks(tokens, 128, body)

    def attend_back(j):
        d_ctx[...] = dot(d_low[...], weights[0, j, 3 * cols :], "NT").astype(BF)
        joined = [qkv[j, spans(r)] for r in range(row_count)]
        given = [d_ctx[spans(r)] for r in range(row_count)]
        d_outs = [given[r][:, h * HEAD_DIM : (h + 1) * HEAD_DIM] for r, h in units]
        d_probs = [dot(d_out, head(joined[r], 2, h), "NT") for (r, h), d_out in zip(units, d_outs)]
        prob_list = [probs[j, r, h] for r, h in units]
        d_scores = []
        for d_prob, prob in zip(d_probs, prob_list):
            wide = prob.astype(F32)
            inner = jnp.sum(d_prob * wide, axis=-1, keepdims=True)
            d_scores.append((wide * (d_prob - inner)).astype(BF))
        d_values = [dot(prob, d_out, "TN").astype(BF) for prob, d_out in zip(prob_list, d_outs)]
        d_queries = [(dot(ds, head(joined[r], 1, h)) * SCALING).astype(BF) for (r, h), ds in zip(units, d_scores)]
        d_keys = [(dot(ds, head(joined[r], 0, h), "TN") * SCALING).astype(BF) for (r, h), ds in zip(units, d_scores)]
        total = jnp.zeros((1, 3 * cols), F32)
        for r in range(row_count):
            mine_heads = slice(r * heads, (r + 1) * heads)
            joined_grad = jnp.concatenate(d_queries[mine_heads] + d_keys[mine_heads] + d_values[mine_heads], axis=1)
            qkv[j, spans(r)] = joined_grad
            total = total + column_sum(joined_grad.astype(F32))
        small_add(8 + shard_of[j], total)

    def input_back(j):
        def body(span):
            d_norm[span] = d_norm[span] + dot(qkv[j, span], weights[0, j, : 3 * cols])

        chunks(tokens, 256, body)

    mine, theirs = rows(core * half, half), rows((1 - core) * half, half)
    mine_cols = pl.ds(pl.multiple_of(core * half, 128), half)
    their_cols = pl.ds(pl.multiple_of((1 - core) * half, 128), half)
    order = [(k, j) for k in range(3) for j in (1, 2, 3, 0)]
    swaps = {
        (k, j): pltpu.make_async_remote_copy(
            src_ref=grads.at[k % 2, j, theirs],
            dst_ref=from_core.at[k % 2, j],
            send_sem=csend.at[k, j],
            recv_sem=crecv.at[k, j],
            device_id=peers["c"],
            device_id_type=MESH,
        )
        for k, j in order
    }
    folds = {
        (k, j): Fold(
            grads.at[k % 2, j, mine], from_core.at[k % 2, j], from_one.at[k, j], from_two.at[k, j],
            fsend.at[k, j], frecv.at[k, j],
        )
        for k, j in order
    }
    over = {
        (k, j): pltpu.make_async_remote_copy(
            src_ref=zone.at[k, j],
            dst_ref=from_z.at[k, landing_place[j] - 1],
            send_sem=zsend.at[k, j - 1],
            recv_sem=zrecv.at[k, landing_place[j] - 1],
            device_id=line[j],
            device_id_type=MESH,
        )
        for k, j in order
        if j and j not in EARLY[k]
    }
    early_slots = [(k, j) for k, j in order if j in EARLY[k]]
    early_base = {k: early_slots.index((k, 1)) for k in range(3)}

    def early_pair(k, place, item):
        found = []
        for p in (0, 1):
            found.append(
                pltpu.make_async_remote_copy(
                    src_ref=grads.at[k % 2, item[1], mine].at[folds[item].keep_one[p]],
                    dst_ref=from_early.at[early_base[k] + place, p],
                    send_sem=esend.at[early_slots.index(item), p],
                    recv_sem=erecv.at[early_base[k] + place, p],
                    device_id=line[item[1]],
                    device_id_type=MESH,
                )
            )
        return found

    early = {(k, j): early_pair(k, landing_place[j] - 1, (k, j)) for k, j in early_slots}

    def merge(k, first):
        parts = [first] if first is not None else []
        for place in range(len(EARLY[k])):
            for copy in early_pair(k, place, (k, 1)):
                copy.wait_recv()
            parts.append(from_early.at[early_base[k] + place])
        folds[k, 0].combine(parts, True)

    sums = [Spread(summed_out[k], half, asend.at[k], arecv.at[k]) for k in range(3)]
    tiny = Everyone(totals, landing, ssend, srecv, everyone)

    def settle(k):
        for place in range(len(EARLY[k]), 3):
            pltpu.make_async_remote_copy(
                src_ref=zone.at[k, 1],
                dst_ref=from_z.at[k, place],
                send_sem=zsend.at[k, place],
                recv_sem=zrecv.at[k, place],
                device_id=peers[1],
                device_id_type=MESH,
            ).wait_recv()
        summed = zone[k, 0].astype(F32)
        for place in range(len(EARLY[k]), 3):
            summed = summed + from_z[k, place].astype(F32)
        for step, peer in enumerate(others):
            outer_in[k, step, 0] = summed.astype(BF)
            copy = pltpu.make_async_remote_copy(
                src_ref=outer_in.at[k, step, 0],
                dst_ref=outer_in.at[k, step, 1],
                send_sem=osend.at[k, step],
                recv_sem=orecv.at[k, step],
                device_id=peer,
                device_id_type=MESH,
            )
            copy.start()
            copy.wait()
            summed = outer_in[k, step, 0].astype(F32) + outer_in[k, step, 1].astype(F32)
        for p in (0, 1):
            summed_out[k][sums[k].own[p]] = summed[p * eighth : (p + 1) * eighth].astype(BF)
        sums[k].start(0)

    def drain(item):
        swaps[item].wait_send()
        folds[item].drain(item not in early)
        for copy in early.get(item, ()):
            copy.wait_send()

    def grad_block(k, j):
        if k == 0:
            for span, picked in ((theirs, their_cols), (mine, mine_cols)):
                grads[0, j, span] = dot(act[j, :, picked], d_low[...], "TN").astype(BF)
                if span is theirs and j:
                    swaps[k, j].start()
            if j == 0:
                feed_out_back(j)
                swaps[k, j].start()
        elif k == 1:
            for span, picked in ((theirs, their_cols), (mine, mine_cols)):
                grads[1, j, span] = dot(hidden_low[:, picked], act[j], "TN").astype(BF)
                if span is theirs:
                    swaps[k, j].start()
        else:
            drain((0, j))
            pl.semaphore_wait(credit.at[j], 1)
            grads[0, j, : 3 * cols] = dot(qkv[j], x_ref[...], "TN").astype(BF)
            grads[0, j, 3 * cols :] = dot(ctx[j], d_low[...], "TN").astype(BF)
            swaps[k, j].start()

    def reduce_turn(turn):
        total = len(order)
        if turn < total:
            item = order[turn]
            swaps[item].wait_recv()
            folds[item].step_core(grads.at[item[0] % 2, item[1], mine])
            if item[0] == 0:
                pl.semaphore_signal(credit.at[item[1]], inc=1, device_id=peers["c"], device_id_type=MESH)
        if 0 <= turn - 1 < total:
            item = k, j = order[turn - 1]
            folds[item].step_one()
            if j == 0 and MERGE_TURN[k] == turn:
                merge(k, from_one.at[item])
            else:
                folds[item].combine([from_one.at[item]], j and item not in early)
                for copy in early.get(item, ()):
                    copy.start()
        for k in range(3):
            if MERGE_TURN[k] == turn and order[turn - 1] != (k, 0):
                merge(k, None)
        if 0 <= turn - 2 < total:
            item = order[turn - 2]
            if item[1] and item not in early:
                folds[item].step_two(zone.at[item[0], item[1]])
                over[item].start()
        for k in range(3):
            if turn == MERGE_TURN[k] + 1:
                folds[k, 0].step_two(zone.at[k, 0])
        for k in (2, 1, 0):
            if turn == SETTLE_TURN[k]:
                settle(k)
            step = turn - SETTLE_TURN[k] - 1
            if 0 <= step < 3:
                sums[k].finish(step)
                if step < 2:
                    sums[k].start(step + 1)
                if k == 2 and step:
                    part = (None, mine, theirs)[step]
                    copy = pltpu.make_async_copy(summed_out[k].at[part], summed_hbm.at[k, part], early_sem.at[1 + step])
                    copy.start()
                    early_copies.append(copy)
                elif step == 2:
                    copy = pltpu.make_async_copy(summed_out[k], summed_hbm.at[k], early_sem.at[k])
                    copy.start()
                    early_copies.append(copy)

    early_copies = []

    vecs[0] = jnp.zeros_like(vecs[0])
    for row, start, ref in (
        (0, 0, b_query), (0, 2 * cols, b_value), (1, 0, b_inner), (2, 0, b_out), (3, 0, gain_one),
        (4, 0, shift_one), (5, 0, b_outer), (6, 0, gain_two), (7, 0, shift_two),
    ):
        size = ref.shape[0]
        vecs[0, row : row + 1, start : start + size] = ref[...].astype(F32).reshape(1, size)
    for number in (1, 5, 6, 7):
        local_copies[number].wait()
    pl.semaphore_wait(barrier, len(greeted))
    send_own(0)
    for u in (1, 2, 3):
        vec_copies[u].start()
    build_masks()
    totals[0] = jnp.zeros_like(totals[0])
    local_copies[0].wait()
    project(0)
    gather_turn(0)
    gather_turn(1)
    attend(0)
    gather_turn(2)
    for j in (1, 2, 3):
        gather_turn(2 + j)
        if j == 1:
            for place in range(3):
                pltpu.make_async_remote_copy(
                    src_ref=vecs.at[0],
                    dst_ref=vecs.at[place + 1],
                    send_sem=v_send.at[place],
                    recv_sem=v_recv.at[place],
                    device_id=peers[1],
                    device_id_type=MESH,
                ).wait_recv()
        project(j)
        attend(j)
    gather_turn(6)
    project_out()
    norm_first()
    gather_turn(7)
    local_copies[2].wait()
    feed_in(0)
    feed_in(1)
    gather_turn(8)
    feed_in(2)
    feed_in(3)
    gather_turn(9)
    local_copies[3].wait()
    feed_out(0)
    feed_out(1)
    for j in (2, 3):
        spreads[2, j].finish(2)
        feed_out(j)
    local_copies[4].wait()
    norm_second()
    out_copy = pltpu.make_async_copy(cot, out_hbm, local_sem.at[0])
    out_copy.start()

    grad_block(0, 1)
    grad_block(0, 2)
    reduce_turn(0)
    grad_block(0, 3)
    feed_out_back(1)
    feed_out_back(2)
    reduce_turn(1)
    feed_out_back(3)
    grad_block(0, 0)
    feed_in_back(1, True)
    reduce_turn(2)
    for j in (2, 3, 0):
        feed_in_back(j, False)
    norm_first_back()
    grad_block(1, 1)
    reduce_turn(3)
    for place, j in enumerate((2, 3, 0)):
        grad_block(1, j)
        attend_back((1, 2, 3)[place])
        reduce_turn(4 + place)
    attend_back(0)

    def tiny_turn(number):
        if number < len(everyone):
            tiny.finish(number)
            if number + 1 < len(everyone):
                tiny.start(number + 1)

    for place, j in enumerate((1, 2, 3, 0)):
        grad_block(2, j)
        if place:
            input_back(order[7 + place][1])
        reduce_turn(7 + place)
    input_back(0)
    grad_in_copy = pltpu.make_async_copy(d_norm, grad_in_hbm, local_sem.at[1])
    grad_in_copy.start()
    reduce_turn(11)
    tiny.start(0)
    for extra in range(6):
        tiny_turn(extra)
        reduce_turn(len(order) + extra)
    for extra in range(6, len(everyone)):
        tiny_turn(extra)
    small_copy = pltpu.make_async_copy(totals.at[len(everyone)], small_hbm, local_sem.at[2])
    small_copy.start()

    def settled(copies):
        for copy in copies:
            copy.wait_send()

    for k in range(3):
        settled(near[k])
        for u in (2, 3):
            pl.when(middle == 1)(lambda k=k, u=u: settled(across[k, u] + onward[k, u]))
    for item in gathered:
        spreads[item].drain()
    for j in (1, 2, 3):
        vec_copies[j].wait_send()
    for item in order:
        if item[0]:
            drain(item)
        if item in over:
            over[item].wait_send()
    for spread in sums:
        spread.drain()
    tiny.drain()
    for copy in [out_copy, grad_in_copy, small_copy] + early_copies:
        copy.wait()


def block(outer, x, cot, seg, pad, *others):
    tokens, width = x.shape
    side = others[4].shape[0]
    half, cols = side // 2, side // 4
    heads = cols // HEAD_DIM
    row_count = tokens // SEQ
    steps = 5 + int(math.log2(outer))
    more = max(steps - 5, 1)
    outer_rows = half // 4 if outer > 1 else 16
    early = sum(len(slots) for slots in EARLY)
    dma = pltpu.SemaphoreType.DMA
    vmem = pltpu.VMEM
    any_space = pl.BlockSpec(memory_space=pl.ANY)
    in_vmem = pl.BlockSpec(memory_space=pltpu.VMEM)
    return pl.pallas_call(
        functools.partial(block_body, outer),
        out_shape=(
            jax.ShapeDtypeStruct((tokens, width), BF),
            jax.ShapeDtypeStruct((tokens, width), F32),
            jax.ShapeDtypeStruct((3, side, width), BF),
            jax.ShapeDtypeStruct((16, width), F32),
        ),
        in_specs=[any_space] * 2 + [in_vmem] * 2 + [any_space] * 6 + [in_vmem] * 9,
        out_specs=(any_space,) * 4,
        scratch_shapes=[
            vmem((3, 4, side, width), BF),
            vmem((tokens, width), BF),
            vmem((tokens, width), BF),
            vmem((row_count, SEQ, SEQ), F32),
            vmem((4, 8, width), F32),
            vmem((4, tokens, 3 * cols), BF),
            vmem((4, tokens, cols), BF),
            vmem((4, row_count, heads, SEQ, SEQ), BF),
            vmem((tokens, width), F32),
            vmem((tokens, 1), F32),
            vmem((tokens, width), BF),
            vmem((4, tokens, side), BF),
            vmem((max(3 * side, 4 * tokens), side), BF),
            vmem((tokens, width), F32),
            vmem((tokens, width), F32),
            vmem((tokens, width), BF),
            vmem((tokens, cols), BF),
            vmem((2, 4, side, width), BF),
            vmem((2, 4, half, width), BF),
            vmem((3, 4, 2, half // 4, width), BF),
            vmem((3, 4, 2, half // 8, width), BF),
            vmem((3, 4, half // 4, width), BF),
            vmem((3, 3, half // 4, width), BF),
            vmem((early, 2, half // 4, width), BF),
            vmem((3, more, 2, outer_rows, width), BF),
            vmem((steps + 1, 16, width), F32),
            vmem((steps, 16, width), F32),
            dma((3, 3, 2, 2)), dma((3, 3, 2)), dma((3, 3, 5)), dma((3, 3, 5)), dma((3,)), dma((3,)), dma((8,)), dma((4,)),
            dma((3, 4)), dma((3, 4)), dma((3, 4, 4)), dma((3, 4, 4)), dma((3, 3)), dma((3, 3)), dma((early, 2)), dma((early, 2)),
            dma((3, 5)), dma((3, 5)), dma((3, more)), dma((3, more)), dma((steps,)), dma((steps,)),
            pltpu.SemaphoreType.REGULAR((4,)),
        ],
        compiler_params=pltpu.CompilerParams(
            collective_id=0, has_side_effects=True, vmem_limit_bytes=67043328
        ),
        name="block",
    )(x, cot, seg, pad, *others)


def local(
    outer, block_input, cotangent, segment_ids, pad_mask,
    w_query, b_query, w_key, w_value, b_value, w_out, b_out, gain_one, shift_one,
    w_inner, b_inner, w_outer, b_outer, gain_two, shift_two,
):
    tokens, width = block_input.shape
    cols = w_query.shape[1]
    output, grad_input, summed, small = block(
        outer, block_input, cotangent, segment_ids.reshape(-1, SEQ), pad_mask.reshape(-1, SEQ),
        w_query.T, w_key.T, w_value.T, w_out, w_inner, w_outer,
        b_query, b_value, b_inner, b_out, gain_one, shift_one, b_outer, gain_two, shift_two,
    )
    outs = list(finish(output, grad_input, summed, small, cols))
    for place in (2, 4, 5):
        outs[place] = outs[place].T
    return tuple(outs)


def finish_body(
    out_hbm, grad_in_hbm, summed_hbm, small_ref,
    output, grad_input, g_query, gb_query, g_key, g_value, gb_value, g_out, gb_out, gg_one, gs_one,
    g_inner, gb_inner, g_outer, gb_outer, gg_two, gs_two,
    out_held, in_held, summed, wide, turned, flat, in_sem, out_sem,
):
    z = lax.axis_index("tensor")
    cols = gb_query.shape[0]
    reads = [pltpu.make_async_copy(summed_hbm.at[k], summed.at[k], in_sem.at[k]) for k in (0, 1, 2)]
    reads.append(pltpu.make_async_copy(grad_in_hbm, in_held, in_sem.at[3]))
    reads.append(pltpu.make_async_copy(out_hbm, out_held, in_sem.at[4]))
    for copy in reads:
        copy.start()
    for row, ref in ((0, gb_out), (1, gg_one), (2, gs_one), (3, gb_outer), (4, gg_two), (5, gs_two)):
        ref[...] = small_ref[row : row + 1, :].reshape(ref.shape)
    own = small_ref[pl.ds(8 + z, 1), :]
    gb_query[...] = own[:, :cols].reshape(gb_query.shape)
    gb_value[...] = own[:, 2 * cols : 3 * cols].reshape(gb_value.shape)
    gb_inner[...] = small_ref[pl.ds(12 + z, 1), :].reshape(gb_inner.shape)
    writes = []

    def write(source, target):
        copy = pltpu.make_async_copy(source, target, out_sem.at[len(writes)])
        copy.start()
        writes.append(copy)

    for k, target in ((0, g_outer), (1, g_inner)):
        reads[k].wait()
        wide[k] = summed[k].astype(F32)
        write(wide.at[k], target)
    reads[2].wait()
    for part, target in enumerate((g_query, g_key, g_value)):
        turned[part] = summed[2, part * cols : (part + 1) * cols].astype(F32)
        write(turned.at[part], target)
    flat[...] = summed[2, 3 * cols :].astype(F32)
    write(flat, g_out)
    reads[3].wait()
    write(in_held, grad_input)
    reads[4].wait()
    write(out_held, output)
    for copy in writes:
        copy.wait()


def finish(output, grad_input, summed, small, cols):
    (tokens, width), side = output.shape, summed.shape[1]
    shape = jax.ShapeDtypeStruct
    any_space = pl.BlockSpec(memory_space=pl.ANY)
    in_vmem = pl.BlockSpec(memory_space=pltpu.VMEM)
    line, short, flat, big = shape((width,), F32), shape((cols,), F32), shape((cols, width), F32), shape((side, width), F32)
    outs = (
        (shape((tokens, width), BF), 0), (shape((tokens, width), F32), 0), (flat, 0), (short, 1), (flat, 0), (flat, 0),
        (short, 1), (flat, 0), (line, 1), (line, 1), (line, 1), (big, 0), (line, 1), (big, 0),
        (line, 1), (line, 1), (line, 1),
    )
    dma = pltpu.SemaphoreType.DMA
    return pl.pallas_call(
        finish_body,
        out_shape=tuple(item for item, _ in outs),
        in_specs=[any_space, any_space, any_space, in_vmem],
        out_specs=tuple(in_vmem if held else any_space for _, held in outs),
        scratch_shapes=[
            pltpu.VMEM((tokens, width), BF),
            pltpu.VMEM((tokens, width), F32),
            pltpu.VMEM((3, side, width), BF),
            pltpu.VMEM((2, side, width), F32),
            pltpu.VMEM((3, cols, width), F32),
            pltpu.VMEM((cols, width), F32),
            dma((5,)), dma((8,)),
        ],
        compiler_params=pltpu.CompilerParams(vmem_limit_bytes=67043328),
        name="finish",
    )(output, grad_input, summed, small)


def solution(mesh):
    outer = mesh.shape["dp"] // GROUP
    row, col, both, rep = P("tensor", None), P(None, "tensor"), P(("dp", "tensor"), None), P()
    part = P("tensor")
    return jax.shard_map(
        functools.partial(local, outer),
        mesh=mesh,
        in_specs=(
            both, both, P("dp"), P("dp"), col, part, col, col, part, row, rep, rep, rep,
            col, part, row, rep, rep, rep,
        ),
        out_specs=(
            both, both, col, part, col, col, part, row, rep, rep, rep, col, part, row, rep, rep, rep,
        ),
        check_vma=False,
    )
```
